32 devices in a mesh: gx: 4 (over x, core), gy: 4 (over z), gz: 2 (over y).
Axes of the slice: x: 2, y: 2, z: 4, core: 2. Of those that a mesh axis runs over, the one named last changes fastest.
Arguments:
- volume: bfloat16 [4, 16, 32, 256], P(None, 'gx', 'gy', 'gz'), may hold values from -6 to 6
- act_one: bfloat16 [16, 16, 32, 256], P(None, 'gx', 'gy', 'gz'), may hold values from -6 to 6
- act_two: bfloat16 [16, 16, 32, 256], P(None, 'gx', 'gy', 'gz'), may hold values from -6 to 6
- weight_one: bfloat16 [16, 4, 3, 3, 3], replicated, may hold values from -0.625 to 0.625
- weight_two: bfloat16 [16, 16, 3, 3, 3], replicated, may hold values from -0.3125 to 0.3125
- cotangent: bfloat16 [16, 16, 32, 256], P(None, 'gx', 'gy', 'gz'), may hold values from -18 to 18
Outputs:
- grad_weight_one: float32 [16, 4, 3, 3, 3], replicated
- grad_bias_one: float32 [16], replicated
- grad_weight_two: float32 [16, 16, 3, 3, 3], replicated
- grad_bias_two: float32 [16], replicated
- grad_volume: float32 [4, 16, 32, 256], P(None, 'gx', 'gy', 'gz')
The draws below stay inside these ranges and needn't reach their ends.
All inputs are finite; a program needn't handle non-finite values.
Results may differ from the reference program's by a relative error of at most 0.0055.
Values may be sent and summed in bfloat16 or wider, within the bound.
No kernel may reach another device: no remote copies, remote signals or barrier semaphores. Data moves between devices by JAX's collectives and lax.ppermute only.
A program may use at most 64 MiB of HBM per device.

```python
import math
import jax
import jax.numpy as jnp
from jax import lax

CHAN_IN = 4
CHAN = 16
NX = 16
NY = 32
NZ = 256


def draw_cotangent(key, part):
    extent = (CHAN, NX, NY, NZ)
    rising = 1.0 + 2.0 * jnp.arange(NX, dtype=jnp.float32) / (NX - 1)
    values = jax.random.normal(key, extent, jnp.float32)
    return jnp.clip(values * rising[None, :, None, None], -18.0, 18.0).astype(jnp.bfloat16)


def block_scale(own_key, dims, shards, least, top_value):
    def one(axis_at, blocks):
        heights = jax.random.uniform(jax.random.fold_in(jax.random.fold_in(own_key, 6), axis_at), (blocks,), jnp.float32, least / len(shards), top_value / len(shards))
        return jnp.repeat(jnp.exp(heights), dims[axis_at] // blocks).reshape((-1,) + (1,) * (len(dims) - axis_at - 1))

    level = one(*shards[0])
    for cut in shards[1:]:
        level = level * one(*cut)
    return level


def normal_values(own_key, shape, spread, limit, cuts=(), kind=jnp.bfloat16):
    factor_of = block_scale(own_key, shape, cuts, -0.22, 0.18) if cuts else 1.0
    array = jax.random.normal(own_key, shape, jnp.float32) * spread * factor_of
    return jnp.minimum(jnp.maximum(array, -limit), limit).astype(kind)


def setup_inputs(seed: int = 0) -> dict:
    arg_keys = jax.random.split(jax.random.key(seed), 7)
    return {
        "volume": normal_values(arg_keys[0], (CHAN_IN, NX, NY, NZ), 1.0, 6.0, ((1, 4), (2, 4), (3, 2))),
        "act_one": normal_values(arg_keys[1], (CHAN, NX, NY, NZ), 1.0, 6.0, ((1, 4), (2, 4), (3, 2))),
        "act_two": normal_values(arg_keys[2], (CHAN, NX, NY, NZ), 1.0, 6.0, ((1, 4), (2, 4), (3, 2))),
        "weight_one": normal_values(arg_keys[3], (CHAN, CHAN_IN, 3, 3, 3), (CHAN_IN * 27) ** -0.5, 0.625),
        "weight_two": normal_values(arg_keys[4], (CHAN, CHAN, 3, 3, 3), (CHAN * 27) ** -0.5, 0.3125),
        "cotangent": draw_cotangent(jax.random.fold_in(arg_keys[6], 71), 0),
    }


def slope_of(saved):
    return jnp.where(saved > 0, 1.0, 0.3).astype(jnp.float32)

def tap_list():
    return [(tap_x, tap_y, tap_z) for tap_x in range(3) for tap_y in range(3) for tap_z in range(3)]

def weight_grad(delta, source):
    outputs = delta.shape[0]
    inputs = source.shape[0]
    flat_delta = delta.reshape(outputs, -1)
    columns = []
    for tap_x, tap_y, tap_z in tap_list():
        shifted = jnp.roll(source, (1 - tap_x, 1 - tap_y, 1 - tap_z), axis=(1, 2, 3))
        columns.append(jnp.dot(flat_delta, shifted.reshape(inputs, -1).T, preferred_element_type=jnp.float32))
    return jnp.stack(columns, -1).reshape(outputs, inputs, 3, 3, 3)

def back_through(weights, delta):
    outputs = delta.shape[0]
    inputs = weights.shape[1]
    total = jnp.zeros((inputs, delta.shape[1] * delta.shape[2] * delta.shape[3]), jnp.float32)
    for tap_x, tap_y, tap_z in tap_list():
        shifted = jnp.roll(delta, (tap_x - 1, tap_y - 1, tap_z - 1), axis=(1, 2, 3))
        total = total + jnp.dot(weights[:, :, tap_x, tap_y, tap_z].T, shifted.reshape(outputs, -1), preferred_element_type=jnp.float32)
    return total.reshape((inputs,) + delta.shape[1:])

def reference(volume, act_one, act_two, weight_one, weight_two, cotangent):
    norm = 1.0 / math.sqrt(NX * NY * NZ)
    delta_two = (cotangent.astype(jnp.float32) * slope_of(act_two)).astype(jnp.bfloat16)
    grad_bias_two = lax.optimization_barrier(jnp.sum(delta_two.astype(jnp.float32), axis=(1, 2, 3))) * norm
    grad_weight_two = weight_grad(delta_two, act_one) * norm
    back = back_through(weight_two, delta_two)
    delta_one = (back * slope_of(act_one)).astype(jnp.bfloat16)
    grad_bias_one = lax.optimization_barrier(jnp.sum(delta_one.astype(jnp.float32), axis=(1, 2, 3))) * norm
    grad_weight_one = weight_grad(delta_one, volume) * norm
    grad_volume = back_through(weight_one, delta_one)
    return (grad_weight_one, grad_bias_one, grad_weight_two, grad_bias_two, grad_volume)
```

```python
import math

import jax
import jax.numpy as jnp
from jax import lax
from jax.experimental import pallas as pl
from jax.experimental.pallas import tpu as pltpu
from jax.sharding import PartitionSpec as P

AXES = ("gx", "gy", "gz")
F32 = jnp.float32
BF16 = jnp.bfloat16
LANES = 128


def lane_ids(rows):
    return lax.broadcasted_iota(jnp.int32, (rows, LANES), 1)


def slope(saved):
    return jnp.where(saved > 0, 1.0, 0.3).astype(F32)


def put_edges(packed, block, spot):
    lane = lane_ids(block.shape[0])
    moved = pltpu.roll(block, (2 * spot + 1) % LANES, 1)
    return jnp.where((lane == 2 * spot) | (lane == 2 * spot + 1), moved, packed)


def z_shifts(block, edges, spot):
    lane = lane_ids(block.shape[0])
    near = pltpu.roll(edges, (LANES - 2 * spot - 1) % LANES, 1)
    after = pltpu.roll(jnp.where(lane == 0, near, block), LANES - 1, 1)
    before = pltpu.roll(jnp.where(lane == LANES - 1, near, block), 1, 1)
    return before, after


def prep_body(nx, ny, cot_ref, act_two_ref, act_one_ref, vol_ref, delta_ref, act_ref, edge_ref):
    chan = cot_ref.shape[0]
    edges = jnp.zeros((chan, LANES), F32)
    vol_edges = jnp.zeros((8, LANES), F32)
    for x in range(nx):
        delta = cot_ref[:, x].astype(F32) * slope(act_two_ref[:, x].astype(F32))
        delta = jnp.swapaxes(delta, 0, 1)
        act = jnp.swapaxes(act_one_ref[:, x].astype(F32), 0, 1)
        for y in range(ny):
            spot = x * ny + y
            delta_ref[spot] = delta[y].astype(BF16)
            act_ref[spot] = act[y].astype(BF16)
            edges = put_edges(edges, delta[y], spot)
        vol = vol_rows(vol_ref, x)
        for y in range(ny):
            vol_edges = put_edges(vol_edges, vol[y], nx * ny + x * ny + y)
    vol_edges = jnp.concatenate([vol_edges] * (chan // 8), 0)
    half = lane_ids(chan) < 2 * nx * ny
    edge_ref[...] = jnp.where(half, edges, vol_edges).astype(BF16)


def vol_rows(vol_ref, x):
    vol = vol_ref[:, x].astype(F32)
    rest = jnp.ones((8 - vol.shape[0],) + vol.shape[1:], F32)
    return jnp.swapaxes(jnp.concatenate([vol, rest], 0), 0, 1)


def pack_x_body(nx, ny, delta_ref, act_ref, edge_ref, low_ref, high_ref):
    for y in range(ny):
        for k in range(2):
            low_ref[k * ny + y] = delta_ref[k * ny + y]
            high_ref[k * ny + y] = delta_ref[(nx - 2 + k) * ny + y]
        low_ref[2 * ny + y] = act_ref[y]
        high_ref[2 * ny + y] = act_ref[(nx - 1) * ny + y]
    low_ref[3 * ny] = edge_ref[...]
    high_ref[3 * ny] = edge_ref[...]


def pack_y_body(nx, ny, delta_ref, act_ref, edge_ref, left_ref, right_ref, low_ref, high_ref):
    def delta_at(wide, y):
        if wide < 2:
            return left_ref[wide * ny + y]
        if wide < nx + 2:
            return delta_ref[(wide - 2) * ny + y]
        return right_ref[(wide - nx - 2) * ny + y]

    def act_at(wide, y):
        if wide == 0:
            return left_ref[2 * ny + y]
        if wide == nx + 1:
            return right_ref[2 * ny + y]
        return act_ref[(wide - 1) * ny + y]

    for wide in range(nx + 4):
        for k in range(2):
            low_ref[2 * wide + k] = delta_at(wide, k)
            high_ref[2 * wide + k] = delta_at(wide, ny - 2 + k)
    base = 2 * (nx + 4)
    for wide in range(nx + 2):
        low_ref[base + wide] = act_at(wide, 0)
        high_ref[base + wide] = act_at(wide, ny - 1)
    base += nx + 2
    for ref in (low_ref, high_ref):
        ref[base] = left_ref[3 * ny]
        ref[base + 1] = edge_ref[...]
        ref[base + 2] = right_ref[3 * ny]


def main_body(
    nx, ny, delta_ref, act_ref, edge_ref, left_ref, right_ref, up_ref, down_ref, vol_ref, w_ref,
    sums_ref, one_ref, one_edge_ref, shifted, act_wide, grad_two,
):
    wide_y = ny + 4
    acts_base = 2 * (nx + 4)
    edge_base = acts_base + nx + 2
    for wide in range(nx + 4):
        if wide < 2:
            piece, row, part = left_ref, wide, 0
            own_edges = left_ref[3 * ny]
            edge_x = nx - 2 + wide
        elif wide < nx + 2:
            piece, row, part = delta_ref, wide - 2, 1
            own_edges = edge_ref[...]
            edge_x = wide - 2
        else:
            piece, row, part = right_ref, wide - nx - 2, 2
            own_edges = right_ref[3 * ny]
            edge_x = wide - nx - 2
        for tall in range(wide_y):
            if tall < 2:
                block = up_ref[2 * wide + tall]
                edges = up_ref[edge_base + part]
                edge_y = ny - 2 + tall
            elif tall < ny + 2:
                block = piece[row * ny + tall - 2]
                edges = own_edges
                edge_y = tall - 2
            else:
                block = down_ref[2 * wide + tall - ny - 2]
                edges = down_ref[edge_base + part]
                edge_y = tall - ny - 2
            before, after = z_shifts(block, edges, edge_x * ny + edge_y)
            at = slice(tall * LANES, (tall + 1) * LANES)
            shifted[0, wide, :, at] = after
            shifted[1, wide, :, at] = block
            shifted[2, wide, :, at] = before
    for wide in range(nx + 2):
        act_wide[wide, :, 0:LANES] = up_ref[acts_base + wide]
        act_wide[wide, :, (ny + 1) * LANES : (ny + 2) * LANES] = down_ref[acts_base + wide]
        for y in range(ny):
            if wide == 0:
                block = left_ref[2 * ny + y]
            elif wide == nx + 1:
                block = right_ref[2 * ny + y]
            else:
                block = act_ref[(wide - 1) * ny + y]
            act_wide[wide, :, (y + 1) * LANES : (y + 2) * LANES] = block

    span = (ny + 2) * LANES
    inner = slice(LANES, (ny + 1) * LANES)
    weights = w_ref[...]
    chan = act_wide.shape[1]
    one_edges = jnp.zeros((chan, LANES), F32)
    total_two = None
    for wide in range(nx + 2):
        rows = jnp.concatenate(
            [
                shifted[c, wide + 2 - a, :, (2 - b) * LANES : (2 - b) * LANES + span]
                for a in range(3)
                for b in range(3)
                for c in range(3)
            ],
            0,
        )
        back = jnp.dot(weights, rows, preferred_element_type=F32)
        acts = act_wide[wide]
        delta = back * slope(acts.astype(F32))
        one_ref[wide] = delta.astype(BF16)
        for tall in range(ny + 2):
            one_edges = put_edges(
                one_edges, delta[:, tall * LANES : (tall + 1) * LANES], wide * (ny + 2) + tall
            )
        if 1 <= wide <= nx:
            term = lax.dot_general(
                rows[:, inner], acts[:, inner], (((1,), (1,)), ((), ())), preferred_element_type=F32
            )
            total_two = term if total_two is None else total_two + term
    one_edge_ref[...] = one_edges.astype(BF16)

    total_one = None
    for x in range(nx):
        vol = vol_rows(vol_ref, x)
        shifts = [[], [], []]
        for y in range(ny):
            spot = nx * ny + x * ny + y
            before, after = z_shifts(vol[y], edge_ref[0:8].astype(F32), spot)
            shifts[0].append(before)
            shifts[1].append(vol[y])
            shifts[2].append(after)
        lhs = jnp.concatenate([jnp.concatenate(row, 1) for row in shifts] + [jnp.zeros((8, ny * LANES), F32)], 0)
        rhs = jnp.concatenate(
            [
                one_ref[x + 2 - a, :, (2 - b) * LANES : (2 - b) * LANES + ny * LANES]
                for a in range(3)
                for b in range(3)
            ]
            + [shifted[1, x + 2, :, 2 * LANES : (ny + 2) * LANES]],
            0,
        )
        term = lax.dot_general(
            lhs.astype(BF16), rhs, (((1,), (1,)), ((), ())), preferred_element_type=F32
        )
        total_one = term if total_one is None else total_one + term

    grad_two[:, 0:chan] = total_two
    lane = lane_ids(8)
    slots = grad_two.shape[0] // 8
    per = LANES // chan
    for group in range(-(-slots // per)):
        packed = jnp.zeros((8, LANES), F32)
        for s in range(per):
            slot = group * per + s
            if slot < slots:
                moved = grad_two[slot * 8 : slot * 8 + 8, :]
                if s:
                    moved = pltpu.roll(moved, chan * s, 1)
                packed = jnp.where((lane >= chan * s) & (lane < chan * (s + 1)), moved, packed)
        sums_ref[group * 8 : group * 8 + 8, :] = packed
    base = -(-slots // per) * 8
    width = total_one.shape[1]
    tail = jnp.zeros((8, 2 * LANES - width), F32)
    tiles = [jnp.concatenate([total_one[8 * c : 8 * c + 8], tail], 1) for c in range(3)]
    head = lax.broadcasted_iota(jnp.int32, (8, 2 * LANES), 0) < 4
    first = jnp.where(head, tiles[0], pltpu.roll(tiles[1], 4, 0))
    second = jnp.where(head, tiles[2], tiles[1])
    for k in range(2):
        sums_ref[base + 16 * k : base + 16 * k + 8, :] = first[:, k * LANES : (k + 1) * LANES]
        sums_ref[base + 16 * k + 8 : base + 16 * k + 16, :] = second[:, k * LANES : (k + 1) * LANES]


def unpack_body(norm, sums_ref, one_ref, bias_one_ref, two_ref, bias_two_ref):
    chan = two_ref.shape[2]
    per = LANES // chan
    slots = 2 * two_ref.shape[0]
    for slot in range(slots):
        group, s = divmod(slot, per)
        block = sums_ref[group * 8 : group * 8 + 8, :] * norm
        if s:
            block = pltpu.roll(block, LANES - chan * s, 1)
        two_ref[slot // 2, (slot % 2) * 8 : (slot % 2) * 8 + 8, :] = block[:, :chan]
    base = -(-slots // per) * 8
    tiles = [sums_ref[base + 8 * k : base + 8 * k + 8, :] * norm for k in range(4)]

    def piece(k, index):
        block = tiles[2 * (index // per) + k]
        s = index % per
        return pltpu.roll(block, LANES - chan * s, 1) if s else block

    ins = one_ref.shape[1]
    for ab in range(9):
        first = piece(0, ab)
        second = piece(1, ab)
        one_ref[3 * ab] = first[0:ins, :chan]
        one_ref[3 * ab + 1] = first[4 : 4 + ins, :chan]
        one_ref[3 * ab + 2] = second[0:ins, :chan]
    bias_one_ref[...] = piece(1, 4)[4:5, :chan]
    bias_two_ref[...] = piece(1, 9)[4:5, :chan]


def volume_body(nx, ny, one_ref, edge_ref, w_ref, out_ref, shifted):
    for wide in range(nx + 2):
        for tall in range(ny + 2):
            at = slice(tall * LANES, (tall + 1) * LANES)
            block = one_ref[wide, :, at]
            before, after = z_shifts(block, edge_ref[...], wide * (ny + 2) + tall)
            shifted[0, wide, :, at] = after
            shifted[1, wide, :, at] = before
    weights = w_ref[...]
    ins = out_ref.shape[0]
    for x in range(nx):
        rows = []
        for a in range(3):
            for b in range(3):
                at = slice((2 - b) * LANES, (2 - b + ny) * LANES)
                rows += [shifted[0, x + 2 - a, :, at], one_ref[x + 2 - a, :, at], shifted[1, x + 2 - a, :, at]]
        grad = jnp.dot(weights, jnp.concatenate(rows, 0), preferred_element_type=F32)
        stack = jnp.stack([grad[:8, y * LANES : (y + 1) * LANES] for y in range(ny)], 0)
        out_ref[:, x] = jnp.swapaxes(stack, 0, 1)[:ins]


def ring(axis, step):
    count = lax.axis_size(axis)
    return [(i, (i + step) % count) for i in range(count)]


def swap_edges(edges):
    if lax.axis_size("gz") == 2:
        return lax.ppermute(edges, "gz", ring("gz", 1))
    before = lax.ppermute(edges, "gz", ring("gz", 1))
    after = lax.ppermute(edges, "gz", ring("gz", -1))
    even = lax.broadcasted_iota(jnp.int32, edges.shape, 1) % 2 == 0
    return jnp.where(even, before, after)


def sum_over(total, axis):
    count = lax.axis_size(axis)
    step = 1
    while step < count:
        total = total + lax.ppermute(total, axis, [(i, i ^ step) for i in range(count)])
        step *= 2
    return total


def local(volume, act_one, act_two, weight_one, weight_two, cotangent):
    chan, nx, ny, nz = act_one.shape
    ins = volume.shape[0]
    cells = nx * ny * nz
    for axis in AXES:
        cells *= lax.axis_size(axis)
    norm = 1.0 / math.sqrt(cells)
    flat_two = jnp.transpose(weight_two, (1, 2, 3, 4, 0)).reshape(chan, 27 * chan)
    flat_one = jnp.transpose(weight_one, (1, 2, 3, 4, 0)).reshape(ins, 27 * chan)
    flat_one = jnp.pad(flat_one, ((0, chan - ins), (0, 0)))
    blocks = jax.ShapeDtypeStruct((nx * ny, chan, LANES), BF16)
    edge = jax.ShapeDtypeStruct((chan, LANES), BF16)

    def call(body, out_shape, scratch, flops, *args):
        many = isinstance(out_shape, (tuple, list))
        spec = pl.BlockSpec(memory_space=pltpu.VMEM)
        return pl.pallas_call(
            body,
            out_shape=out_shape,
            in_specs=[spec] * len(args),
            out_specs=[spec] * len(out_shape) if many else spec,
            scratch_shapes=scratch,
            cost_estimate=pl.CostEstimate(flops=flops, bytes_accessed=1 << 18, transcendentals=0),
        )(*args)

    delta, act, edges = call(
        lambda *refs: prep_body(nx, ny, *refs),
        (blocks, blocks, edge),
        [],
        1 << 20,
        cotangent, act_two, act_one, volume,
    )
    edges = swap_edges(edges)
    side = jax.ShapeDtypeStruct((3 * ny + 1, chan, LANES), BF16)
    low, high = call(
        lambda *refs: pack_x_body(nx, ny, *refs), (side, side), [], 1 << 20, delta, act, edges
    )
    right = lax.ppermute(low, "gx", ring("gx", -1))
    left = lax.ppermute(high, "gx", ring("gx", 1))
    side = jax.ShapeDtypeStruct((2 * (nx + 4) + nx + 2 + 3, chan, LANES), BF16)
    low, high = call(
        lambda *refs: pack_y_body(nx, ny, *refs), (side, side), [], 1 << 20,
        delta, act, edges, left, right,
    )
    down = lax.ppermute(low, "gy", ring("gy", -1))
    up = lax.ppermute(high, "gy", ring("gy", 1))
    slots = 27 * chan // 8
    rows = -(-slots // (LANES // chan)) * 8 + 32
    sums, one, one_edges = call(
        lambda *refs: main_body(nx, ny, *refs),
        (
            jax.ShapeDtypeStruct((rows, LANES), F32),
            jax.ShapeDtypeStruct((nx + 2, chan, (ny + 2) * LANES), BF16),
            edge,
        ),
        [
            pltpu.VMEM((3, nx + 4, chan, (ny + 4) * LANES), BF16),
            pltpu.VMEM((nx + 2, chan, (ny + 2) * LANES), BF16),
            pltpu.VMEM((27 * chan, LANES), F32),
        ],
        1 << 28,
        delta, act, edges, left, right, up, down, volume, flat_two,
    )
    one_edges = swap_edges(one_edges)
    grad_volume = call(
        lambda *refs: volume_body(nx, ny, *refs),
        jax.ShapeDtypeStruct(volume.shape, F32),
        [pltpu.VMEM((2, nx + 2, chan, (ny + 2) * LANES), BF16)],
        1 << 27,
        one, one_edges, flat_one,
    )
    for axis in ("gx", "gz", "gy"):
        sums = sum_over(sums, axis)
    grad_one, bias_one, grad_two, bias_two = call(
        lambda *refs: unpack_body(norm, *refs),
        (
            jax.ShapeDtypeStruct((27, ins, chan), F32),
            jax.ShapeDtypeStruct((1, chan), F32),
            jax.ShapeDtypeStruct((27, chan, chan), F32),
            jax.ShapeDtypeStruct((1, chan), F32),
        ),
        [],
        1 << 20,
        sums,
    )
    grad_one = jnp.transpose(grad_one.reshape(3, 3, 3, ins, chan), (4, 3, 0, 1, 2))
    grad_two = jnp.transpose(grad_two.reshape(3, 3, 3, chan, chan), (3, 4, 0, 1, 2))
    return (grad_one, bias_one.reshape(chan), grad_two, bias_two.reshape(chan), grad_volume)


def solution(mesh):
    placed = P(None, *AXES)
    return jax.shard_map(
        local,
        mesh=mesh,
        in_specs=(placed, placed, placed, P(), P(), placed),
        out_specs=(P(), P(), P(), P(), placed),
        check_vma=False,
    )
```

```python
import math

import jax
import jax.numpy as jnp
from jax import lax
from jax.experimental import pallas as pl
from jax.experimental.pallas import tpu as pltpu
from jax.sharding import PartitionSpec as P

AXES = ("gx", "gy", "gz")
F32 = jnp.float32
BF16 = jnp.bfloat16
LANES = 128


def lane_ids(rows):
    return lax.broadcasted_iota(jnp.int32, (rows, LANES), 1)


def slope(saved):
    return jnp.where(saved > 0, 1.0, 0.3).astype(F32)


def put_edges(packed, block, spot):
    lane = lane_ids(block.shape[0])
    moved = pltpu.roll(block, (2 * spot + 1) % LANES, 1)
    return jnp.where((lane == 2 * spot) | (lane == 2 * spot + 1), moved, packed)


def z_shifts(block, edges, spot):
    lane = lane_ids(block.shape[0])
    near = pltpu.roll(edges, (LANES - 2 * spot - 1) % LANES, 1)
    after = pltpu.roll(jnp.where(lane == 0, near, block), LANES - 1, 1)
    before = pltpu.roll(jnp.where(lane == LANES - 1, near, block), 1, 1)
    return before, after


def prep_body(nx, ny, cot_ref, act_two_ref, act_one_ref, vol_ref, delta_ref, act_ref, edge_ref):
    chan = cot_ref.shape[0]
    edges = jnp.zeros((chan, LANES), F32)
    vol_edges = jnp.zeros((8, LANES), F32)
    for x in range(nx):
        delta = cot_ref[:, x].astype(F32) * slope(act_two_ref[:, x].astype(F32))
        delta = jnp.swapaxes(delta, 0, 1)
        act = jnp.swapaxes(act_one_ref[:, x].astype(F32), 0, 1)
        for y in range(ny):
            spot = x * ny + y
            delta_ref[spot] = delta[y].astype(BF16)
            act_ref[spot] = act[y].astype(BF16)
            edges = put_edges(edges, delta[y], spot)
        vol = vol_rows(vol_ref, x)
        for y in range(ny):
            vol_edges = put_edges(vol_edges, vol[y], nx * ny + x * ny + y)
    vol_edges = jnp.concatenate([vol_edges] * (chan // 8), 0)
    half = lane_ids(chan) < 2 * nx * ny
    edge_ref[...] = jnp.where(half, edges, vol_edges).astype(BF16)


def vol_rows(vol_ref, x):
    vol = vol_ref[:, x].astype(F32)
    rest = jnp.ones((8 - vol.shape[0],) + vol.shape[1:], F32)
    return jnp.swapaxes(jnp.concatenate([vol, rest], 0), 0, 1)


def pack_x_body(nx, ny, delta_ref, act_ref, edge_ref, low_ref, high_ref):
    for y in range(ny):
        for k in range(2):
            low_ref[k * ny + y] = delta_ref[k * ny + y]
            high_ref[k * ny + y] = delta_ref[(nx - 2 + k) * ny + y]
        low_ref[2 * ny + y] = act_ref[y]
        high_ref[2 * ny + y] = act_ref[(nx - 1) * ny + y]
    low_ref[3 * ny] = edge_ref[...]
    high_ref[3 * ny] = edge_ref[...]


def pack_y_body(nx, ny, delta_ref, act_ref, edge_ref, left_ref, right_ref, low_ref, high_ref):
    def delta_at(wide, y):
        if wide < 2:
            return left_ref[wide * ny + y]
        if wide < nx + 2:
            return delta_ref[(wide - 2) * ny + y]
        return right_ref[(wide - nx - 2) * ny + y]

    def act_at(wide, y):
        if wide == 0:
            return left_ref[2 * ny + y]
        if wide == nx + 1:
            return right_ref[2 * ny + y]
        return act_ref[(wide - 1) * ny + y]

    for wide in range(nx + 4):
        for k in range(2):
            low_ref[2 * wide + k] = delta_at(wide, k)
            high_ref[2 * wide + k] = delta_at(wide, ny - 2 + k)
    base = 2 * (nx + 4)
    for wide in range(nx + 2):
        low_ref[base + wide] = act_at(wide, 0)
        high_ref[base + wide] = act_at(wide, ny - 1)
    base += nx + 2
    for ref in (low_ref, high_ref):
        ref[base] = left_ref[3 * ny]
        ref[base + 1] = edge_ref[...]
        ref[base + 2] = right_ref[3 * ny]


def main_body(
    nx, ny, delta_ref, act_ref, edge_ref, left_ref, right_ref, up_ref, down_ref, vol_ref, w_ref,
    sums_ref, one_ref, one_edge_ref, shifted, act_wide, grad_two,
):
    wide_y = ny + 4
    acts_base = 2 * (nx + 4)
    edge_base = acts_base + nx + 2
    for wide in range(nx + 4):
        if wide < 2:
            piece, row, part = left_ref, wide, 0
            own_edges = left_ref[3 * ny]
            edge_x = nx - 2 + wide
        elif wide < nx + 2:
            piece, row, part = delta_ref, wide - 2, 1
            own_edges = edge_ref[...]
            edge_x = wide - 2
        else:
            piece, row, part = right_ref, wide - nx - 2, 2
            own_edges = right_ref[3 * ny]
            edge_x = wide - nx - 2
        for tall in range(wide_y):
            if tall < 2:
                block = up_ref[2 * wide + tall]
                edges = up_ref[edge_base + part]
                edge_y = ny - 2 + tall
            elif tall < ny + 2:
                block = piece[row * ny + tall - 2]
                edges = own_edges
                edge_y = tall - 2
            else:
                block = down_ref[2 * wide + tall - ny - 2]
                edges = down_ref[edge_base + part]
                edge_y = tall - ny - 2
            before, after = z_shifts(block, edges, edge_x * ny + edge_y)
            at = slice(tall * LANES, (tall + 1) * LANES)
            shifted[0, wide, :, at] = after
            shifted[1, wide, :, at] = block
            shifted[2, wide, :, at] = before
    for wide in range(nx + 2):
        act_wide[wide, :, 0:LANES] = up_ref[acts_base + wide]
        act_wide[wide, :, (ny + 1) * LANES : (ny + 2) * LANES] = down_ref[acts_base + wide]
        for y in range(ny):
            if wide == 0:
                block = left_ref[2 * ny + y]
            elif wide == nx + 1:
                block = right_ref[2 * ny + y]
            else:
                block = act_ref[(wide - 1) * ny + y]
            act_wide[wide, :, (y + 1) * LANES : (y + 2) * LANES] = block

    span = (ny + 2) * LANES
    inner = slice(LANES, (ny + 1) * LANES)
    weights = w_ref[...]
    chan = act_wide.shape[1]
    one_edges = jnp.zeros((chan, LANES), F32)
    total_two = None
    for wide in range(nx + 2):
        rows = jnp.concatenate(
            [
                shifted[c, wide + 2 - a, :, (2 - b) * LANES : (2 - b) * LANES + span]
                for a in range(3)
                for b in range(3)
                for c in range(3)
            ],
            0,
        )
        back = jnp.dot(weights, rows, preferred_element_type=F32)
        acts = act_wide[wide]
        delta = back * slope(acts.astype(F32))
        one_ref[wide] = delta.astype(BF16)
        for tall in range(ny + 2):
            one_edges = put_edges(
                one_edges, delta[:, tall * LANES : (tall + 1) * LANES], wide * (ny + 2) + tall
            )
        if 1 <= wide <= nx:
            term = lax.dot_general(
                rows[:, inner], acts[:, inner], (((1,), (1,)), ((), ())), preferred_element_type=F32
            )
            total_two = term if total_two is None else total_two + term
    one_edge_ref[...] = one_edges.astype(BF16)

    total_one = None
    for x in range(nx):
        vol = vol_rows(vol_ref, x)
        shifts = [[], [], []]
        for y in range(ny):
            spot = nx * ny + x * ny + y
            before, after = z_shifts(vol[y], edge_ref[0:8].astype(F32), spot)
            shifts[0].append(before)
            shifts[1].append(vol[y])
            shifts[2].append(after)
        lhs = jnp.concatenate([jnp.concatenate(row, 1) for row in shifts] + [jnp.zeros((8, ny * LANES), F32)], 0)
        rhs = jnp.concatenate(
            [
                one_ref[x + 2 - a, :, (2 - b) * LANES : (2 - b) * LANES + ny * LANES]
                for a in range(3)
                for b in range(3)
            ]
            + [shifted[1, x + 2, :, 2 * LANES : (ny + 2) * LANES]],
            0,
        )
        term = lax.dot_general(
            lhs.astype(BF16), rhs, (((1,), (1,)), ((), ())), preferred_element_type=F32
        )
        total_one = term if total_one is None else total_one + term

    grad_two[:, 0:chan] = total_two
    lane = lane_ids(8)
    slots = grad_two.shape[0] // 8
    per = LANES // chan
    for group in range(-(-slots // per)):
        packed = jnp.zeros((8, LANES), F32)
        for s in range(per):
            slot = group * per + s
            if slot < slots:
                moved = grad_two[slot * 8 : slot * 8 + 8, :]
                if s:
                    moved = pltpu.roll(moved, chan * s, 1)
                packed = jnp.where((lane >= chan * s) & (lane < chan * (s + 1)), moved, packed)
        sums_ref[group * 8 : group * 8 + 8, :] = packed
    base = -(-slots // per) * 8
    width = total_one.shape[1]
    tail = jnp.zeros((8, 2 * LANES - width), F32)
    tiles = [jnp.concatenate([total_one[8 * c : 8 * c + 8], tail], 1) for c in range(3)]
    head = lax.broadcasted_iota(jnp.int32, (8, 2 * LANES), 0) < 4
    first = jnp.where(head, tiles[0], pltpu.roll(tiles[1], 4, 0))
    second = jnp.where(head, tiles[2], tiles[1])
    for k in range(2):
        sums_ref[base + 16 * k : base + 16 * k + 8, :] = first[:, k * LANES : (k + 1) * LANES]
        sums_ref[base + 16 * k + 8 : base + 16 * k + 16, :] = second[:, k * LANES : (k + 1) * LANES]


def unpack_body(norm, sums_ref, one_ref, bias_one_ref, two_ref, bias_two_ref):
    chan = two_ref.shape[2]
    per = LANES // chan
    slots = 2 * two_ref.shape[0]
    for slot in range(slots):
        group, s = divmod(slot, per)
        block = sums_ref[group * 8 : group * 8 + 8, :] * norm
        if s:
            block = pltpu.roll(block, LANES - chan * s, 1)
        two_ref[slot // 2, (slot % 2) * 8 : (slot % 2) * 8 + 8, :] = block[:, :chan]
    base = -(-slots // per) * 8
    tiles = [sums_ref[base + 8 * k : base + 8 * k + 8, :] * norm for k in range(4)]

    def piece(k, index):
        block = tiles[2 * (index // per) + k]
        s = index % per
        return pltpu.roll(block, LANES - chan * s, 1) if s else block

    ins = one_ref.shape[1]
    for ab in range(9):
        first = piece(0, ab)
        second = piece(1, ab)
        one_ref[3 * ab] = first[0:ins, :chan]
        one_ref[3 * ab + 1] = first[4 : 4 + ins, :chan]
        one_ref[3 * ab + 2] = second[0:ins, :chan]
    bias_one_ref[...] = piece(1, 4)[4:5, :chan]
    bias_two_ref[...] = piece(1, 9)[4:5, :chan]


def volume_body(nx, ny, one_ref, edge_ref, w_ref, out_ref, shifted):
    for wide in range(nx + 2):
        for tall in range(ny + 2):
            at = slice(tall * LANES, (tall + 1) * LANES)
            block = one_ref[wide, :, at]
            before, after = z_shifts(block, edge_ref[...], wide * (ny + 2) + tall)
            shifted[0, wide, :, at] = after
            shifted[1, wide, :, at] = before
    weights = w_ref[...]
    ins = out_ref.shape[0]
    for x in range(nx):
        rows = []
        for a in range(3):
            for b in range(3):
                at = slice((2 - b) * LANES, (2 - b + ny) * LANES)
                rows += [shifted[0, x + 2 - a, :, at], one_ref[x + 2 - a, :, at], shifted[1, x + 2 - a, :, at]]
        grad = jnp.dot(weights, jnp.concatenate(rows, 0), preferred_element_type=F32)
        stack = jnp.stack([grad[:8, y * LANES : (y + 1) * LANES] for y in range(ny)], 0)
        out_ref[:, x] = jnp.swapaxes(stack, 0, 1)[:ins]


def ring(axis, step):
    count = lax.axis_size(axis)
    return [(i, (i + step) % count) for i in range(count)]


def swap_edges(edges):
    if lax.axis_size("gz") == 2:
        return lax.ppermute(edges, "gz", ring("gz", 1))
    before = lax.ppermute(edges, "gz", ring("gz", 1))
    after = lax.ppermute(edges, "gz", ring("gz", -1))
    even = lax.broadcasted_iota(jnp.int32, edges.shape, 1) % 2 == 0
    return jnp.where(even, before, after)


def sum_over(total, axis, step, stop=None):
    count = lax.axis_size(axis)
    while step < (count if stop is None else min(stop, count)):
        total = total + lax.ppermute(total, axis, [(i, i ^ step) for i in range(count)])
        step *= 2
    return total


def near(array):
    return pltpu.with_memory_space_constraint(array, pltpu.VMEM)


def call(body, out_shape, scratch, flops, *args):
    many = isinstance(out_shape, (tuple, list))
    spec = pl.BlockSpec(memory_space=pltpu.VMEM)
    return pl.pallas_call(
        body,
        out_shape=out_shape,
        in_specs=[spec] * len(args),
        out_specs=[spec] * len(out_shape) if many else spec,
        scratch_shapes=scratch,
        cost_estimate=pl.CostEstimate(flops=flops, bytes_accessed=1 << 18, transcendentals=0),
    )(*args)


def local(volume, act_one, act_two, weight_one, weight_two, cotangent):
    chan, nx, ny, nz = act_one.shape
    ins = volume.shape[0]
    cells = nx * ny * nz
    for axis in AXES:
        cells *= lax.axis_size(axis)
    norm = 1.0 / math.sqrt(cells)
    flat_two = jnp.transpose(weight_two, (1, 2, 3, 4, 0)).reshape(chan, 27 * chan)
    flat_one = jnp.transpose(weight_one, (1, 2, 3, 4, 0)).reshape(ins, 27 * chan)
    flat_one = jnp.pad(flat_one, ((0, chan - ins), (0, 0)))
    blocks = pltpu.VMEM((nx * ny, chan, LANES), BF16)
    edge = pltpu.VMEM((chan, LANES), BF16)
    flat_two = near(flat_two)
    flat_one = near(flat_one)

    delta, act, edges = call(
        lambda *refs: prep_body(nx, ny, *refs),
        (blocks, blocks, edge),
        [],
        1 << 20,
        cotangent, act_two, act_one, volume,
    )
    edges = near(swap_edges(edges))
    delta, act = near(delta), near(act)
    side = pltpu.VMEM((3 * ny + 1, chan, LANES), BF16)
    low, high = call(
        lambda *refs: pack_x_body(nx, ny, *refs), (side, side), [], 1 << 20, delta, act, edges
    )
    right = near(lax.ppermute(low, "gx", ring("gx", -1)))
    left = near(lax.ppermute(high, "gx", ring("gx", 1)))
    side = pltpu.VMEM((2 * (nx + 4) + nx + 2 + 3, chan, LANES), BF16)
    low, high = call(
        lambda *refs: pack_y_body(nx, ny, *refs), (side, side), [], 1 << 20,
        delta, act, edges, left, right,
    )
    down = near(lax.ppermute(low, "gy", ring("gy", -1)))
    up = near(lax.ppermute(high, "gy", ring("gy", 1)))
    slots = 27 * chan // 8
    rows = -(-slots // (LANES // chan)) * 8 + 32
    sums, one, one_edges = call(
        lambda *refs: main_body(nx, ny, *refs),
        (
            pltpu.VMEM((rows, LANES), F32),
            pltpu.VMEM((nx + 2, chan, (ny + 2) * LANES), BF16),
            edge,
        ),
        [
            pltpu.VMEM((3, nx + 4, chan, (ny + 4) * LANES), BF16),
            pltpu.VMEM((nx + 2, chan, (ny + 2) * LANES), BF16),
            pltpu.VMEM((27 * chan, LANES), F32),
        ],
        1 << 28,
        delta, act, edges, left, right, up, down, near(volume), flat_two,
    )
    sums = sum_over(sums, "gx", 1, 2)
    sums, one_edges = lax.optimization_barrier((sums, one_edges))
    sums = sum_over(sums, "gx", 2)
    one_edges = near(swap_edges(one_edges))
    sums = sum_over(sums, "gz", 1)
    grad_volume = call(
        lambda *refs: volume_body(nx, ny, *refs),
        jax.ShapeDtypeStruct(volume.shape, F32),
        [pltpu.VMEM((2, nx + 2, chan, (ny + 2) * LANES), BF16)],
        1 << 27,
        near(one), near(one_edges), flat_one,
    )
    sums, grad_volume = lax.optimization_barrier((sums, grad_volume))
    sums = near(sum_over(sums, "gy", 1))
    grad_one, bias_one, grad_two, bias_two = call(
        lambda *refs: unpack_body(norm, *refs),
        (
            jax.ShapeDtypeStruct((27, ins, chan), F32),
            jax.ShapeDtypeStruct((1, chan), F32),
            jax.ShapeDtypeStruct((27, chan, chan), F32),
            jax.ShapeDtypeStruct((1, chan), F32),
        ),
        [],
        1 << 20,
        sums,
    )
    grad_one = jnp.transpose(grad_one.reshape(3, 3, 3, ins, chan), (4, 3, 0, 1, 2))
    grad_two = jnp.transpose(grad_two.reshape(3, 3, 3, chan, chan), (3, 4, 0, 1, 2))
    return (grad_one, bias_one.reshape(chan), grad_two, bias_two.reshape(chan), grad_volume)


def solution(mesh):
    placed = P(None, *AXES)
    return jax.shard_map(
        local,
        mesh=mesh,
        in_specs=(placed, placed, placed, P(), P(), placed),
        out_specs=(P(), P(), P(), P(), placed),
        check_vma=False,
    )
```

```python
import math

import jax
import jax.numpy as jnp
from jax import lax
from jax.experimental import pallas as pl
from jax.experimental.pallas import tpu as pltpu
from jax.sharding import PartitionSpec as P

AXES = ("gx", "gy", "gz")
F32 = jnp.float32
BF16 = jnp.bfloat16
LANES = 128


def lane_ids(rows):
    return lax.broadcasted_iota(jnp.int32, (rows, LANES), 1)


def slope(saved):
    return jnp.where(saved > 0, 1.0, 0.3).astype(F32)


def put_edges(packed, block, spot):
    lane = lane_ids(block.shape[0])
    moved = pltpu.roll(block, (2 * spot + 1) % LANES, 1)
    return jnp.where((lane == 2 * spot) | (lane == 2 * spot + 1), moved, packed)


def z_shifts(block, edges, spot):
    lane = lane_ids(block.shape[0])
    near = pltpu.roll(edges, (LANES - 2 * spot - 1) % LANES, 1)
    after = pltpu.roll(jnp.where(lane == 0, near, block), LANES - 1, 1)
    before = pltpu.roll(jnp.where(lane == LANES - 1, near, block), 1, 1)
    return before, after


def prep_body(nx, ny, cot_ref, act_two_ref, act_one_ref, vol_ref, delta_ref, act_ref, edge_ref):
    chan = cot_ref.shape[0]
    edges = jnp.zeros((chan, LANES), F32)
    vol_edges = jnp.zeros((8, LANES), F32)
    for x in range(nx):
        delta = cot_ref[:, x].astype(F32) * slope(act_two_ref[:, x].astype(F32))
        delta = jnp.swapaxes(delta, 0, 1)
        act = jnp.swapaxes(act_one_ref[:, x].astype(F32), 0, 1)
        for y in range(ny):
            spot = x * ny + y
            delta_ref[spot] = delta[y].astype(BF16)
            act_ref[spot] = act[y].astype(BF16)
            edges = put_edges(edges, delta[y], spot)
        vol = vol_rows(vol_ref, x)
        for y in range(ny):
            vol_edges = put_edges(vol_edges, vol[y], nx * ny + x * ny + y)
    vol_edges = jnp.concatenate([vol_edges] * (chan // 8), 0)
    half = lane_ids(chan) < 2 * nx * ny
    edge_ref[...] = jnp.where(half, edges, vol_edges).astype(BF16)


def vol_rows(vol_ref, x):
    vol = vol_ref[:, x].astype(F32)
    rest = jnp.ones((8 - vol.shape[0],) + vol.shape[1:], F32)
    return jnp.swapaxes(jnp.concatenate([vol, rest], 0), 0, 1)


def pack_y_body(nx, ny, delta_ref, act_ref, edge_ref, low_ref, high_ref):
    for x in range(nx):
        for k in range(2):
            low_ref[2 * x + k] = delta_ref[x * ny + k]
            high_ref[2 * x + k] = delta_ref[x * ny + ny - 2 + k]
        low_ref[2 * nx + x] = act_ref[x * ny]
        high_ref[2 * nx + x] = act_ref[x * ny + ny - 1]
    low_ref[3 * nx] = edge_ref[...]
    high_ref[3 * nx] = edge_ref[...]


def tall_delta(ny, delta_ref, up_ref, down_ref, x, tall):
    if tall < 2:
        return up_ref[2 * x + tall]
    if tall < ny + 2:
        return delta_ref[x * ny + tall - 2]
    return down_ref[2 * x + tall - ny - 2]


def tall_act(nx, ny, act_ref, up_ref, down_ref, x, tall):
    if tall == 0:
        return up_ref[2 * nx + x]
    if tall == ny + 1:
        return down_ref[2 * nx + x]
    return act_ref[x * ny + tall - 1]


def tall_spot(nx, ny, x, tall):
    if tall < 2:
        return nx * ny + x * ny + ny - 2 + tall
    if tall < ny + 2:
        return x * ny + tall - 2
    return nx * ny + x * ny + tall - ny - 2


def pack_x_body(nx, ny, delta_ref, act_ref, edge_ref, up_ref, down_ref, low_ref, high_ref, merged_ref):
    lane = lane_ids(edge_ref.shape[0])
    half = 2 * nx * ny
    up = pltpu.roll(up_ref[3 * nx], half, 1)
    down = pltpu.roll(down_ref[3 * nx], half, 1)
    beyond = jnp.where(lax.rem(lane, 2 * ny) < ny, down, up)
    merged = jnp.where(lane < half, edge_ref[...], beyond)
    merged_ref[...] = merged
    for ref, planes, act_plane in ((low_ref, (0, 1), 0), (high_ref, (nx - 2, nx - 1), nx - 1)):
        for k in range(2):
            for tall in range(ny + 4):
                ref[k * (ny + 4) + tall] = tall_delta(ny, delta_ref, up_ref, down_ref, planes[k], tall)
        base = 2 * (ny + 4)
        for tall in range(ny + 2):
            ref[base + tall] = tall_act(nx, ny, act_ref, up_ref, down_ref, act_plane, tall)
        ref[base + ny + 2] = merged


def store_shifts(shifted, plane, tall, block, edges, spot):
    before, after = z_shifts(block, edges, spot)
    at = slice(tall * LANES, (tall + 1) * LANES)
    shifted[0, plane, :, at] = after
    shifted[1, plane, :, at] = block
    shifted[2, plane, :, at] = before


def back_plane(ny, plane_at, wide, weights, acts, one_edges, with_sum):
    span = (ny + 2) * LANES
    inner = slice(LANES, (ny + 1) * LANES)
    rows = jnp.concatenate(
        [
            plane_at(c, wide + 2 - a, slice((2 - b) * LANES, (2 - b) * LANES + span))
            for a in range(3)
            for b in range(3)
            for c in range(3)
        ],
        0,
    )
    delta = jnp.dot(weights, rows, preferred_element_type=F32) * slope(acts.astype(F32))
    for tall in range(ny + 2):
        one_edges = put_edges(
            one_edges, delta[:, tall * LANES : (tall + 1) * LANES], wide * (ny + 2) + tall
        )
    term = None
    if with_sum:
        term = lax.dot_general(
            rows[:, inner], acts[:, inner], (((1,), (1,)), ((), ())), preferred_element_type=F32
        )
    return delta.astype(BF16), one_edges, term


def add(total, term):
    return term if total is None else total + term


def inner_body(
    nx, ny, delta_ref, act_ref, edge_ref, merged_ref, up_ref, down_ref, vol_ref, w_ref,
    shifted, one_ref, one_edge_ref, two_ref, vol_out_ref,
):
    chan = edge_ref.shape[0]
    merged = merged_ref[...]
    for x in range(nx):
        for tall in range(ny + 4):
            block = tall_delta(ny, delta_ref, up_ref, down_ref, x, tall)
            store_shifts(shifted, x, tall, block, merged, tall_spot(nx, ny, x, tall))
    one_edges = jnp.zeros((chan, LANES), F32)
    total = None
    for x in range(1, nx - 1):
        acts = jnp.concatenate(
            [tall_act(nx, ny, act_ref, up_ref, down_ref, x, tall) for tall in range(ny + 2)], 1
        )
        one, one_edges, term = back_plane(
            ny, lambda c, wide, at: shifted[c, wide - 2, :, at], x + 1, w_ref[...], acts, one_edges, True
        )
        one_ref[x - 1] = one
        total = add(total, term)
    one_edge_ref[...] = one_edges
    two_ref[...] = total
    edges = edge_ref[0:8].astype(F32)
    for x in range(nx):
        vol = vol_rows(vol_ref, x)
        shifts = [[], [], []]
        for y in range(ny):
            before, after = z_shifts(vol[y], edges, nx * ny + x * ny + y)
            shifts[0].append(before)
            shifts[1].append(vol[y])
            shifts[2].append(after)
        lhs = [jnp.concatenate(row, 1) for row in shifts] + [jnp.zeros((8, ny * LANES), F32)]
        vol_out_ref[x] = jnp.concatenate(lhs, 0).astype(BF16)


def outer_body(
    nx, ny, act_ref, up_ref, down_ref, left_ref, right_ref, w_ref,
    own_ref, inner_ref, inner_edge_ref, two_ref, vol_ref,
    sums_ref, one_ref, one_edge_ref, far, grad_two,
):
    chan = act_ref.shape[1]
    base = 2 * (ny + 4)
    for side, ref in ((0, left_ref), (1, right_ref)):
        edges = ref[base + ny + 2]
        for k in range(2):
            for tall in range(ny + 4):
                from_x = nx - 2 + k if side == 0 else k
                store_shifts(
                    far, 2 * side + k, tall, ref[k * (ny + 4) + tall], edges, tall_spot(nx, ny, from_x, tall)
                )

    def plane_at(c, wide, at):
        if wide < 2:
            return far[c, wide, :, at]
        if wide < nx + 2:
            return own_ref[c, wide - 2, :, at]
        return far[c, wide - nx, :, at]

    one_edges = inner_edge_ref[...]
    total_two = two_ref[...]
    for wide in (0, 1, nx, nx + 1):
        if wide == 0:
            blocks = [left_ref[base + tall] for tall in range(ny + 2)]
        elif wide == nx + 1:
            blocks = [right_ref[base + tall] for tall in range(ny + 2)]
        else:
            blocks = [
                tall_act(nx, ny, act_ref, up_ref, down_ref, wide - 1, tall) for tall in range(ny + 2)
            ]
        acts = jnp.concatenate(blocks, 1)
        one, one_edges, term = back_plane(
            ny, plane_at, wide, w_ref[...], acts, one_edges, 1 <= wide <= nx
        )
        one_ref[wide] = one
        if term is not None:
            total_two = total_two + term
    for x in range(1, nx - 1):
        one_ref[x + 1] = inner_ref[x - 1]
    one_edge_ref[...] = one_edges.astype(BF16)

    total_one = None
    for x in range(nx):
        rhs = jnp.concatenate(
            [
                one_ref[x + 2 - a, :, (2 - b) * LANES : (2 - b + ny) * LANES]
                for a in range(3)
                for b in range(3)
            ]
            + [own_ref[1, x, :, 2 * LANES : (ny + 2) * LANES]],
            0,
        )
        term = lax.dot_general(
            vol_ref[x], rhs, (((1,), (1,)), ((), ())), preferred_element_type=F32
        )
        total_one = add(total_one, term)

    grad_two[:, 0:chan] = total_two
    lane = lane_ids(8)
    slots = grad_two.shape[0] // 8
    per = LANES // chan
    for group in range(-(-slots // per)):
        packed = jnp.zeros((8, LANES), F32)
        for s in range(per):
            slot = group * per + s
            if slot < slots:
                moved = grad_two[slot * 8 : slot * 8 + 8, :]
                if s:
                    moved = pltpu.roll(moved, chan * s, 1)
                packed = jnp.where((lane >= chan * s) & (lane < chan * (s + 1)), moved, packed)
        sums_ref[group * 8 : group * 8 + 8, :] = packed
    start = -(-slots // per) * 8
    width = total_one.shape[1]
    tail = jnp.zeros((8, 2 * LANES - width), F32)
    tiles = [jnp.concatenate([total_one[8 * c : 8 * c + 8], tail], 1) for c in range(3)]
    head = lax.broadcasted_iota(jnp.int32, (8, 2 * LANES), 0) < 4
    first = jnp.where(head, tiles[0], pltpu.roll(tiles[1], 4, 0))
    second = jnp.where(head, tiles[2], tiles[1])
    for k in range(2):
        sums_ref[start + 16 * k : start + 16 * k + 8, :] = first[:, k * LANES : (k + 1) * LANES]
        sums_ref[start + 16 * k + 8 : start + 16 * k + 16, :] = second[:, k * LANES : (k + 1) * LANES]


def unpack_body(norm, sums_ref, one_ref, bias_one_ref, two_ref, bias_two_ref):
    chan = two_ref.shape[2]
    per = LANES // chan
    slots = 2 * two_ref.shape[0]
    for slot in range(slots):
        group, s = divmod(slot, per)
        block = sums_ref[group * 8 : group * 8 + 8, :] * norm
        if s:
            block = pltpu.roll(block, LANES - chan * s, 1)
        two_ref[slot // 2, (slot % 2) * 8 : (slot % 2) * 8 + 8, :] = block[:, :chan]
    base = -(-slots // per) * 8
    tiles = [sums_ref[base + 8 * k : base + 8 * k + 8, :] * norm for k in range(4)]

    def piece(k, index):
        block = tiles[2 * (index // per) + k]
        s = index % per
        return pltpu.roll(block, LANES - chan * s, 1) if s else block

    ins = one_ref.shape[1]
    for ab in range(9):
        first = piece(0, ab)
        second = piece(1, ab)
        one_ref[3 * ab] = first[0:ins, :chan]
        one_ref[3 * ab + 1] = first[4 : 4 + ins, :chan]
        one_ref[3 * ab + 2] = second[0:ins, :chan]
    bias_one_ref[...] = piece(1, 4)[4:5, :chan]
    bias_two_ref[...] = piece(1, 9)[4:5, :chan]


def volume_body(nx, ny, one_ref, edge_ref, w_ref, out_ref, shifted):
    for wide in range(nx + 2):
        for tall in range(ny + 2):
            at = slice(tall * LANES, (tall + 1) * LANES)
            block = one_ref[wide, :, at]
            before, after = z_shifts(block, edge_ref[...], wide * (ny + 2) + tall)
            shifted[0, wide, :, at] = after
            shifted[1, wide, :, at] = before
    weights = w_ref[...]
    ins = out_ref.shape[0]
    for x in range(nx):
        rows = []
        for a in range(3):
            for b in range(3):
                at = slice((2 - b) * LANES, (2 - b + ny) * LANES)
                rows += [shifted[0, x + 2 - a, :, at], one_ref[x + 2 - a, :, at], shifted[1, x + 2 - a, :, at]]
        grad = jnp.dot(weights, jnp.concatenate(rows, 0), preferred_element_type=F32)
        stack = jnp.stack([grad[:8, y * LANES : (y + 1) * LANES] for y in range(ny)], 0)
        out_ref[:, x] = jnp.swapaxes(stack, 0, 1)[:ins]


def ring(axis, step):
    count = lax.axis_size(axis)
    return [(i, (i + step) % count) for i in range(count)]


def swap_edges(edges):
    if lax.axis_size("gz") == 2:
        return lax.ppermute(edges, "gz", ring("gz", 1))
    before = lax.ppermute(edges, "gz", ring("gz", 1))
    after = lax.ppermute(edges, "gz", ring("gz", -1))
    even = lax.broadcasted_iota(jnp.int32, edges.shape, 1) % 2 == 0
    return jnp.where(even, before, after)


def exchange_add(total, axis, step, stop=None):
    count = lax.axis_size(axis)
    rows = lax.axis_size("gx")
    while step < (count if stop is None else min(stop, count)):
        if axis == "gx":
            moved = lax.ppermute(total, "gx", [(i, i ^ step) for i in range(1, rows, 2)])
        else:
            moved = lax.ppermute(
                total,
                ("gx", axis),
                [(i * count + k, i * count + (k ^ step)) for i in range(1, rows, 2) for k in range(count)],
            )
        total = total + moved
        step *= 2
    return total


def near(array):
    return pltpu.with_memory_space_constraint(array, pltpu.VMEM)


def call(body, out_shape, scratch, flops, *args):
    many = isinstance(out_shape, (tuple, list))
    spec = pl.BlockSpec(memory_space=pltpu.VMEM)
    return pl.pallas_call(
        body,
        out_shape=out_shape,
        in_specs=[spec] * len(args),
        out_specs=[spec] * len(out_shape) if many else spec,
        scratch_shapes=scratch,
        cost_estimate=pl.CostEstimate(flops=flops, bytes_accessed=1 << 18, transcendentals=0),
    )(*args)


def local(volume, act_one, act_two, weight_one, weight_two, cotangent):
    chan, nx, ny, nz = act_one.shape
    ins = volume.shape[0]
    cells = nx * ny * nz
    for axis in AXES:
        cells *= lax.axis_size(axis)
    norm = 1.0 / math.sqrt(cells)
    flat_two = jnp.transpose(weight_two, (1, 2, 3, 4, 0)).reshape(chan, 27 * chan)
    flat_one = jnp.transpose(weight_one, (1, 2, 3, 4, 0)).reshape(ins, 27 * chan)
    flat_one = jnp.pad(flat_one, ((0, chan - ins), (0, 0)))
    blocks = pltpu.VMEM((nx * ny, chan, LANES), BF16)
    edge = pltpu.VMEM((chan, LANES), BF16)
    flat_two = near(flat_two)
    flat_one = near(flat_one)

    delta, act, edges = call(
        lambda *refs: prep_body(nx, ny, *refs),
        (blocks, blocks, edge),
        [],
        1 << 20,
        cotangent, act_two, act_one, volume,
    )
    edges = near(swap_edges(edges))
    delta, act = near(delta), near(act)
    side = pltpu.VMEM((3 * nx + 1, chan, LANES), BF16)
    low, high = call(
        lambda *refs: pack_y_body(nx, ny, *refs), (side, side), [], 1 << 20, delta, act, edges
    )
    down = near(lax.ppermute(low, "gy", ring("gy", -1)))
    up = near(lax.ppermute(high, "gy", ring("gy", 1)))
    side = pltpu.VMEM((3 * (ny + 4) - 1, chan, LANES), BF16)
    low, high, merged = call(
        lambda *refs: pack_x_body(nx, ny, *refs), (side, side, edge), [], 1 << 20,
        delta, act, edges, up, down,
    )
    right = near(lax.ppermute(low, "gx", ring("gx", -1)))
    left = near(lax.ppermute(high, "gx", ring("gx", 1)))
    span = (ny + 2) * LANES
    own, inner, inner_edges, inner_two, vols = call(
        lambda *refs: inner_body(nx, ny, *refs),
        (
            pltpu.VMEM((3, nx, chan, (ny + 4) * LANES), BF16),
            pltpu.VMEM((nx - 2, chan, span), BF16),
            pltpu.VMEM((chan, LANES), F32),
            pltpu.VMEM((27 * chan, chan), F32),
            pltpu.VMEM((nx, 32, ny * LANES), BF16),
        ),
        [],
        1 << 27,
        delta, act, edges, near(merged), up, down, near(volume), flat_two,
    )
    slots = 27 * chan // 8
    rows = -(-slots // (LANES // chan)) * 8 + 32
    sums, one, one_edges = call(
        lambda *refs: outer_body(nx, ny, *refs),
        (
            pltpu.VMEM((rows, LANES), F32),
            pltpu.VMEM((nx + 2, chan, span), BF16),
            edge,
        ),
        [
            pltpu.VMEM((3, 4, chan, (ny + 4) * LANES), BF16),
            pltpu.VMEM((27 * chan, LANES), F32),
        ],
        1 << 28,
        act, up, down, left, right, flat_two,
        near(own), near(inner), near(inner_edges), near(inner_two), near(vols),
    )
    across = lax.axis_size("gx")
    sums = sums + lax.ppermute(sums, "gx", [(i - 1, i) for i in range(1, across, 2)])
    sums, one_edges = lax.optimization_barrier((sums, one_edges))
    sums = exchange_add(sums, "gx", 2)
    one_edges = near(swap_edges(one_edges))
    sums = exchange_add(sums, "gz", 1)
    grad_volume = call(
        lambda *refs: volume_body(nx, ny, *refs),
        jax.ShapeDtypeStruct(volume.shape, F32),
        [pltpu.VMEM((2, nx + 2, chan, span), BF16)],
        1 << 27,
        near(one), near(one_edges), flat_one,
    )
    sums, grad_volume = lax.optimization_barrier((sums, grad_volume))
    sums = exchange_add(sums, "gy", 1)
    back = lax.ppermute(sums, "gx", [(i, i - 1) for i in range(1, across, 2)])
    sums = near(jnp.where(lax.axis_index("gx") % 2 == 1, sums, back))
    grad_one, bias_one, grad_two, bias_two = call(
        lambda *refs: unpack_body(norm, *refs),
        (
            jax.ShapeDtypeStruct((27, ins, chan), F32),
            jax.ShapeDtypeStruct((1, chan), F32),
            jax.ShapeDtypeStruct((27, chan, chan), F32),
            jax.ShapeDtypeStruct((1, chan), F32),
        ),
        [],
        1 << 20,
        sums,
    )
    grad_one = jnp.transpose(grad_one.reshape(3, 3, 3, ins, chan), (4, 3, 0, 1, 2))
    grad_two = jnp.transpose(grad_two.reshape(3, 3, 3, chan, chan), (3, 4, 0, 1, 2))
    return (grad_one, bias_one.reshape(chan), grad_two, bias_two.reshape(chan), grad_volume)


def solution(mesh):
    placed = P(None, *AXES)
    return jax.shard_map(
        local,
        mesh=mesh,
        in_specs=(placed, placed, placed, P(), P(), placed),
        out_specs=(P(), P(), P(), P(), placed),
        check_vma=False,
    )
```

```python
import math

import jax
import jax.numpy as jnp
from jax import lax
from jax.experimental import pallas as pl
from jax.experimental.pallas import tpu as pltpu
from jax.sharding import PartitionSpec as P

AXES = ("gx", "gy", "gz")
F32 = jnp.float32
BF16 = jnp.bfloat16
LANES = 128


def lane_ids(rows):
    return lax.broadcasted_iota(jnp.int32, (rows, LANES), 1)


def slope(saved):
    return jnp.where(saved > 0, 1.0, 0.3).astype(F32)


def put_edges(packed, block, spot):
    lane = lane_ids(block.shape[0])
    moved = pltpu.roll(block, (2 * spot + 1) % LANES, 1)
    return jnp.where((lane == 2 * spot) | (lane == 2 * spot + 1), moved, packed)


def z_shifts(block, edges, spot):
    lane = lane_ids(block.shape[0])
    near = pltpu.roll(edges, (LANES - 2 * spot - 1) % LANES, 1)
    after = pltpu.roll(jnp.where(lane == 0, near, block), LANES - 1, 1)
    before = pltpu.roll(jnp.where(lane == LANES - 1, near, block), 1, 1)
    return before, after


def prep_body(nx, ny, cot_ref, act_two_ref, act_one_ref, vol_ref, delta_ref, act_ref, edge_ref, rows_ref):
    chan = cot_ref.shape[0]
    edges = jnp.zeros((chan, LANES), F32)
    vol_edges = jnp.zeros((8, LANES), F32)
    for x in range(nx):
        delta = cot_ref[:, x].astype(F32) * slope(act_two_ref[:, x].astype(F32))
        delta = jnp.swapaxes(delta, 0, 1)
        act = jnp.swapaxes(act_one_ref[:, x].astype(F32), 0, 1)
        for y in range(ny):
            spot = x * ny + y
            delta_ref[spot] = delta[y].astype(BF16)
            act_ref[spot] = act[y].astype(BF16)
            edges = put_edges(edges, delta[y], spot)
        vol = vol_rows(vol_ref, x)
        for y in range(ny):
            rows_ref[x, y] = vol[y]
            vol_edges = put_edges(vol_edges, vol[y], nx * ny + x * ny + y)
    vol_edges = jnp.concatenate([vol_edges] * (chan // 8), 0)
    half = lane_ids(chan) < 2 * nx * ny
    edge_ref[...] = jnp.where(half, edges, vol_edges).astype(BF16)


def vol_rows(vol_ref, x):
    vol = vol_ref[:, x].astype(F32)
    rest = jnp.ones((8 - vol.shape[0],) + vol.shape[1:], F32)
    return jnp.swapaxes(jnp.concatenate([vol, rest], 0), 0, 1)


def pack_y_body(nx, ny, delta_ref, act_ref, edge_ref, low_ref, high_ref):
    for x in range(nx):
        for k in range(2):
            low_ref[2 * x + k] = delta_ref[x * ny + k]
            high_ref[2 * x + k] = delta_ref[x * ny + ny - 2 + k]
        low_ref[2 * nx + x] = act_ref[x * ny]
        high_ref[2 * nx + x] = act_ref[x * ny + ny - 1]
    low_ref[3 * nx] = edge_ref[...]
    high_ref[3 * nx] = edge_ref[...]


def tall_delta(ny, delta_ref, up_ref, down_ref, x, tall):
    if tall < 2:
        return up_ref[2 * x + tall]
    if tall < ny + 2:
        return delta_ref[x * ny + tall - 2]
    return down_ref[2 * x + tall - ny - 2]


def tall_act(nx, ny, act_ref, up_ref, down_ref, x, tall):
    if tall == 0:
        return up_ref[2 * nx + x]
    if tall == ny + 1:
        return down_ref[2 * nx + x]
    return act_ref[x * ny + tall - 1]


def tall_spot(nx, ny, x, tall):
    if tall < 2:
        return nx * ny + x * ny + ny - 2 + tall
    if tall < ny + 2:
        return x * ny + tall - 2
    return nx * ny + x * ny + tall - ny - 2


def pack_x_body(nx, ny, delta_ref, act_ref, edge_ref, up_ref, down_ref, low_ref, high_ref, merged_ref):
    lane = lane_ids(edge_ref.shape[0])
    half = 2 * nx * ny
    up = pltpu.roll(up_ref[3 * nx], half, 1)
    down = pltpu.roll(down_ref[3 * nx], half, 1)
    beyond = jnp.where(lax.rem(lane, 2 * ny) < ny, down, up)
    merged = jnp.where(lane < half, edge_ref[...], beyond)
    merged_ref[...] = merged
    for ref, planes, act_plane in ((low_ref, (0, 1), 0), (high_ref, (nx - 2, nx - 1), nx - 1)):
        for k in range(2):
            for tall in range(ny + 4):
                ref[k * (ny + 4) + tall] = tall_delta(ny, delta_ref, up_ref, down_ref, planes[k], tall)
        base = 2 * (ny + 4)
        for tall in range(ny + 2):
            ref[base + tall] = tall_act(nx, ny, act_ref, up_ref, down_ref, act_plane, tall)
        ref[base + ny + 2] = merged


def store_shifts(shifted, plane, tall, block, edges, spot):
    before, after = z_shifts(block, edges, spot)
    at = slice(tall * LANES, (tall + 1) * LANES)
    shifted[0, plane, :, at] = after
    shifted[1, plane, :, at] = block
    shifted[2, plane, :, at] = before


def back_plane(ny, plane_at, wide, weights, acts, one_edges, with_sum):
    span = (ny + 2) * LANES
    inner = slice(LANES, (ny + 1) * LANES)
    rows = jnp.concatenate(
        [
            plane_at(c, wide + 2 - a, slice((2 - b) * LANES, (2 - b) * LANES + span))
            for a in range(3)
            for b in range(3)
            for c in range(3)
        ],
        0,
    )
    delta = jnp.dot(weights, rows, preferred_element_type=F32) * slope(acts.astype(F32))
    for tall in range(ny + 2):
        one_edges = put_edges(
            one_edges, delta[:, tall * LANES : (tall + 1) * LANES], wide * (ny + 2) + tall
        )
    term = None
    if with_sum:
        term = lax.dot_general(
            rows[:, inner], acts[:, inner], (((1,), (1,)), ((), ())), preferred_element_type=F32
        )
    return delta.astype(BF16), one_edges, term


def add(total, term):
    return term if total is None else total + term


def inner_body(
    nx, ny, delta_ref, act_ref, edge_ref, merged_ref, up_ref, down_ref, vol_ref, w_ref,
    shifted, one_ref, one_edge_ref, two_ref, vol_out_ref,
):
    chan = edge_ref.shape[0]
    merged = merged_ref[...]
    for x in range(nx):
        for tall in range(ny + 4):
            block = tall_delta(ny, delta_ref, up_ref, down_ref, x, tall)
            store_shifts(shifted, x, tall, block, merged, tall_spot(nx, ny, x, tall))
    one_edges = jnp.zeros((chan, LANES), F32)
    total = None
    for x in range(1, nx - 1):
        acts = jnp.concatenate(
            [tall_act(nx, ny, act_ref, up_ref, down_ref, x, tall) for tall in range(ny + 2)], 1
        )
        one, one_edges, term = back_plane(
            ny, lambda c, wide, at: shifted[c, wide - 2, :, at], x + 1, w_ref[...], acts, one_edges, True
        )
        one_ref[x - 1] = one
        total = add(total, term)
    one_edge_ref[...] = one_edges
    two_ref[...] = total
    edges = edge_ref[0:8].astype(F32)
    for x in range(nx):
        vol = vol_ref[x]
        shifts = [[], [], []]
        for y in range(ny):
            before, after = z_shifts(vol[y], edges, nx * ny + x * ny + y)
            shifts[0].append(before)
            shifts[1].append(vol[y])
            shifts[2].append(after)
        lhs = [jnp.concatenate(row, 1) for row in shifts] + [jnp.zeros((8, ny * LANES), F32)]
        vol_out_ref[x] = jnp.concatenate(lhs, 0).astype(BF16)


def outer_body(
    nx, ny, act_ref, up_ref, down_ref, left_ref, right_ref, w_ref,
    own_ref, inner_ref, inner_edge_ref, two_ref, vol_ref,
    sums_ref, one_ref, one_edge_ref, far, grad_two,
):
    chan = act_ref.shape[1]
    base = 2 * (ny + 4)
    for side, ref in ((0, left_ref), (1, right_ref)):
        edges = ref[base + ny + 2]
        for k in range(2):
            for tall in range(ny + 4):
                from_x = nx - 2 + k if side == 0 else k
                store_shifts(
                    far, 2 * side + k, tall, ref[k * (ny + 4) + tall], edges, tall_spot(nx, ny, from_x, tall)
                )

    def plane_at(c, wide, at):
        if wide < 2:
            return far[c, wide, :, at]
        if wide < nx + 2:
            return own_ref[c, wide - 2, :, at]
        return far[c, wide - nx, :, at]

    one_edges = inner_edge_ref[...]
    total_two = two_ref[...]
    for wide in (0, 1, nx, nx + 1):
        if wide == 0:
            blocks = [left_ref[base + tall] for tall in range(ny + 2)]
        elif wide == nx + 1:
            blocks = [right_ref[base + tall] for tall in range(ny + 2)]
        else:
            blocks = [
                tall_act(nx, ny, act_ref, up_ref, down_ref, wide - 1, tall) for tall in range(ny + 2)
            ]
        acts = jnp.concatenate(blocks, 1)
        one, one_edges, term = back_plane(
            ny, plane_at, wide, w_ref[...], acts, one_edges, 1 <= wide <= nx
        )
        one_ref[wide] = one
        if term is not None:
            total_two = total_two + term
    for x in range(1, nx - 1):
        one_ref[x + 1] = inner_ref[x - 1]
    one_edge_ref[...] = one_edges.astype(BF16).astype(F32)

    total_one = None
    for x in range(nx):
        rhs = jnp.concatenate(
            [
                one_ref[x + 2 - a, :, (2 - b) * LANES : (2 - b + ny) * LANES]
                for a in range(3)
                for b in range(3)
            ]
            + [own_ref[1, x, :, 2 * LANES : (ny + 2) * LANES]],
            0,
        )
        term = lax.dot_general(
            vol_ref[x], rhs, (((1,), (1,)), ((), ())), preferred_element_type=F32
        )
        total_one = add(total_one, term)

    grad_two[:, 0:chan] = total_two
    lane = lane_ids(8)
    slots = grad_two.shape[0] // 8
    per = LANES // chan
    for group in range(-(-slots // per)):
        packed = jnp.zeros((8, LANES), F32)
        for s in range(per):
            slot = group * per + s
            if slot < slots:
                moved = grad_two[slot * 8 : slot * 8 + 8, :]
                if s:
                    moved = pltpu.roll(moved, chan * s, 1)
                packed = jnp.where((lane >= chan * s) & (lane < chan * (s + 1)), moved, packed)
        sums_ref[group * 8 : group * 8 + 8, :] = packed
    start = -(-slots // per) * 8
    width = total_one.shape[1]
    tail = jnp.zeros((8, 2 * LANES - width), F32)
    tiles = [jnp.concatenate([total_one[8 * c : 8 * c + 8], tail], 1) for c in range(3)]
    head = lax.broadcasted_iota(jnp.int32, (8, 2 * LANES), 0) < 4
    first = jnp.where(head, tiles[0], pltpu.roll(tiles[1], 4, 0))
    second = jnp.where(head, tiles[2], tiles[1])
    for k in range(2):
        sums_ref[start + 16 * k : start + 16 * k + 8, :] = first[:, k * LANES : (k + 1) * LANES]
        sums_ref[start + 16 * k + 8 : start + 16 * k + 16, :] = second[:, k * LANES : (k + 1) * LANES]


def unpack_body(norm, sums_ref, one_ref, bias_one_ref, two_ref, bias_two_ref):
    chan = two_ref.shape[2]
    per = LANES // chan
    slots = 2 * two_ref.shape[0]
    for slot in range(slots):
        group, s = divmod(slot, per)
        block = sums_ref[group * 8 : group * 8 + 8, :] * norm
        if s:
            block = pltpu.roll(block, LANES - chan * s, 1)
        two_ref[slot // 2, (slot % 2) * 8 : (slot % 2) * 8 + 8, :] = block[:, :chan]
    base = -(-slots // per) * 8
    tiles = [sums_ref[base + 8 * k : base + 8 * k + 8, :] * norm for k in range(4)]

    def piece(k, index):
        block = tiles[2 * (index // per) + k]
        s = index % per
        return pltpu.roll(block, LANES - chan * s, 1) if s else block

    ins = one_ref.shape[1]
    for ab in range(9):
        first = piece(0, ab)
        second = piece(1, ab)
        one_ref[3 * ab] = first[0:ins, :chan]
        one_ref[3 * ab + 1] = first[4 : 4 + ins, :chan]
        one_ref[3 * ab + 2] = second[0:ins, :chan]
    bias_one_ref[...] = piece(1, 4)[4:5, :chan]
    bias_two_ref[...] = piece(1, 9)[4:5, :chan]


def volume_body(nx, ny, one_ref, edge_ref, w_ref, out_ref, shifted):
    edges = edge_ref[...].astype(BF16)
    for wide in range(nx + 2):
        for tall in range(ny + 2):
            at = slice(tall * LANES, (tall + 1) * LANES)
            block = one_ref[wide, :, at]
            before, after = z_shifts(block, edges, wide * (ny + 2) + tall)
            shifted[0, wide, :, at] = after
            shifted[1, wide, :, at] = before
    weights = w_ref[...]
    ins = out_ref.shape[0]
    for x in range(nx):
        rows = []
        for a in range(3):
            for b in range(3):
                at = slice((2 - b) * LANES, (2 - b + ny) * LANES)
                rows += [shifted[0, x + 2 - a, :, at], one_ref[x + 2 - a, :, at], shifted[1, x + 2 - a, :, at]]
        grad = jnp.dot(weights, jnp.concatenate(rows, 0), preferred_element_type=F32)
        stack = jnp.stack([grad[:8, y * LANES : (y + 1) * LANES] for y in range(ny)], 0)
        out_ref[:, x] = jnp.swapaxes(stack, 0, 1)[:ins]


def ring(axis, step):
    count = lax.axis_size(axis)
    return [(i, (i + step) % count) for i in range(count)]


def swap_edges(edges):
    if lax.axis_size("gz") == 2:
        return lax.ppermute(edges, "gz", ring("gz", 1))
    before = lax.ppermute(edges, "gz", ring("gz", 1))
    after = lax.ppermute(edges, "gz", ring("gz", -1))
    even = lax.broadcasted_iota(jnp.int32, edges.shape, 1) % 2 == 0
    return jnp.where(even, before, after)


def exchange(total, axis, step, cross):
    count = lax.axis_size(axis)
    if axis == "gx":
        return lax.ppermute(total, "gx", [(i, i ^ step ^ cross) for i in range(count)])
    pairs = [
        (i * count + k, (i ^ cross) * count + (k ^ step))
        for i in range(lax.axis_size("gx"))
        for k in range(count)
    ]
    return lax.ppermute(total, ("gx", axis), pairs)


def doublings(axis, first=1):
    step = first
    while step < lax.axis_size(axis):
        yield step
        step *= 2


def near(array):
    return pltpu.with_memory_space_constraint(array, pltpu.VMEM)


def call(body, out_shape, scratch, flops, *args):
    many = isinstance(out_shape, (tuple, list))
    spec = pl.BlockSpec(memory_space=pltpu.VMEM)
    return pl.pallas_call(
        body,
        out_shape=out_shape,
        in_specs=[spec] * len(args),
        out_specs=[spec] * len(out_shape) if many else spec,
        scratch_shapes=scratch,
        cost_estimate=pl.CostEstimate(flops=flops, bytes_accessed=1 << 18, transcendentals=0),
    )(*args)


def local(volume, act_one, act_two, weight_one, weight_two, cotangent):
    chan, nx, ny, nz = act_one.shape
    ins = volume.shape[0]
    cells = nx * ny * nz
    for axis in AXES:
        cells *= lax.axis_size(axis)
    norm = 1.0 / math.sqrt(cells)
    flat_two = jnp.transpose(weight_two, (1, 2, 3, 4, 0)).reshape(chan, 27 * chan)
    flat_one = jnp.transpose(weight_one, (1, 2, 3, 4, 0)).reshape(ins, 27 * chan)
    flat_one = jnp.pad(flat_one, ((0, chan - ins), (0, 0)))
    blocks = pltpu.VMEM((nx * ny, chan, LANES), BF16)
    edge = pltpu.VMEM((chan, LANES), BF16)
    flat_two = near(flat_two)
    flat_one = near(flat_one)

    delta, act, edges, vols = call(
        lambda *refs: prep_body(nx, ny, *refs),
        (blocks, blocks, edge, pltpu.VMEM((nx, ny, 8, LANES), F32)),
        [],
        1 << 20,
        cotangent, act_two, act_one, volume,
    )
    edges = near(swap_edges(edges))
    delta, act = near(delta), near(act)
    side = pltpu.VMEM((3 * nx + 1, chan, LANES), BF16)
    low, high = call(
        lambda *refs: pack_y_body(nx, ny, *refs), (side, side), [], 1 << 20, delta, act, edges
    )
    down = near(lax.ppermute(low, "gy", ring("gy", -1)))
    up = near(lax.ppermute(high, "gy", ring("gy", 1)))
    side = pltpu.VMEM((3 * (ny + 4) - 1, chan, LANES), BF16)
    low, high, merged = call(
        lambda *refs: pack_x_body(nx, ny, *refs), (side, side, edge), [], 1 << 20,
        delta, act, edges, up, down,
    )
    right = near(lax.ppermute(low, "gx", ring("gx", -1)))
    left = near(lax.ppermute(high, "gx", ring("gx", 1)))
    span = (ny + 2) * LANES
    own, inner, inner_edges, inner_two, vols = call(
        lambda *refs: inner_body(nx, ny, *refs),
        (
            pltpu.VMEM((3, nx, chan, (ny + 4) * LANES), BF16),
            pltpu.VMEM((nx - 2, chan, span), BF16),
            pltpu.VMEM((chan, LANES), F32),
            pltpu.VMEM((27 * chan, chan), F32),
            pltpu.VMEM((nx, 32, ny * LANES), BF16),
        ),
        [],
        1 << 27,
        delta, act, edges, near(merged), up, down, near(vols), flat_two,
    )
    slots = 27 * chan // 8
    rows = -(-slots // (LANES // chan)) * 8 + 32
    sums, one, one_edges = call(
        lambda *refs: outer_body(nx, ny, *refs),
        (
            pltpu.VMEM((rows, LANES), F32),
            pltpu.VMEM((nx + 2, chan, span), BF16),
            pltpu.VMEM((chan, LANES), F32),
        ),
        [
            pltpu.VMEM((3, 4, chan, (ny + 4) * LANES), BF16),
            pltpu.VMEM((27 * chan, LANES), F32),
        ],
        1 << 28,
        act, up, down, left, right, flat_two,
        near(own), near(inner), near(inner_edges), near(inner_two), near(vols),
    )
    sums = sums + exchange(sums, "gx", 1, 0)
    if lax.axis_size("gz") == 2:
        moved = exchange(jnp.concatenate([sums, one_edges], 0), "gz", 1, 0)
        sums = sums + moved[:rows]
        one_edges = moved[rows:]
    else:
        one_edges = swap_edges(one_edges)
        for step in doublings("gz"):
            sums = sums + exchange(sums, "gz", step, 1)
    for step in doublings("gx", 2):
        sums = sums + exchange(sums, "gx", step, 1)
    grad_volume = call(
        lambda *refs: volume_body(nx, ny, *refs),
        jax.ShapeDtypeStruct(volume.shape, F32),
        [pltpu.VMEM((2, nx + 2, chan, span), BF16)],
        1 << 27,
        near(one), near(one_edges), flat_one,
    )
    sums, grad_volume = lax.optimization_barrier((sums, grad_volume))
    for step in doublings("gy"):
        sums = sums + exchange(sums, "gy", step, 1)
    sums = near(sums)
    grad_one, bias_one, grad_two, bias_two = call(
        lambda *refs: unpack_body(norm, *refs),
        (
            jax.ShapeDtypeStruct((27, ins, chan), F32),
            jax.ShapeDtypeStruct((1, chan), F32),
            jax.ShapeDtypeStruct((27, chan, chan), F32),
            jax.ShapeDtypeStruct((1, chan), F32),
        ),
        [],
        1 << 20,
        sums,
    )
    grad_one = jnp.transpose(grad_one.reshape(3, 3, 3, ins, chan), (4, 3, 0, 1, 2))
    grad_two = jnp.transpose(grad_two.reshape(3, 3, 3, chan, chan), (3, 4, 0, 1, 2))
    return (grad_one, bias_one.reshape(chan), grad_two, bias_two.reshape(chan), grad_volume)


def solution(mesh):
    placed = P(None, *AXES)
    return jax.shard_map(
        local,
        mesh=mesh,
        in_specs=(placed, placed, placed, P(), P(), placed),
        out_specs=(P(), P(), P(), P(), placed),
        check_vma=False,
    )
```

```python
import math

import jax
import jax.numpy as jnp
from jax import lax
from jax.experimental import pallas as pl
from jax.experimental.pallas import tpu as pltpu
from jax.sharding import PartitionSpec as P

AXES = ("gx", "gy", "gz")
F32 = jnp.float32
BF16 = jnp.bfloat16
LANES = 128


def lane_ids(rows):
    return lax.broadcasted_iota(jnp.int32, (rows, LANES), 1)


def slope(saved):
    return jnp.where(saved > 0, 1.0, 0.3).astype(F32)


def put_edges(packed, block, spot):
    lane = lane_ids(block.shape[0])
    moved = pltpu.roll(block, (2 * spot + 1) % LANES, 1)
    return jnp.where((lane == 2 * spot) | (lane == 2 * spot + 1), moved, packed)


def z_shifts(block, edges, spot):
    lane = lane_ids(block.shape[0])
    near = pltpu.roll(edges, (LANES - 2 * spot - 1) % LANES, 1)
    after = pltpu.roll(jnp.where(lane == 0, near, block), LANES - 1, 1)
    before = pltpu.roll(jnp.where(lane == LANES - 1, near, block), 1, 1)
    return before, after


def prep_body(nx, ny, cot_ref, act_two_ref, vol_ref, delta_ref, edge_ref, rows_ref):
    chan = cot_ref.shape[0]
    edges = jnp.zeros((chan, LANES), F32)
    vol_edges = jnp.zeros((8, LANES), F32)
    for x in range(nx):
        delta = cot_ref[:, x].astype(F32) * slope(act_two_ref[:, x].astype(F32))
        delta = jnp.swapaxes(delta, 0, 1)
        for y in range(ny):
            spot = x * ny + y
            delta_ref[spot] = delta[y].astype(BF16)
            edges = put_edges(edges, delta[y], spot)
        vol = vol_rows(vol_ref, x)
        for y in range(ny):
            rows_ref[x, y] = vol[y]
            vol_edges = put_edges(vol_edges, vol[y], nx * ny + x * ny + y)
    vol_edges = jnp.concatenate([vol_edges] * (chan // 8), 0)
    half = lane_ids(chan) < 2 * nx * ny
    edge_ref[...] = jnp.where(half, edges, vol_edges).astype(BF16)


def act_body(nx, ny, act_one_ref, act_ref):
    for x in range(nx):
        act = jnp.swapaxes(act_one_ref[:, x].astype(F32), 0, 1)
        for y in range(ny):
            act_ref[x * ny + y] = act[y].astype(BF16)


def vol_rows(vol_ref, x):
    vol = vol_ref[:, x].astype(F32)
    rest = jnp.ones((8 - vol.shape[0],) + vol.shape[1:], F32)
    return jnp.swapaxes(jnp.concatenate([vol, rest], 0), 0, 1)


def pack_y_body(nx, ny, delta_ref, act_ref, edge_ref, low_ref, high_ref):
    for x in range(nx):
        for k in range(2):
            low_ref[2 * x + k] = delta_ref[x * ny + k]
            high_ref[2 * x + k] = delta_ref[x * ny + ny - 2 + k]
        low_ref[2 * nx + x] = act_ref[x * ny]
        high_ref[2 * nx + x] = act_ref[x * ny + ny - 1]
    low_ref[3 * nx] = edge_ref[...]
    high_ref[3 * nx] = edge_ref[...]


def tall_delta(ny, delta_ref, up_ref, down_ref, x, tall):
    if tall < 2:
        return up_ref[2 * x + tall]
    if tall < ny + 2:
        return delta_ref[x * ny + tall - 2]
    return down_ref[2 * x + tall - ny - 2]


def tall_act(nx, ny, act_ref, up_ref, down_ref, x, tall):
    if tall == 0:
        return up_ref[2 * nx + x]
    if tall == ny + 1:
        return down_ref[2 * nx + x]
    return act_ref[x * ny + tall - 1]


def tall_spot(nx, ny, x, tall):
    if tall < 2:
        return nx * ny + x * ny + ny - 2 + tall
    if tall < ny + 2:
        return x * ny + tall - 2
    return nx * ny + x * ny + tall - ny - 2


def pack_x_body(nx, ny, delta_ref, act_ref, edge_ref, up_ref, down_ref, low_ref, high_ref, merged_ref):
    lane = lane_ids(edge_ref.shape[0])
    half = 2 * nx * ny
    up = pltpu.roll(up_ref[3 * nx], half, 1)
    down = pltpu.roll(down_ref[3 * nx], half, 1)
    beyond = jnp.where(lax.rem(lane, 2 * ny) < ny, down, up)
    merged = jnp.where(lane < half, edge_ref[...], beyond)
    merged_ref[...] = merged
    for ref, planes, act_plane in ((low_ref, (0, 1), 0), (high_ref, (nx - 2, nx - 1), nx - 1)):
        for k in range(2):
            for tall in range(ny + 4):
                ref[k * (ny + 4) + tall] = tall_delta(ny, delta_ref, up_ref, down_ref, planes[k], tall)
        base = 2 * (ny + 4)
        for tall in range(ny + 2):
            ref[base + tall] = tall_act(nx, ny, act_ref, up_ref, down_ref, act_plane, tall)
        ref[base + ny + 2] = merged


def store_shifts(shifted, plane, tall, block, edges, spot):
    before, after = z_shifts(block, edges, spot)
    at = slice(tall * LANES, (tall + 1) * LANES)
    shifted[0, plane, :, at] = after
    shifted[1, plane, :, at] = block
    shifted[2, plane, :, at] = before


def tap_rows(ny, plane_at, wide, taps):
    span = (ny + 2) * LANES
    return jnp.concatenate(
        [
            plane_at(c, wide + 2 - a, slice((2 - b) * LANES, (2 - b) * LANES + span))
            for a in taps
            for b in range(3)
            for c in range(3)
        ],
        0,
    )


def tap_back(w_ref, rows, taps):
    per = w_ref.shape[1] // 3
    return jnp.dot(
        w_ref[:, per * taps[0] : per * (taps[-1] + 1)], rows, preferred_element_type=F32
    )


def add_two(ny, totals, rows, acts, taps):
    inner = slice(LANES, (ny + 1) * LANES)
    term = lax.dot_general(
        rows[:, inner], acts[:, inner], (((1,), (1,)), ((), ())), preferred_element_type=F32
    )
    per = rows.shape[0] // len(taps)
    for k, a in enumerate(taps):
        totals[a] = add(totals[a], term[k * per : (k + 1) * per])


def finish_plane(ny, back, acts, wide, one_edges):
    delta = back * slope(acts.astype(F32))
    for tall in range(ny + 2):
        one_edges = put_edges(
            one_edges, delta[:, tall * LANES : (tall + 1) * LANES], wide * (ny + 2) + tall
        )
    return delta.astype(BF16), one_edges


def own_taps(nx, wide):
    return [a for a in range(3) if 2 <= wide + 2 - a <= nx + 1]


def add(total, term):
    return term if total is None else total + term


def inner_body(
    nx, ny, delta_ref, act_ref, edge_ref, merged_ref, up_ref, down_ref, vol_ref, w_ref,
    shifted, one_ref, one_edge_ref, two_ref, vol_out_ref, part_ref,
):
    chan = edge_ref.shape[0]
    merged = merged_ref[...]
    for x in range(nx):
        for tall in range(ny + 4):
            block = tall_delta(ny, delta_ref, up_ref, down_ref, x, tall)
            store_shifts(shifted, x, tall, block, merged, tall_spot(nx, ny, x, tall))
    one_edges = jnp.zeros((chan, LANES), F32)
    totals = [None] * 3
    for wide in range(nx + 2):
        taps = own_taps(nx, wide)
        rows = tap_rows(ny, lambda c, plane, at: shifted[c, plane - 2, :, at], wide, taps)
        back = tap_back(w_ref, rows, taps)
        if 1 <= wide <= nx:
            acts = jnp.concatenate(
                [tall_act(nx, ny, act_ref, up_ref, down_ref, wide - 1, tall) for tall in range(ny + 2)], 1
            )
            add_two(ny, totals, rows, acts, taps)
        if 2 <= wide < nx:
            one_ref[wide - 2], one_edges = finish_plane(ny, back, acts, wide, one_edges)
        else:
            part_ref[wide if wide < 2 else wide - nx + 2] = back
    total = jnp.concatenate(totals, 0)
    one_edge_ref[...] = one_edges
    two_ref[...] = total
    edges = edge_ref[0:8].astype(F32)
    for x in range(nx):
        vol = vol_ref[x]
        shifts = [[], [], []]
        for y in range(ny):
            before, after = z_shifts(vol[y], edges, nx * ny + x * ny + y)
            shifts[0].append(before)
            shifts[1].append(vol[y])
            shifts[2].append(after)
        lhs = [jnp.concatenate(row, 1) for row in shifts] + [jnp.zeros((8, ny * LANES), F32)]
        vol_out_ref[x] = jnp.concatenate(lhs, 0).astype(BF16)


def outer_body(
    nx, ny, act_ref, up_ref, down_ref, left_ref, right_ref, w_ref,
    own_ref, inner_ref, inner_edge_ref, two_ref, vol_ref, part_ref,
    sums_ref, one_ref, one_edge_ref, far, grad_two,
):
    chan = act_ref.shape[1]
    base = 2 * (ny + 4)
    for side, ref in ((0, left_ref), (1, right_ref)):
        edges = ref[base + ny + 2]
        for k in range(2):
            for tall in range(ny + 4):
                from_x = nx - 2 + k if side == 0 else k
                store_shifts(
                    far, 2 * side + k, tall, ref[k * (ny + 4) + tall], edges, tall_spot(nx, ny, from_x, tall)
                )

    def plane_at(c, wide, at):
        if wide < 2:
            return far[c, wide, :, at]
        if wide < nx + 2:
            return own_ref[c, wide - 2, :, at]
        return far[c, wide - nx, :, at]

    one_edges = inner_edge_ref[...]
    totals = [None] * 3
    for wide in (0, 1, nx, nx + 1):
        if wide == 0:
            blocks = [left_ref[base + tall] for tall in range(ny + 2)]
        elif wide == nx + 1:
            blocks = [right_ref[base + tall] for tall in range(ny + 2)]
        else:
            blocks = [
                tall_act(nx, ny, act_ref, up_ref, down_ref, wide - 1, tall) for tall in range(ny + 2)
            ]
        acts = jnp.concatenate(blocks, 1)
        taps = [a for a in range(3) if a not in own_taps(nx, wide)]
        rows = tap_rows(ny, plane_at, wide, taps)
        back = part_ref[wide if wide < 2 else wide - nx + 2] + tap_back(w_ref, rows, taps)
        if 1 <= wide <= nx:
            add_two(ny, totals, rows, acts, taps)
        one_ref[wide], one_edges = finish_plane(ny, back, acts, wide, one_edges)
    third = 9 * chan
    for a in range(3):
        part = slice(third * a, third * (a + 1))
        grad_two[part, 0:chan] = two_ref[part, :] if totals[a] is None else two_ref[part, :] + totals[a]
    for x in range(1, nx - 1):
        one_ref[x + 1] = inner_ref[x - 1]
    one_edge_ref[...] = one_edges.astype(BF16).astype(F32)

    total_one = None
    for x in range(nx):
        rhs = jnp.concatenate(
            [
                one_ref[x + 2 - a, :, (2 - b) * LANES : (2 - b + ny) * LANES]
                for a in range(3)
                for b in range(3)
            ]
            + [own_ref[1, x, :, 2 * LANES : (ny + 2) * LANES]],
            0,
        )
        term = lax.dot_general(
            vol_ref[x], rhs, (((1,), (1,)), ((), ())), preferred_element_type=F32
        )
        total_one = add(total_one, term)

    lane = lane_ids(8)
    slots = grad_two.shape[0] // 8
    per = LANES // chan
    groups = -(-slots // per)
    tail = jnp.zeros((8, 2 * LANES - total_one.shape[1]), F32)
    tiles = [jnp.concatenate([total_one[8 * c : 8 * c + 8], tail], 1) for c in range(3)]
    head = lax.broadcasted_iota(jnp.int32, (8, 2 * LANES), 0) < 4
    first = jnp.where(head, tiles[0], pltpu.roll(tiles[1], 4, 0))
    second = jnp.where(head, tiles[2], tiles[1])
    sums_ref[groups * 8 : groups * 8 + 8, :] = first[:, :LANES]
    sums_ref[groups * 8 + 8 : groups * 8 + 16, :] = second[:, :LANES]
    rest = second[:, LANES:]
    rest = jnp.where(head[:, :LANES], rest, pltpu.roll(rest, LANES - chan, 1))
    spare = {slots: first[:, LANES:], slots + 1: rest}
    for group in range(groups):
        packed = jnp.zeros((8, LANES), F32)
        for s in range(per):
            slot = group * per + s
            if slot < slots:
                moved = grad_two[slot * 8 : slot * 8 + 8, :]
            else:
                moved = spare[slot]
            if s:
                moved = pltpu.roll(moved, chan * s, 1)
            packed = jnp.where((lane >= chan * s) & (lane < chan * (s + 1)), moved, packed)
        sums_ref[group * 8 : group * 8 + 8, :] = packed


def unpack_body(norm, sums_ref, one_ref, bias_one_ref, two_ref, bias_two_ref):
    chan = two_ref.shape[2]
    per = LANES // chan
    slots = 2 * two_ref.shape[0]
    for slot in range(slots):
        group, s = divmod(slot, per)
        block = sums_ref[group * 8 : group * 8 + 8, :] * norm
        if s:
            block = pltpu.roll(block, LANES - chan * s, 1)
        two_ref[slot // 2, (slot % 2) * 8 : (slot % 2) * 8 + 8, :] = block[:, :chan]
    base = slots // per * 8

    def piece(k, index):
        if index < per:
            block, s = sums_ref[base + 8 * (k + 1) : base + 8 * (k + 2), :], index
        else:
            block, s = sums_ref[base : base + 8, :], slots % per + k
        return (pltpu.roll(block, LANES - chan * s, 1) if s else block) * norm

    ins = one_ref.shape[1]
    for ab in range(9):
        first = piece(0, ab)
        second = piece(1, ab)
        one_ref[3 * ab] = first[0:ins, :chan]
        one_ref[3 * ab + 1] = first[4 : 4 + ins, :chan]
        one_ref[3 * ab + 2] = second[0:ins, :chan]
    bias_one_ref[...] = piece(1, 4)[4:5, :chan]
    bias_two_ref[...] = piece(1, 8)[4:5, :chan]


def volume_body(nx, ny, one_ref, edge_ref, w_ref, out_ref, shifted):
    edges = edge_ref[...].astype(BF16)
    for wide in range(nx + 2):
        for tall in range(ny + 2):
            at = slice(tall * LANES, (tall + 1) * LANES)
            block = one_ref[wide, :, at]
            before, after = z_shifts(block, edges, wide * (ny + 2) + tall)
            shifted[0, wide, :, at] = after
            shifted[1, wide, :, at] = before
    weights = w_ref[...]
    ins = out_ref.shape[0]
    for x in range(nx):
        rows = []
        for a in range(3):
            for b in range(3):
                at = slice((2 - b) * LANES, (2 - b + ny) * LANES)
                rows += [shifted[0, x + 2 - a, :, at], one_ref[x + 2 - a, :, at], shifted[1, x + 2 - a, :, at]]
        grad = jnp.dot(weights, jnp.concatenate(rows, 0), preferred_element_type=F32)
        stack = jnp.stack([grad[:8, y * LANES : (y + 1) * LANES] for y in range(ny)], 0)
        out_ref[:, x] = jnp.swapaxes(stack, 0, 1)[:ins]


def ring(axis, step):
    count = lax.axis_size(axis)
    return [(i, (i + step) % count) for i in range(count)]


def swap_edges(edges):
    if lax.axis_size("gz") == 2:
        return lax.ppermute(edges, "gz", ring("gz", 1))
    before = lax.ppermute(edges, "gz", ring("gz", 1))
    after = lax.ppermute(edges, "gz", ring("gz", -1))
    even = lax.broadcasted_iota(jnp.int32, edges.shape, 1) % 2 == 0
    return jnp.where(even, before, after)


def exchange(total, axis, step, cross):
    count = lax.axis_size(axis)
    if axis == "gx":
        return lax.ppermute(total, "gx", [(i, i ^ step ^ cross) for i in range(count)])
    pairs = [
        (i * count + k, (i ^ cross) * count + (k ^ step))
        for i in range(lax.axis_size("gx"))
        for k in range(count)
    ]
    return lax.ppermute(total, ("gx", axis), pairs)


def doublings(axis, first=1):
    step = first
    while step < lax.axis_size(axis):
        yield step
        step *= 2


def near(array):
    return pltpu.with_memory_space_constraint(array, pltpu.VMEM)


def call(body, out_shape, scratch, flops, *args):
    many = isinstance(out_shape, (tuple, list))
    spec = pl.BlockSpec(memory_space=pltpu.VMEM)
    return pl.pallas_call(
        body,
        out_shape=out_shape,
        in_specs=[spec] * len(args),
        out_specs=[spec] * len(out_shape) if many else spec,
        scratch_shapes=scratch,
        cost_estimate=pl.CostEstimate(flops=flops, bytes_accessed=1 << 18, transcendentals=0),
    )(*args)


def local(volume, act_one, act_two, weight_one, weight_two, cotangent):
    chan, nx, ny, nz = act_one.shape
    ins = volume.shape[0]
    cells = nx * ny * nz
    for axis in AXES:
        cells *= lax.axis_size(axis)
    norm = 1.0 / math.sqrt(cells)
    flat_two = jnp.transpose(weight_two, (1, 2, 3, 4, 0)).reshape(chan, 27 * chan)
    flat_one = jnp.transpose(weight_one, (1, 2, 3, 4, 0)).reshape(ins, 27 * chan)
    flat_one = jnp.pad(flat_one, ((0, chan - ins), (0, 0)))
    blocks = pltpu.VMEM((nx * ny, chan, LANES), BF16)
    edge = pltpu.VMEM((chan, LANES), BF16)
    flat_two = near(flat_two)
    flat_one = near(flat_one)

    delta, edges, vols = call(
        lambda *refs: prep_body(nx, ny, *refs),
        (blocks, edge, pltpu.VMEM((nx, ny, 8, LANES), F32)),
        [],
        1 << 20,
        cotangent, act_two, volume,
    )
    edges, act_one = lax.optimization_barrier((edges, act_one))
    act = call(lambda *refs: act_body(nx, ny, *refs), blocks, [], 1 << 24, act_one)
    edges = near(swap_edges(edges))
    delta, act = near(delta), near(act)
    side = pltpu.VMEM((3 * nx + 1, chan, LANES), BF16)
    low, high = call(
        lambda *refs: pack_y_body(nx, ny, *refs), (side, side), [], 1 << 20, delta, act, edges
    )
    down = near(lax.ppermute(low, "gy", ring("gy", -1)))
    up = near(lax.ppermute(high, "gy", ring("gy", 1)))
    side = pltpu.VMEM((3 * (ny + 4) - 1, chan, LANES), BF16)
    low, high, merged = call(
        lambda *refs: pack_x_body(nx, ny, *refs), (side, side, edge), [], 1 << 20,
        delta, act, edges, up, down,
    )
    right = near(lax.ppermute(low, "gx", ring("gx", -1)))
    left = near(lax.ppermute(high, "gx", ring("gx", 1)))
    span = (ny + 2) * LANES
    own, inner, inner_edges, inner_two, vols, part = call(
        lambda *refs: inner_body(nx, ny, *refs),
        (
            pltpu.VMEM((3, nx, chan, (ny + 4) * LANES), BF16),
            pltpu.VMEM((nx - 2, chan, span), BF16),
            pltpu.VMEM((chan, LANES), F32),
            pltpu.VMEM((27 * chan, chan), F32),
            pltpu.VMEM((nx, 32, ny * LANES), BF16),
            pltpu.VMEM((4, chan, span), F32),
        ),
        [],
        1 << 27,
        delta, act, edges, near(merged), up, down, near(vols), flat_two,
    )
    slots = 27 * chan // 8
    rows = -(-slots // (LANES // chan)) * 8 + 16
    sums, one, one_edges = call(
        lambda *refs: outer_body(nx, ny, *refs),
        (
            pltpu.VMEM((rows, LANES), F32),
            pltpu.VMEM((nx + 2, chan, span), BF16),
            pltpu.VMEM((chan, LANES), F32),
        ),
        [
            pltpu.VMEM((3, 4, chan, (ny + 4) * LANES), BF16),
            pltpu.VMEM((27 * chan, LANES), F32),
        ],
        1 << 28,
        act, up, down, left, right, flat_two,
        near(own), near(inner), near(inner_edges), near(inner_two), near(vols), near(part),
    )
    sums = sums + exchange(sums, "gx", 1, 0)
    if lax.axis_size("gz") == 2:
        moved = exchange(jnp.concatenate([sums, one_edges], 0), "gz", 1, 0)
        sums = sums + moved[:rows]
        one_edges = moved[rows:]
    else:
        one_edges = swap_edges(one_edges)
        for step in doublings("gz"):
            sums = sums + exchange(sums, "gz", step, 1)
    for step in doublings("gx", 2):
        sums = sums + exchange(sums, "gx", step, 1)
    grad_volume = call(
        lambda *refs: volume_body(nx, ny, *refs),
        jax.ShapeDtypeStruct(volume.shape, F32),
        [pltpu.VMEM((2, nx + 2, chan, span), BF16)],
        1 << 27,
        near(one), near(one_edges), flat_one,
    )
    sums, grad_volume = lax.optimization_barrier((sums, grad_volume))
    for step in doublings("gy"):
        sums = sums + exchange(sums, "gy", step, 1)
    sums = near(sums)
    grad_one, bias_one, grad_two, bias_two = call(
        lambda *refs: unpack_body(norm, *refs),
        (
            jax.ShapeDtypeStruct((27, ins, chan), F32),
            jax.ShapeDtypeStruct((1, chan), F32),
            jax.ShapeDtypeStruct((27, chan, chan), F32),
            jax.ShapeDtypeStruct((1, chan), F32),
        ),
        [],
        1 << 20,
        sums,
    )
    grad_one = jnp.transpose(grad_one.reshape(3, 3, 3, ins, chan), (4, 3, 0, 1, 2))
    grad_two = jnp.transpose(grad_two.reshape(3, 3, 3, chan, chan), (3, 4, 0, 1, 2))
    return (grad_one, bias_one.reshape(chan), grad_two, bias_two.reshape(chan), grad_volume)


def solution(mesh):
    placed = P(None, *AXES)
    return jax.shard_map(
        local,
        mesh=mesh,
        in_specs=(placed, placed, placed, P(), P(), placed),
        out_specs=(P(), P(), P(), P(), placed),
        check_vma=False,
    )
```

```python
import math

import jax
import jax.numpy as jnp
from jax import lax
from jax.experimental import pallas as pl
from jax.experimental.pallas import tpu as pltpu
from jax.sharding import PartitionSpec as P

AXES = ("gx", "gy", "gz")
F32 = jnp.float32
BF16 = jnp.bfloat16
LANES = 128


def lane_ids(rows):
    return lax.broadcasted_iota(jnp.int32, (rows, LANES), 1)


def slope(saved):
    return jnp.where(saved > 0, 1.0, 0.3).astype(F32)


def put_edges(packed, block, spot):
    lane = lane_ids(block.shape[0])
    moved = pltpu.roll(block, (2 * spot + 1) % LANES, 1)
    return jnp.where((lane == 2 * spot) | (lane == 2 * spot + 1), moved, packed)


def z_shifts(block, edges, spot):
    lane = lane_ids(block.shape[0])
    near = pltpu.roll(edges, (LANES - 2 * spot - 1) % LANES, 1)
    after = pltpu.roll(jnp.where(lane == 0, near, block), LANES - 1, 1)
    before = pltpu.roll(jnp.where(lane == LANES - 1, near, block), 1, 1)
    return before, after


def prep_body(nx, ny, cot_ref, act_two_ref, vol_ref, delta_ref, edge_ref, rows_ref):
    chan = cot_ref.shape[0]
    edges = jnp.zeros((chan, LANES), F32)
    vol_edges = jnp.zeros((8, LANES), F32)
    for x in range(nx):
        delta = cot_ref[:, x].astype(F32) * slope(act_two_ref[:, x].astype(F32))
        delta = jnp.swapaxes(delta, 0, 1)
        for y in range(ny):
            spot = x * ny + y
            delta_ref[spot] = delta[y].astype(BF16)
            edges = put_edges(edges, delta[y], spot)
        vol = vol_rows(vol_ref, x)
        for y in range(ny):
            rows_ref[x, y] = vol[y]
            vol_edges = put_edges(vol_edges, vol[y], nx * ny + x * ny + y)
    vol_edges = jnp.concatenate([vol_edges] * (chan // 8), 0)
    half = lane_ids(chan) < 2 * nx * ny
    edge_ref[...] = jnp.where(half, edges, vol_edges).astype(BF16)


def act_body(nx, ny, act_one_ref, act_ref):
    for x in range(nx):
        act = jnp.swapaxes(act_one_ref[:, x].astype(F32), 0, 1)
        for y in range(ny):
            act_ref[x * ny + y] = act[y].astype(BF16)


def vol_rows(vol_ref, x):
    vol = vol_ref[:, x].astype(F32)
    rest = jnp.ones((8 - vol.shape[0],) + vol.shape[1:], F32)
    return jnp.swapaxes(jnp.concatenate([vol, rest], 0), 0, 1)


def pack_y_body(nx, ny, delta_ref, act_ref, edge_ref, low_ref, high_ref):
    for x in range(nx):
        for k in range(2):
            low_ref[2 * x + k] = delta_ref[x * ny + k]
            high_ref[2 * x + k] = delta_ref[x * ny + ny - 2 + k]
        low_ref[2 * nx + x] = act_ref[x * ny]
        high_ref[2 * nx + x] = act_ref[x * ny + ny - 1]
    low_ref[3 * nx] = edge_ref[...]
    high_ref[3 * nx] = edge_ref[...]


def tall_delta(ny, delta_ref, up_ref, down_ref, x, tall):
    if tall < 2:
        return up_ref[2 * x + tall]
    if tall < ny + 2:
        return delta_ref[x * ny + tall - 2]
    return down_ref[2 * x + tall - ny - 2]


def tall_act(nx, ny, act_ref, up_ref, down_ref, x, tall):
    if tall == 0:
        return up_ref[2 * nx + x]
    if tall == ny + 1:
        return down_ref[2 * nx + x]
    return act_ref[x * ny + tall - 1]


def tall_spot(nx, ny, x, tall):
    if tall < 2:
        return nx * ny + x * ny + ny - 2 + tall
    if tall < ny + 2:
        return x * ny + tall - 2
    return nx * ny + x * ny + tall - ny - 2


def pack_x_body(nx, ny, delta_ref, act_ref, edge_ref, up_ref, down_ref, low_ref, high_ref, merged_ref):
    lane = lane_ids(edge_ref.shape[0])
    half = 2 * nx * ny
    up = pltpu.roll(up_ref[3 * nx], half, 1)
    down = pltpu.roll(down_ref[3 * nx], half, 1)
    beyond = jnp.where(lax.rem(lane, 2 * ny) < ny, down, up)
    merged = jnp.where(lane < half, edge_ref[...], beyond)
    merged_ref[...] = merged
    for ref, planes, act_plane in ((low_ref, (0, 1), 0), (high_ref, (nx - 2, nx - 1), nx - 1)):
        for k in range(2):
            for tall in range(ny + 4):
                ref[k * (ny + 4) + tall] = tall_delta(ny, delta_ref, up_ref, down_ref, planes[k], tall)
        base = 2 * (ny + 4)
        for tall in range(ny + 2):
            ref[base + tall] = tall_act(nx, ny, act_ref, up_ref, down_ref, act_plane, tall)
        ref[base + ny + 2] = merged


def store_shifts(shifted, plane, tall, block, edges, spot):
    before, after = z_shifts(block, edges, spot)
    at = slice(tall * LANES, (tall + 1) * LANES)
    shifted[0, plane, :, at] = after
    shifted[1, plane, :, at] = block
    shifted[2, plane, :, at] = before


def tap_rows(ny, plane_at, wide, taps):
    span = (ny + 2) * LANES
    return jnp.concatenate(
        [
            plane_at(c, wide + 2 - a, slice((2 - b) * LANES, (2 - b) * LANES + span))
            for a in taps
            for b in range(3)
            for c in range(3)
        ],
        0,
    )


def tap_back(w_ref, rows, taps):
    per = w_ref.shape[1] // 3
    return jnp.dot(
        w_ref[:, per * taps[0] : per * (taps[-1] + 1)], rows, preferred_element_type=F32
    )


def add_two(ny, totals, rows, acts, taps):
    inner = slice(LANES, (ny + 1) * LANES)
    term = lax.dot_general(
        rows[:, inner], acts[:, inner], (((1,), (1,)), ((), ())), preferred_element_type=F32
    )
    per = rows.shape[0] // len(taps)
    for k, a in enumerate(taps):
        totals[a] = add(totals[a], term[k * per : (k + 1) * per])


def finish_plane(ny, back, acts, wide, one_edges):
    delta = back * slope(acts.astype(F32))
    for tall in range(ny + 2):
        one_edges = put_edges(
            one_edges, delta[:, tall * LANES : (tall + 1) * LANES], wide * (ny + 2) + tall
        )
    return delta.astype(BF16), one_edges


def own_taps(nx, wide):
    return [a for a in range(3) if 2 <= wide + 2 - a <= nx + 1]


def add(total, term):
    return term if total is None else total + term


def inner_body(
    nx, ny, delta_ref, act_ref, edge_ref, merged_ref, up_ref, down_ref, vol_ref, w_ref,
    shifted, one_ref, one_edge_ref, two_ref, vol_out_ref, part_ref,
):
    chan = edge_ref.shape[0]
    merged = merged_ref[...]
    for x in range(nx):
        for tall in range(ny + 4):
            block = tall_delta(ny, delta_ref, up_ref, down_ref, x, tall)
            store_shifts(shifted, x, tall, block, merged, tall_spot(nx, ny, x, tall))
    one_edges = jnp.zeros((chan, LANES), F32)
    totals = [None] * 3
    for wide in range(nx + 2):
        taps = own_taps(nx, wide)
        rows = tap_rows(ny, lambda c, plane, at: shifted[c, plane - 2, :, at], wide, taps)
        back = tap_back(w_ref, rows, taps)
        if 1 <= wide <= nx:
            acts = jnp.concatenate(
                [tall_act(nx, ny, act_ref, up_ref, down_ref, wide - 1, tall) for tall in range(ny + 2)], 1
            )
            add_two(ny, totals, rows, acts, taps)
        if 2 <= wide < nx:
            one_ref[wide - 2], one_edges = finish_plane(ny, back, acts, wide, one_edges)
        else:
            part_ref[wide if wide < 2 else wide - nx + 2] = back
    total = jnp.concatenate(totals, 0)
    one_edge_ref[...] = one_edges
    two_ref[...] = total
    edges = edge_ref[0:8].astype(F32)
    for x in range(nx):
        vol = vol_ref[x]
        shifts = [[], [], []]
        for y in range(ny):
            before, after = z_shifts(vol[y], edges, nx * ny + x * ny + y)
            shifts[0].append(before)
            shifts[1].append(vol[y])
            shifts[2].append(after)
        lhs = [jnp.concatenate(row, 1) for row in shifts] + [jnp.zeros((8, ny * LANES), F32)]
        vol_out_ref[x] = jnp.concatenate(lhs, 0).astype(BF16)


def outer_body(
    nx, ny, act_ref, up_ref, down_ref, left_ref, right_ref, w_ref,
    own_ref, inner_ref, inner_edge_ref, two_ref, vol_ref, part_ref,
    sums_ref, one_ref, one_edge_ref, far, grad_two,
):
    chan = act_ref.shape[1]
    base = 2 * (ny + 4)
    for side, ref in ((0, left_ref), (1, right_ref)):
        edges = ref[base + ny + 2]
        for k in range(2):
            for tall in range(ny + 4):
                from_x = nx - 2 + k if side == 0 else k
                store_shifts(
                    far, 2 * side + k, tall, ref[k * (ny + 4) + tall], edges, tall_spot(nx, ny, from_x, tall)
                )

    def plane_at(c, wide, at):
        if wide < 2:
            return far[c, wide, :, at]
        if wide < nx + 2:
            return own_ref[c, wide - 2, :, at]
        return far[c, wide - nx, :, at]

    one_edges = inner_edge_ref[...]
    totals = [None] * 3
    for wide in (0, 1, nx, nx + 1):
        if wide == 0:
            blocks = [left_ref[base + tall] for tall in range(ny + 2)]
        elif wide == nx + 1:
            blocks = [right_ref[base + tall] for tall in range(ny + 2)]
        else:
            blocks = [
                tall_act(nx, ny, act_ref, up_ref, down_ref, wide - 1, tall) for tall in range(ny + 2)
            ]
        acts = jnp.concatenate(blocks, 1)
        taps = [a for a in range(3) if a not in own_taps(nx, wide)]
        rows = tap_rows(ny, plane_at, wide, taps)
        back = part_ref[wide if wide < 2 else wide - nx + 2] + tap_back(w_ref, rows, taps)
        if 1 <= wide <= nx:
            add_two(ny, totals, rows, acts, taps)
        one_ref[wide], one_edges = finish_plane(ny, back, acts, wide, one_edges)
    third = 9 * chan
    for a in range(3):
        part = slice(third * a, third * (a + 1))
        grad_two[part, 0:chan] = two_ref[part, :] if totals[a] is None else two_ref[part, :] + totals[a]
    for x in range(1, nx - 1):
        one_ref[x + 1] = inner_ref[x - 1]
    one_edge_ref[...] = one_edges.astype(BF16).astype(F32)

    total_one = None
    for x in range(nx):
        rhs = jnp.concatenate(
            [
                one_ref[x + 2 - a, :, (2 - b) * LANES : (2 - b + ny) * LANES]
                for a in range(3)
                for b in range(3)
            ]
            + [own_ref[1, x, :, 2 * LANES : (ny + 2) * LANES]],
            0,
        )
        term = lax.dot_general(
            vol_ref[x], rhs, (((1,), (1,)), ((), ())), preferred_element_type=F32
        )
        total_one = add(total_one, term)

    lane = lane_ids(8)
    slots = grad_two.shape[0] // 8
    per = LANES // chan
    groups = -(-slots // per)
    tail = jnp.zeros((8, 2 * LANES - total_one.shape[1]), F32)
    tiles = [jnp.concatenate([total_one[8 * c : 8 * c + 8], tail], 1) for c in range(3)]
    head = lax.broadcasted_iota(jnp.int32, (8, 2 * LANES), 0) < 4
    first = jnp.where(head, tiles[0], pltpu.roll(tiles[1], 4, 0))
    second = jnp.where(head, tiles[2], tiles[1])
    sums_ref[groups * 8 : groups * 8 + 8, :] = first[:, :LANES]
    sums_ref[groups * 8 + 8 : groups * 8 + 16, :] = second[:, :LANES]
    rest = second[:, LANES:]
    rest = jnp.where(head[:, :LANES], rest, pltpu.roll(rest, LANES - chan, 1))
    spare = {slots: first[:, LANES:], slots + 1: rest}
    for group in range(groups):
        packed = jnp.zeros((8, LANES), F32)
        for s in range(per):
            slot = group * per + s
            if slot < slots:
                moved = grad_two[slot * 8 : slot * 8 + 8, :]
            else:
                moved = spare[slot]
            if s:
                moved = pltpu.roll(moved, chan * s, 1)
            packed = jnp.where((lane >= chan * s) & (lane < chan * (s + 1)), moved, packed)
        sums_ref[group * 8 : group * 8 + 8, :] = packed


def unpack_body(norm, sums_ref, one_ref, bias_one_ref, two_ref, bias_two_ref):
    chan = two_ref.shape[2]
    per = LANES // chan
    slots = 2 * two_ref.shape[0]
    for slot in range(slots):
        group, s = divmod(slot, per)
        block = sums_ref[group * 8 : group * 8 + 8, :] * norm
        if s:
            block = pltpu.roll(block, LANES - chan * s, 1)
        two_ref[slot // 2, (slot % 2) * 8 : (slot % 2) * 8 + 8, :] = block[:, :chan]
    base = slots // per * 8

    def piece(k, index):
        if index < per:
            block, s = sums_ref[base + 8 * (k + 1) : base + 8 * (k + 2), :], index
        else:
            block, s = sums_ref[base : base + 8, :], slots % per + k
        return (pltpu.roll(block, LANES - chan * s, 1) if s else block) * norm

    ins = one_ref.shape[1]
    for ab in range(9):
        first = piece(0, ab)
        second = piece(1, ab)
        one_ref[3 * ab] = first[0:ins, :chan]
        one_ref[3 * ab + 1] = first[4 : 4 + ins, :chan]
        one_ref[3 * ab + 2] = second[0:ins, :chan]
    bias_one_ref[...] = piece(1, 4)[4:5, :chan]
    bias_two_ref[...] = piece(1, 8)[4:5, :chan]


def volume_body(nx, ny, one_ref, edge_ref, w_ref, out_ref, shifted):
    edges = edge_ref[...].astype(BF16)
    for wide in range(nx + 2):
        for tall in range(ny + 2):
            at = slice(tall * LANES, (tall + 1) * LANES)
            block = one_ref[wide, :, at]
            before, after = z_shifts(block, edges, wide * (ny + 2) + tall)
            shifted[0, wide, :, at] = after
            shifted[1, wide, :, at] = before
    weights = w_ref[...]
    ins = out_ref.shape[0]
    for x in range(nx):
        rows = []
        for a in range(3):
            for b in range(3):
                at = slice((2 - b) * LANES, (2 - b + ny) * LANES)
                rows += [shifted[0, x + 2 - a, :, at], one_ref[x + 2 - a, :, at], shifted[1, x + 2 - a, :, at]]
        grad = jnp.dot(weights, jnp.concatenate(rows, 0), preferred_element_type=F32)
        stack = jnp.stack([grad[:8, y * LANES : (y + 1) * LANES] for y in range(ny)], 0)
        out_ref[:, x] = jnp.swapaxes(stack, 0, 1)[:ins]


def ring(axis, step):
    count = lax.axis_size(axis)
    return [(i, (i + step) % count) for i in range(count)]


def swap_edges(edges):
    if lax.axis_size("gz") == 2:
        return lax.ppermute(edges, "gz", ring("gz", 1))
    before = lax.ppermute(edges, "gz", ring("gz", 1))
    after = lax.ppermute(edges, "gz", ring("gz", -1))
    even = lax.broadcasted_iota(jnp.int32, edges.shape, 1) % 2 == 0
    return jnp.where(even, before, after)


def exchange(total, axis, step, cross):
    count = lax.axis_size(axis)
    if axis == "gx":
        return lax.ppermute(total, "gx", [(i, i ^ step ^ cross) for i in range(count)])
    pairs = [
        (i * count + k, (i ^ cross) * count + (k ^ step))
        for i in range(lax.axis_size("gx"))
        for k in range(count)
    ]
    return lax.ppermute(total, ("gx", axis), pairs)


def doublings(axis, first=1):
    step = first
    while step < lax.axis_size(axis):
        yield step
        step *= 2


def near(array):
    return pltpu.with_memory_space_constraint(array, pltpu.VMEM)


def call(body, out_shape, scratch, flops, *args):
    many = isinstance(out_shape, (tuple, list))
    spec = pl.BlockSpec(memory_space=pltpu.VMEM)
    return pl.pallas_call(
        body,
        out_shape=out_shape,
        in_specs=[spec] * len(args),
        out_specs=[spec] * len(out_shape) if many else spec,
        scratch_shapes=scratch,
        cost_estimate=pl.CostEstimate(flops=flops, bytes_accessed=1 << 18, transcendentals=0),
    )(*args)


def local(volume, act_one, act_two, weight_one, weight_two, cotangent):
    chan, nx, ny, nz = act_one.shape
    ins = volume.shape[0]
    cells = nx * ny * nz
    for axis in AXES:
        cells *= lax.axis_size(axis)
    norm = 1.0 / math.sqrt(cells)
    flat_two = jnp.transpose(weight_two, (1, 2, 3, 4, 0)).reshape(chan, 27 * chan)
    flat_one = jnp.transpose(weight_one, (1, 2, 3, 4, 0)).reshape(ins, 27 * chan)
    flat_one = jnp.pad(flat_one, ((0, chan - ins), (0, 0)))
    blocks = pltpu.VMEM((nx * ny, chan, LANES), BF16)
    edge = pltpu.VMEM((chan, LANES), BF16)
    flat_two = near(flat_two)
    flat_one = near(flat_one)

    delta, edges, vols = call(
        lambda *refs: prep_body(nx, ny, *refs),
        (blocks, edge, pltpu.VMEM((nx, ny, 8, LANES), F32)),
        [],
        1 << 20,
        cotangent, act_two, volume,
    )
    edges, act_one = lax.optimization_barrier((edges, act_one))
    act = call(lambda *refs: act_body(nx, ny, *refs), blocks, [], 1 << 24, act_one)
    edges = near(swap_edges(edges))
    delta, act = near(delta), near(act)
    side = pltpu.VMEM((3 * nx + 1, chan, LANES), BF16)
    low, high = call(
        lambda *refs: pack_y_body(nx, ny, *refs), (side, side), [], 1 << 20, delta, act, edges
    )
    down = near(lax.ppermute(low, "gy", ring("gy", -1)))
    up = near(lax.ppermute(high, "gy", ring("gy", 1)))
    side = pltpu.VMEM((3 * (ny + 4) - 1, chan, LANES), BF16)
    low, high, merged = call(
        lambda *refs: pack_x_body(nx, ny, *refs), (side, side, edge), [], 1 << 20,
        delta, act, edges, up, down,
    )
    right = near(lax.ppermute(low, "gx", ring("gx", -1)))
    left = near(lax.ppermute(high, "gx", ring("gx", 1)))
    span = (ny + 2) * LANES
    own, inner, inner_edges, inner_two, vols, part = call(
        lambda *refs: inner_body(nx, ny, *refs),
        (
            pltpu.VMEM((3, nx, chan, (ny + 4) * LANES), BF16),
            pltpu.VMEM((nx - 2, chan, span), BF16),
            pltpu.VMEM((chan, LANES), F32),
            pltpu.VMEM((27 * chan, chan), F32),
            pltpu.VMEM((nx, 32, ny * LANES), BF16),
            pltpu.VMEM((4, chan, span), F32),
        ),
        [],
        1 << 27,
        delta, act, edges, near(merged), up, down, near(vols), flat_two,
    )
    slots = 27 * chan // 8
    rows = -(-slots // (LANES // chan)) * 8 + 16
    sums, one, one_edges = call(
        lambda *refs: outer_body(nx, ny, *refs),
        (
            pltpu.VMEM((rows, LANES), F32),
            pltpu.VMEM((nx + 2, chan, span), BF16),
            pltpu.VMEM((chan, LANES), F32),
        ),
        [
            pltpu.VMEM((3, 4, chan, (ny + 4) * LANES), BF16),
            pltpu.VMEM((27 * chan, LANES), F32),
        ],
        1 << 28,
        act, up, down, left, right, flat_two,
        near(own), near(inner), near(inner_edges), near(inner_two), near(vols), near(part),
    )
    if lax.axis_size("gz") == 2:
        moved = exchange(jnp.concatenate([sums, one_edges], 0), "gx", 1, 0)
        sums = sums + moved[:rows]
        moved = exchange(jnp.concatenate([sums, moved[rows:]], 0), "gz", 1, 1)
        sums = sums + moved[:rows]
        one_edges = moved[rows:]
    else:
        one_edges = swap_edges(one_edges)
        sums = sums + exchange(sums, "gx", 1, 0)
        for step in doublings("gz"):
            sums = sums + exchange(sums, "gz", step, 1)
    for step in doublings("gx", 2):
        sums = sums + exchange(sums, "gx", step, 1)
    grad_volume = call(
        lambda *refs: volume_body(nx, ny, *refs),
        jax.ShapeDtypeStruct(volume.shape, F32),
        [pltpu.VMEM((2, nx + 2, chan, span), BF16)],
        1 << 27,
        near(one), near(one_edges), flat_one,
    )
    sums, grad_volume = lax.optimization_barrier((sums, grad_volume))
    for step in doublings("gy"):
        sums = sums + exchange(sums, "gy", step, 1)
    sums = near(sums)
    grad_one, bias_one, grad_two, bias_two = call(
        lambda *refs: unpack_body(norm, *refs),
        (
            jax.ShapeDtypeStruct((27, ins, chan), F32),
            jax.ShapeDtypeStruct((1, chan), F32),
            jax.ShapeDtypeStruct((27, chan, chan), F32),
            jax.ShapeDtypeStruct((1, chan), F32),
        ),
        [],
        1 << 20,
        sums,
    )
    grad_one = jnp.transpose(grad_one.reshape(3, 3, 3, ins, chan), (4, 3, 0, 1, 2))
    grad_two = jnp.transpose(grad_two.reshape(3, 3, 3, chan, chan), (3, 4, 0, 1, 2))
    return (grad_one, bias_one.reshape(chan), grad_two, bias_two.reshape(chan), grad_volume)


def solution(mesh):
    placed = P(None, *AXES)
    return jax.shard_map(
        local,
        mesh=mesh,
        in_specs=(placed, placed, placed, P(), P(), placed),
        out_specs=(P(), P(), P(), P(), placed),
        check_vma=False,
    )
```

```python
import math

import jax
import jax.numpy as jnp
from jax import lax
from jax.experimental import pallas as pl
from jax.experimental.pallas import tpu as pltpu
from jax.sharding import PartitionSpec as P

AXES = ("gx", "gy", "gz")
F32 = jnp.float32
BF16 = jnp.bfloat16
LANES = 128


def lane_ids(rows):
    return lax.broadcasted_iota(jnp.int32, (rows, LANES), 1)


def slope(saved):
    return jnp.where(saved > 0, 1.0, 0.3).astype(F32)


def put_edges(packed, block, spot):
    lane = lane_ids(block.shape[0])
    moved = pltpu.roll(block, (2 * spot + 1) % LANES, 1)
    return jnp.where((lane == 2 * spot) | (lane == 2 * spot + 1), moved, packed)


def z_shifts(block, edges, spot):
    lane = lane_ids(block.shape[0])
    near = pltpu.roll(edges, (LANES - 2 * spot - 1) % LANES, 1)
    after = pltpu.roll(jnp.where(lane == 0, near, block), LANES - 1, 1)
    before = pltpu.roll(jnp.where(lane == LANES - 1, near, block), 1, 1)
    return before, after


def prep_body(nx, ny, cot_ref, act_two_ref, vol_ref, delta_ref, edge_ref, rows_ref):
    chan = cot_ref.shape[0]
    edges = jnp.zeros((chan, LANES), F32)
    vol_edges = jnp.zeros((8, LANES), F32)
    for x in range(nx):
        delta = cot_ref[:, x].astype(F32) * slope(act_two_ref[:, x].astype(F32))
        delta = jnp.swapaxes(delta, 0, 1)
        for y in range(ny):
            spot = x * ny + y
            delta_ref[spot] = delta[y].astype(BF16)
            edges = put_edges(edges, delta[y], spot)
        vol = vol_rows(vol_ref, x)
        for y in range(ny):
            rows_ref[x, y] = vol[y]
            vol_edges = put_edges(vol_edges, vol[y], nx * ny + x * ny + y)
    vol_edges = jnp.concatenate([vol_edges] * (chan // 8), 0)
    half = lane_ids(chan) < 2 * nx * ny
    edge_ref[...] = jnp.where(half, edges, vol_edges).astype(BF16)


def act_body(nx, ny, act_one_ref, act_ref):
    for x in range(nx):
        act = jnp.swapaxes(act_one_ref[:, x].astype(F32), 0, 1)
        for y in range(ny):
            act_ref[x * ny + y] = act[y].astype(BF16)


def vol_rows(vol_ref, x):
    vol = vol_ref[:, x].astype(F32)
    rest = jnp.ones((8 - vol.shape[0],) + vol.shape[1:], F32)
    return jnp.swapaxes(jnp.concatenate([vol, rest], 0), 0, 1)


def pack_y_body(nx, ny, delta_ref, act_ref, edge_ref, low_ref, high_ref):
    for x in range(nx):
        for k in range(2):
            low_ref[2 * x + k] = delta_ref[x * ny + k]
            high_ref[2 * x + k] = delta_ref[x * ny + ny - 2 + k]
        low_ref[2 * nx + x] = act_ref[x * ny]
        high_ref[2 * nx + x] = act_ref[x * ny + ny - 1]
    low_ref[3 * nx] = edge_ref[...]
    high_ref[3 * nx] = edge_ref[...]


def tall_delta(ny, delta_ref, up_ref, down_ref, x, tall):
    if tall < 2:
        return up_ref[2 * x + tall]
    if tall < ny + 2:
        return delta_ref[x * ny + tall - 2]
    return down_ref[2 * x + tall - ny - 2]


def tall_act(nx, ny, act_ref, up_ref, down_ref, x, tall):
    if tall == 0:
        return up_ref[2 * nx + x]
    if tall == ny + 1:
        return down_ref[2 * nx + x]
    return act_ref[x * ny + tall - 1]


def tall_spot(nx, ny, x, tall):
    if tall < 2:
        return nx * ny + x * ny + ny - 2 + tall
    if tall < ny + 2:
        return x * ny + tall - 2
    return nx * ny + x * ny + tall - ny - 2


def pack_x_body(
    nx, ny, even_ref, delta_ref, act_ref, edge_ref, up_ref, down_ref, near_ref, cross_ref, merged_ref
):
    lane = lane_ids(edge_ref.shape[0])
    half = 2 * nx * ny
    up = pltpu.roll(up_ref[3 * nx], half, 1)
    down = pltpu.roll(down_ref[3 * nx], half, 1)
    beyond = jnp.where(lax.rem(lane, 2 * ny) < ny, down, up)
    merged = jnp.where(lane < half, edge_ref[...], beyond)
    merged_ref[...] = merged

    def fill(low_ref, high_ref):
        for ref, planes, act_plane in ((low_ref, (0, 1), 0), (high_ref, (nx - 2, nx - 1), nx - 1)):
            for k in range(2):
                for tall in range(ny + 4):
                    ref[k * (ny + 4) + tall] = tall_delta(ny, delta_ref, up_ref, down_ref, planes[k], tall)
            base = 2 * (ny + 4)
            for tall in range(ny + 2):
                ref[base + tall] = tall_act(nx, ny, act_ref, up_ref, down_ref, act_plane, tall)
            ref[base + ny + 2] = merged

    @pl.when(even_ref[0] == 1)
    def _():
        fill(cross_ref, near_ref)

    @pl.when(even_ref[0] == 0)
    def _():
        fill(near_ref, cross_ref)


def store_shifts(shifted, plane, tall, block, edges, spot):
    before, after = z_shifts(block, edges, spot)
    at = slice(tall * LANES, (tall + 1) * LANES)
    shifted[0, plane, :, at] = after
    shifted[1, plane, :, at] = block
    shifted[2, plane, :, at] = before


def tap_rows(ny, plane_at, wide, taps):
    span = (ny + 2) * LANES
    return jnp.concatenate(
        [
            plane_at(c, wide + 2 - a, slice((2 - b) * LANES, (2 - b) * LANES + span))
            for a in taps
            for b in range(3)
            for c in range(3)
        ],
        0,
    )


def tap_back(w_ref, rows, taps):
    per = w_ref.shape[1] // 3
    return jnp.dot(
        w_ref[:, per * taps[0] : per * (taps[-1] + 1)], rows, preferred_element_type=F32
    )


def add_two(ny, totals, rows, acts, taps):
    inner = slice(LANES, (ny + 1) * LANES)
    term = lax.dot_general(
        rows[:, inner], acts[:, inner], (((1,), (1,)), ((), ())), preferred_element_type=F32
    )
    per = rows.shape[0] // len(taps)
    for k, a in enumerate(taps):
        totals[a] = add(totals[a], term[k * per : (k + 1) * per])


def finish_plane(ny, back, acts, wide, one_edges):
    delta = back * slope(acts.astype(F32))
    for tall in range(ny + 2):
        one_edges = put_edges(
            one_edges, delta[:, tall * LANES : (tall + 1) * LANES], wide * (ny + 2) + tall
        )
    return delta.astype(BF16), one_edges


def add_one(nx, ny, totals, one, wide, vol_ref, delta_plane):
    taps = [a for a in range(3) if 0 <= wide - 2 + a < nx]
    rhs = [one[:, (2 - b) * LANES : (2 - b + ny) * LANES] for b in range(3)]
    if delta_plane is not None:
        rhs.append(delta_plane)
    rhs = jnp.concatenate(rhs, 0)
    lhs = jnp.concatenate([vol_ref[wide - 2 + a] for a in taps], 0)
    term = lax.dot_general(lhs, rhs, (((1,), (1,)), ((), ())), preferred_element_type=F32)
    if delta_plane is None:
        term = jnp.concatenate([term, jnp.zeros((term.shape[0], one.shape[0]), F32)], 1)
    per = lhs.shape[0] // len(taps)
    for k, a in enumerate(taps):
        totals[a] = add(totals[a], term[k * per : (k + 1) * per])


def own_taps(nx, wide):
    return [a for a in range(3) if 2 <= wide + 2 - a <= nx + 1]


def add(total, term):
    return term if total is None else total + term


def inner_body(
    nx, ny, delta_ref, act_ref, edge_ref, merged_ref, up_ref, down_ref, vol_ref, w_ref,
    shifted, one_ref, one_edge_ref, two_ref, vol_out_ref, part_ref, first_ref,
):
    chan = edge_ref.shape[0]
    merged = merged_ref[...]
    for x in range(nx):
        for tall in range(ny + 4):
            block = tall_delta(ny, delta_ref, up_ref, down_ref, x, tall)
            store_shifts(shifted, x, tall, block, merged, tall_spot(nx, ny, x, tall))
    one_edges = jnp.zeros((chan, LANES), F32)
    totals = [None] * 3
    for wide in range(nx + 2):
        taps = own_taps(nx, wide)
        rows = tap_rows(ny, lambda c, plane, at: shifted[c, plane - 2, :, at], wide, taps)
        back = tap_back(w_ref, rows, taps)
        if 1 <= wide <= nx:
            acts = jnp.concatenate(
                [tall_act(nx, ny, act_ref, up_ref, down_ref, wide - 1, tall) for tall in range(ny + 2)], 1
            )
            add_two(ny, totals, rows, acts, taps)
        if 2 <= wide < nx:
            one_ref[wide - 2], one_edges = finish_plane(ny, back, acts, wide, one_edges)
        else:
            part_ref[wide if wide < 2 else wide - nx + 2] = back
    total = jnp.concatenate(totals, 0)
    one_edge_ref[...] = one_edges
    two_ref[...] = total
    edges = edge_ref[0:8].astype(F32)
    for x in range(nx):
        vol = vol_ref[x]
        shifts = [[], [], []]
        for y in range(ny):
            before, after = z_shifts(vol[y], edges, nx * ny + x * ny + y)
            shifts[0].append(before)
            shifts[1].append(vol[y])
            shifts[2].append(after)
        lhs = [jnp.concatenate(row, 1) for row in shifts] + [jnp.zeros((8, ny * LANES), F32)]
        vol_out_ref[x] = jnp.concatenate(lhs, 0).astype(BF16)
    totals = [None] * 3
    middle = slice(2 * LANES, (ny + 2) * LANES)
    for wide in range(2, nx):
        add_one(nx, ny, totals, one_ref[wide - 2], wide, vol_out_ref, shifted[1, wide - 1, :, middle])
    first_ref[...] = jnp.concatenate(totals, 0)


def outer_body(
    nx, ny, even_ref, act_ref, up_ref, down_ref, near_ref, cross_ref, w_ref,
    own_ref, inner_ref, inner_edge_ref, two_ref, vol_ref, part_ref, first_ref,
    sums_ref, one_ref, one_edge_ref, far, grad_two,
):
    chan = act_ref.shape[1]
    base = 2 * (ny + 4)
    even = jnp.broadcast_to(even_ref[0], (chan, LANES)) == 1

    def beside(side, index):
        near, cross = near_ref[index], cross_ref[index]
        return jnp.where(even, near, cross) if side else jnp.where(even, cross, near)

    for side in range(2):
        edges = beside(side, base + ny + 2)
        for k in range(2):
            for tall in range(ny + 4):
                from_x = nx - 2 + k if side == 0 else k
                store_shifts(
                    far, 2 * side + k, tall, beside(side, k * (ny + 4) + tall), edges, tall_spot(nx, ny, from_x, tall)
                )

    def plane_at(c, wide, at):
        if wide < 2:
            return far[c, wide, :, at]
        if wide < nx + 2:
            return own_ref[c, wide - 2, :, at]
        return far[c, wide - nx, :, at]

    one_edges = inner_edge_ref[...]
    totals = [None] * 3
    for wide in (0, 1, nx, nx + 1):
        if wide == 0:
            blocks = [beside(0, base + tall) for tall in range(ny + 2)]
        elif wide == nx + 1:
            blocks = [beside(1, base + tall) for tall in range(ny + 2)]
        else:
            blocks = [
                tall_act(nx, ny, act_ref, up_ref, down_ref, wide - 1, tall) for tall in range(ny + 2)
            ]
        acts = jnp.concatenate(blocks, 1)
        taps = [a for a in range(3) if a not in own_taps(nx, wide)]
        rows = tap_rows(ny, plane_at, wide, taps)
        back = part_ref[wide if wide < 2 else wide - nx + 2] + tap_back(w_ref, rows, taps)
        if 1 <= wide <= nx:
            add_two(ny, totals, rows, acts, taps)
        one_ref[wide], one_edges = finish_plane(ny, back, acts, wide, one_edges)
    third = 9 * chan
    for a in range(3):
        part = slice(third * a, third * (a + 1))
        grad_two[part, 0:chan] = two_ref[part, :] if totals[a] is None else two_ref[part, :] + totals[a]
    for x in range(1, nx - 1):
        one_ref[x + 1] = inner_ref[x - 1]
    one_edge_ref[...] = one_edges.astype(BF16).astype(F32)

    per = first_ref.shape[0] // 3
    totals = [first_ref[per * a : per * (a + 1), :] for a in range(3)]
    middle = slice(2 * LANES, (ny + 2) * LANES)
    for wide in (0, 1, nx, nx + 1):
        plane = own_ref[1, wide - 1, :, middle] if 1 <= wide <= nx else None
        add_one(nx, ny, totals, one_ref[wide], wide, vol_ref, plane)
    total_one = jnp.concatenate(
        [total[:, : 3 * chan] for total in totals] + [totals[1][:, 3 * chan :]], 1
    )

    lane = lane_ids(8)
    slots = grad_two.shape[0] // 8
    per = LANES // chan
    groups = -(-slots // per)
    tail = jnp.zeros((8, 2 * LANES - total_one.shape[1]), F32)
    tiles = [jnp.concatenate([total_one[8 * c : 8 * c + 8], tail], 1) for c in range(3)]
    head = lax.broadcasted_iota(jnp.int32, (8, 2 * LANES), 0) < 4
    first = jnp.where(head, tiles[0], pltpu.roll(tiles[1], 4, 0))
    second = jnp.where(head, tiles[2], tiles[1])
    sums_ref[groups * 8 : groups * 8 + 8, :] = first[:, :LANES]
    sums_ref[groups * 8 + 8 : groups * 8 + 16, :] = second[:, :LANES]
    rest = second[:, LANES:]
    rest = jnp.where(head[:, :LANES], rest, pltpu.roll(rest, LANES - chan, 1))
    spare = {slots: first[:, LANES:], slots + 1: rest}
    for group in range(groups):
        packed = jnp.zeros((8, LANES), F32)
        for s in range(per):
            slot = group * per + s
            if slot < slots:
                moved = grad_two[slot * 8 : slot * 8 + 8, :]
            else:
                moved = spare[slot]
            if s:
                moved = pltpu.roll(moved, chan * s, 1)
            packed = jnp.where((lane >= chan * s) & (lane < chan * (s + 1)), moved, packed)
        sums_ref[group * 8 : group * 8 + 8, :] = packed


def unpack_body(norm, sums_ref, one_ref, bias_one_ref, two_ref, bias_two_ref):
    chan = two_ref.shape[2]
    per = LANES // chan
    slots = 2 * two_ref.shape[0]
    for slot in range(slots):
        group, s = divmod(slot, per)
        block = sums_ref[group * 8 : group * 8 + 8, :] * norm
        if s:
            block = pltpu.roll(block, LANES - chan * s, 1)
        two_ref[slot // 2, (slot % 2) * 8 : (slot % 2) * 8 + 8, :] = block[:, :chan]
    base = slots // per * 8

    def piece(k, index):
        if index < per:
            block, s = sums_ref[base + 8 * (k + 1) : base + 8 * (k + 2), :], index
        else:
            block, s = sums_ref[base : base + 8, :], slots % per + k
        return (pltpu.roll(block, LANES - chan * s, 1) if s else block) * norm

    ins = one_ref.shape[1]
    for ab in range(9):
        first = piece(0, ab)
        second = piece(1, ab)
        one_ref[3 * ab] = first[0:ins, :chan]
        one_ref[3 * ab + 1] = first[4 : 4 + ins, :chan]
        one_ref[3 * ab + 2] = second[0:ins, :chan]
    bias_one_ref[...] = piece(1, 4)[4:5, :chan]
    bias_two_ref[...] = piece(1, 8)[4:5, :chan]


def volume_body(nx, ny, one_ref, edge_ref, w_ref, out_ref, shifted):
    edges = edge_ref[...].astype(BF16)
    for wide in range(nx + 2):
        for tall in range(ny + 2):
            at = slice(tall * LANES, (tall + 1) * LANES)
            block = one_ref[wide, :, at]
            before, after = z_shifts(block, edges, wide * (ny + 2) + tall)
            shifted[0, wide, :, at] = after
            shifted[1, wide, :, at] = before
    weights = w_ref[...]
    ins = out_ref.shape[0]
    for x in range(nx):
        rows = []
        for a in range(3):
            for b in range(3):
                at = slice((2 - b) * LANES, (2 - b + ny) * LANES)
                rows += [shifted[0, x + 2 - a, :, at], one_ref[x + 2 - a, :, at], shifted[1, x + 2 - a, :, at]]
        grad = jnp.dot(weights, jnp.concatenate(rows, 0), preferred_element_type=F32)
        stack = jnp.stack([grad[:8, y * LANES : (y + 1) * LANES] for y in range(ny)], 0)
        out_ref[:, x] = jnp.swapaxes(stack, 0, 1)[:ins]


def ring(axis, step):
    count = lax.axis_size(axis)
    return [(i, (i + step) % count) for i in range(count)]


def swap_edges(edges):
    if lax.axis_size("gz") == 2:
        return lax.ppermute(edges, "gz", ring("gz", 1))
    before = lax.ppermute(edges, "gz", ring("gz", 1))
    after = lax.ppermute(edges, "gz", ring("gz", -1))
    even = lax.broadcasted_iota(jnp.int32, edges.shape, 1) % 2 == 0
    return jnp.where(even, before, after)


def exchange(total, axis, step, cross):
    count = lax.axis_size(axis)
    if axis == "gx":
        return lax.ppermute(total, "gx", [(i, i ^ step ^ cross) for i in range(count)])
    pairs = [
        (i * count + k, (i ^ cross) * count + (k ^ step))
        for i in range(lax.axis_size("gx"))
        for k in range(count)
    ]
    return lax.ppermute(total, ("gx", axis), pairs)


def doublings(axis, first=1):
    step = first
    while step < lax.axis_size(axis):
        yield step
        step *= 2


def near(array):
    return pltpu.with_memory_space_constraint(array, pltpu.VMEM)


def call(body, out_shape, scratch, flops, *args):
    many = isinstance(out_shape, (tuple, list))
    spec = pl.BlockSpec(memory_space=pltpu.VMEM)
    return pl.pallas_call(
        body,
        out_shape=out_shape,
        in_specs=[
            pl.BlockSpec(memory_space=pltpu.SMEM) if arg.dtype == jnp.int32 else spec for arg in args
        ],
        out_specs=[spec] * len(out_shape) if many else spec,
        scratch_shapes=scratch,
        cost_estimate=pl.CostEstimate(flops=flops, bytes_accessed=1 << 18, transcendentals=0),
    )(*args)


def local(volume, act_one, act_two, weight_one, weight_two, cotangent):
    chan, nx, ny, nz = act_one.shape
    ins = volume.shape[0]
    cells = nx * ny * nz
    for axis in AXES:
        cells *= lax.axis_size(axis)
    norm = 1.0 / math.sqrt(cells)
    flat_two = jnp.transpose(weight_two, (1, 2, 3, 4, 0)).reshape(chan, 27 * chan)
    flat_one = jnp.transpose(weight_one, (1, 2, 3, 4, 0)).reshape(ins, 27 * chan)
    flat_one = jnp.pad(flat_one, ((0, chan - ins), (0, 0)))
    blocks = pltpu.VMEM((nx * ny, chan, LANES), BF16)
    edge = pltpu.VMEM((chan, LANES), BF16)
    flat_two = near(flat_two)
    flat_one = near(flat_one)

    delta, edges, vols = call(
        lambda *refs: prep_body(nx, ny, *refs),
        (blocks, edge, pltpu.VMEM((nx, ny, 8, LANES), F32)),
        [],
        1 << 20,
        cotangent, act_two, volume,
    )
    edges, act_one = lax.optimization_barrier((edges, act_one))
    act = call(lambda *refs: act_body(nx, ny, *refs), blocks, [], 1 << 24, act_one)
    edges = near(swap_edges(edges))
    delta, act = near(delta), near(act)
    side = pltpu.VMEM((3 * nx + 1, chan, LANES), BF16)
    low, high = call(
        lambda *refs: pack_y_body(nx, ny, *refs), (side, side), [], 1 << 20, delta, act, edges
    )
    down = near(lax.ppermute(low, "gy", ring("gy", -1)))
    up = near(lax.ppermute(high, "gy", ring("gy", 1)))
    side = pltpu.VMEM((3 * (ny + 4) - 1, chan, LANES), BF16)
    across = lax.axis_size("gx")
    even = (lax.axis_index("gx") % 2 == 0).astype(jnp.int32).reshape(1)
    near_side, cross_side, merged = call(
        lambda *refs: pack_x_body(nx, ny, *refs), (side, side, edge), [], 1 << 20,
        even, delta, act, edges, up, down,
    )
    cross_side = near(lax.ppermute(cross_side, "gx", [(i, (i + i % 2 * 2 - 1) % across) for i in range(across)]))
    near_side = near(lax.ppermute(near_side, "gx", [(i, i ^ 1) for i in range(across)]))
    span = (ny + 2) * LANES
    own, inner, inner_edges, inner_two, vols, part, inner_one = call(
        lambda *refs: inner_body(nx, ny, *refs),
        (
            pltpu.VMEM((3, nx, chan, (ny + 4) * LANES), BF16),
            pltpu.VMEM((nx - 2, chan, span), BF16),
            pltpu.VMEM((chan, LANES), F32),
            pltpu.VMEM((27 * chan, chan), F32),
            pltpu.VMEM((nx, 32, ny * LANES), BF16),
            pltpu.VMEM((4, chan, span), F32),
            pltpu.VMEM((96, 4 * chan), F32),
        ),
        [],
        1 << 27,
        delta, act, edges, near(merged), up, down, near(vols), flat_two,
    )
    slots = 27 * chan // 8
    rows = -(-slots // (LANES // chan)) * 8 + 16
    sums, one, one_edges = call(
        lambda *refs: outer_body(nx, ny, *refs),
        (
            pltpu.VMEM((rows, LANES), F32),
            pltpu.VMEM((nx + 2, chan, span), BF16),
            pltpu.VMEM((chan, LANES), F32),
        ),
        [
            pltpu.VMEM((3, 4, chan, (ny + 4) * LANES), BF16),
            pltpu.VMEM((27 * chan, LANES), F32),
        ],
        1 << 28,
        even, act, up, down, near_side, cross_side, flat_two,
        near(own), near(inner), near(inner_edges), near(inner_two), near(vols), near(part), near(inner_one),
    )
    if lax.axis_size("gz") == 2:
        moved = exchange(jnp.concatenate([sums, one_edges], 0), "gx", 1, 0)
        sums = sums + moved[:rows]
        moved = exchange(jnp.concatenate([sums, moved[rows:]], 0), "gz", 1, 1)
        sums = sums + moved[:rows]
        one_edges = moved[rows:]
    else:
        one_edges = swap_edges(one_edges)
        sums = sums + exchange(sums, "gx", 1, 0)
        for step in doublings("gz"):
            sums = sums + exchange(sums, "gz", step, 1)
    for step in doublings("gx", 2):
        sums = sums + exchange(sums, "gx", step, 1)
    grad_volume = call(
        lambda *refs: volume_body(nx, ny, *refs),
        jax.ShapeDtypeStruct(volume.shape, F32),
        [pltpu.VMEM((2, nx + 2, chan, span), BF16)],
        1 << 27,
        near(one), near(one_edges), flat_one,
    )
    sums, grad_volume = lax.optimization_barrier((sums, grad_volume))
    for step in doublings("gy"):
        sums = sums + exchange(sums, "gy", step, 1)
    sums = near(sums)
    grad_one, bias_one, grad_two, bias_two = call(
        lambda *refs: unpack_body(norm, *refs),
        (
            jax.ShapeDtypeStruct((27, ins, chan), F32),
            jax.ShapeDtypeStruct((1, chan), F32),
            jax.ShapeDtypeStruct((27, chan, chan), F32),
            jax.ShapeDtypeStruct((1, chan), F32),
        ),
        [],
        1 << 20,
        sums,
    )
    grad_one = jnp.transpose(grad_one.reshape(3, 3, 3, ins, chan), (4, 3, 0, 1, 2))
    grad_two = jnp.transpose(grad_two.reshape(3, 3, 3, chan, chan), (3, 4, 0, 1, 2))
    return (grad_one, bias_one.reshape(chan), grad_two, bias_two.reshape(chan), grad_volume)


def solution(mesh):
    placed = P(None, *AXES)
    return jax.shard_map(
        local,
        mesh=mesh,
        in_specs=(placed, placed, placed, P(), P(), placed),
        out_specs=(P(), P(), P(), P(), placed),
        check_vma=False,
    )
```

```python
import math

import jax
import jax.numpy as jnp
from jax import lax
from jax.experimental import pallas as pl
from jax.experimental.pallas import tpu as pltpu
from jax.sharding import PartitionSpec as P

AXES = ("gx", "gy", "gz")
F32 = jnp.float32
BF16 = jnp.bfloat16
LANES = 128


def lane_ids(rows):
    return lax.broadcasted_iota(jnp.int32, (rows, LANES), 1)


def slope(saved):
    return jnp.where(saved > 0, 1.0, 0.3).astype(F32)


def put_edges(packed, block, spot):
    lane = lane_ids(block.shape[0])
    moved = pltpu.roll(block, (2 * spot + 1) % LANES, 1)
    return jnp.where((lane == 2 * spot) | (lane == 2 * spot + 1), moved, packed)


def z_shifts(block, edges, spot):
    lane = lane_ids(block.shape[0])
    near = pltpu.roll(edges, (LANES - 2 * spot - 1) % LANES, 1)
    after = pltpu.roll(jnp.where(lane == 0, near, block), LANES - 1, 1)
    before = pltpu.roll(jnp.where(lane == LANES - 1, near, block), 1, 1)
    return before, after


def prep_body(nx, ny, cot_ref, act_two_ref, vol_ref, delta_ref, edge_ref, rows_ref):
    chan = cot_ref.shape[0]
    edges = jnp.zeros((chan, LANES), F32)
    vol_edges = jnp.zeros((8, LANES), F32)
    for x in range(nx):
        delta = cot_ref[:, x].astype(F32) * slope(act_two_ref[:, x].astype(F32))
        delta = jnp.swapaxes(delta, 0, 1)
        for y in range(ny):
            spot = x * ny + y
            delta_ref[spot] = delta[y].astype(BF16)
            edges = put_edges(edges, delta[y], spot)
        vol = vol_rows(vol_ref, x)
        for y in range(ny):
            rows_ref[x, y] = vol[y]
            vol_edges = put_edges(vol_edges, vol[y], nx * ny + x * ny + y)
    vol_edges = jnp.concatenate([vol_edges] * (chan // 8), 0)
    half = lane_ids(chan) < 2 * nx * ny
    edge_ref[...] = jnp.where(half, edges, vol_edges).astype(BF16)


def act_body(nx, ny, act_one_ref, act_ref):
    for x in range(nx):
        act = jnp.swapaxes(act_one_ref[:, x].astype(F32), 0, 1)
        for y in range(ny):
            act_ref[x * ny + y] = act[y].astype(BF16)


def vol_rows(vol_ref, x):
    vol = vol_ref[:, x].astype(F32)
    rest = jnp.ones((8 - vol.shape[0],) + vol.shape[1:], F32)
    return jnp.swapaxes(jnp.concatenate([vol, rest], 0), 0, 1)


def pack_y_body(nx, ny, delta_ref, act_ref, edge_ref, low_ref, high_ref):
    for x in range(nx):
        for k in range(2):
            low_ref[2 * x + k] = delta_ref[x * ny + k]
            high_ref[2 * x + k] = delta_ref[x * ny + ny - 2 + k]
        low_ref[2 * nx + x] = act_ref[x * ny]
        high_ref[2 * nx + x] = act_ref[x * ny + ny - 1]
    low_ref[3 * nx] = edge_ref[...]
    high_ref[3 * nx] = edge_ref[...]


def tall_delta(ny, delta_ref, up_ref, down_ref, x, tall):
    if tall < 2:
        return up_ref[2 * x + tall]
    if tall < ny + 2:
        return delta_ref[x * ny + tall - 2]
    return down_ref[2 * x + tall - ny - 2]


def tall_act(nx, ny, act_ref, up_ref, down_ref, x, tall):
    if tall == 0:
        return up_ref[2 * nx + x]
    if tall == ny + 1:
        return down_ref[2 * nx + x]
    return act_ref[x * ny + tall - 1]


def tall_spot(nx, ny, x, tall):
    if tall < 2:
        return nx * ny + x * ny + ny - 2 + tall
    if tall < ny + 2:
        return x * ny + tall - 2
    return nx * ny + x * ny + tall - ny - 2


def pack_x_body(
    nx, ny, even_ref, delta_ref, act_ref, edge_ref, up_ref, down_ref, near_ref, cross_ref, merged_ref
):
    lane = lane_ids(edge_ref.shape[0])
    half = 2 * nx * ny
    up = pltpu.roll(up_ref[3 * nx], half, 1)
    down = pltpu.roll(down_ref[3 * nx], half, 1)
    beyond = jnp.where(lax.rem(lane, 2 * ny) < ny, down, up)
    merged = jnp.where(lane < half, edge_ref[...], beyond)
    merged_ref[...] = merged

    def fill(low_ref, high_ref):
        for ref, planes, act_plane in ((low_ref, (0, 1), 0), (high_ref, (nx - 2, nx - 1), nx - 1)):
            for k in range(2):
                for tall in range(ny + 4):
                    ref[k * (ny + 4) + tall] = tall_delta(ny, delta_ref, up_ref, down_ref, planes[k], tall)
            base = 2 * (ny + 4)
            for tall in range(ny + 2):
                ref[base + tall] = tall_act(nx, ny, act_ref, up_ref, down_ref, act_plane, tall)
            ref[base + ny + 2] = merged

    @pl.when(even_ref[0] == 1)
    def _():
        fill(cross_ref, near_ref)

    @pl.when(even_ref[0] == 0)
    def _():
        fill(near_ref, cross_ref)


def store_shifts(shifted, plane, tall, block, edges, spot):
    before, after = z_shifts(block, edges, spot)
    at = slice(tall * LANES, (tall + 1) * LANES)
    shifted[0, plane, :, at] = after
    shifted[1, plane, :, at] = block
    shifted[2, plane, :, at] = before


def tap_rows(ny, plane_at, wide, taps):
    span = (ny + 2) * LANES
    return jnp.concatenate(
        [
            plane_at(c, wide + 2 - a, slice((2 - b) * LANES, (2 - b) * LANES + span))
            for a in taps
            for b in range(3)
            for c in range(3)
        ],
        0,
    )


def tap_back(w_ref, rows, taps):
    per = w_ref.shape[1] // 3
    return jnp.dot(
        w_ref[:, per * taps[0] : per * (taps[-1] + 1)], rows, preferred_element_type=F32
    )


def add_two(ny, totals, rows, acts, taps):
    inner = slice(LANES, (ny + 1) * LANES)
    term = lax.dot_general(
        rows[:, inner], acts[:, inner], (((1,), (1,)), ((), ())), preferred_element_type=F32
    )
    per = rows.shape[0] // len(taps)
    for k, a in enumerate(taps):
        totals[a] = add(totals[a], term[k * per : (k + 1) * per])


def finish_plane(ny, back, acts, wide, one_edges):
    delta = back * slope(acts.astype(F32))
    for tall in range(ny + 2):
        one_edges = put_edges(
            one_edges, delta[:, tall * LANES : (tall + 1) * LANES], wide * (ny + 2) + tall
        )
    return delta.astype(BF16), one_edges


def add_one(nx, ny, totals, one, wide, vol_ref, delta_plane):
    taps = [a for a in range(3) if 0 <= wide - 2 + a < nx]
    rhs = [one[:, (2 - b) * LANES : (2 - b + ny) * LANES] for b in range(3)]
    if delta_plane is not None:
        rhs.append(delta_plane)
    rhs = jnp.concatenate(rhs, 0)
    lhs = jnp.concatenate([vol_ref[wide - 2 + a] for a in taps], 0)
    term = lax.dot_general(lhs, rhs, (((1,), (1,)), ((), ())), preferred_element_type=F32)
    if delta_plane is None:
        term = jnp.concatenate([term, jnp.zeros((term.shape[0], one.shape[0]), F32)], 1)
    per = lhs.shape[0] // len(taps)
    for k, a in enumerate(taps):
        totals[a] = add(totals[a], term[k * per : (k + 1) * per])


def own_taps(nx, wide):
    return [a for a in range(3) if 2 <= wide + 2 - a <= nx + 1]


def add(total, term):
    return term if total is None else total + term


def inner_body(
    nx, ny, delta_ref, act_ref, edge_ref, merged_ref, up_ref, down_ref, vol_ref, w_ref,
    shifted, one_ref, one_edge_ref, two_ref, vol_out_ref, part_ref, first_ref,
):
    chan = edge_ref.shape[0]
    merged = merged_ref[...]
    for x in range(nx):
        for tall in range(ny + 4):
            block = tall_delta(ny, delta_ref, up_ref, down_ref, x, tall)
            store_shifts(shifted, x, tall, block, merged, tall_spot(nx, ny, x, tall))
    one_edges = jnp.zeros((chan, LANES), F32)
    totals = [None] * 3
    for wide in range(nx + 2):
        taps = own_taps(nx, wide)
        rows = tap_rows(ny, lambda c, plane, at: shifted[c, plane - 2, :, at], wide, taps)
        back = tap_back(w_ref, rows, taps)
        if 1 <= wide <= nx:
            acts = jnp.concatenate(
                [tall_act(nx, ny, act_ref, up_ref, down_ref, wide - 1, tall) for tall in range(ny + 2)], 1
            )
            add_two(ny, totals, rows, acts, taps)
        if 2 <= wide < nx:
            one_ref[wide - 2], one_edges = finish_plane(ny, back, acts, wide, one_edges)
        else:
            part_ref[wide if wide < 2 else wide - nx + 2] = back
    total = jnp.concatenate(totals, 0)
    one_edge_ref[...] = one_edges
    two_ref[...] = total
    edges = edge_ref[0:8].astype(F32)
    for x in range(nx):
        vol = vol_ref[x]
        shifts = [[], [], []]
        for y in range(ny):
            before, after = z_shifts(vol[y], edges, nx * ny + x * ny + y)
            shifts[0].append(before)
            shifts[1].append(vol[y])
            shifts[2].append(after)
        lhs = [jnp.concatenate(row, 1) for row in shifts] + [jnp.zeros((8, ny * LANES), F32)]
        vol_out_ref[x] = jnp.concatenate(lhs, 0).astype(BF16)
    totals = [None] * 3
    middle = slice(2 * LANES, (ny + 2) * LANES)
    for wide in range(2, nx):
        add_one(nx, ny, totals, one_ref[wide - 2], wide, vol_out_ref, shifted[1, wide - 1, :, middle])
    first_ref[...] = jnp.concatenate(totals, 0)


def outer_body(
    nx, ny, even_ref, act_ref, up_ref, down_ref, cross_ref, near_ref, w_ref,
    own_ref, inner_ref, inner_edge_ref, two_ref, vol_ref, part_ref, first_ref,
    sums_ref, one_ref, one_edge_ref, far, grad_two,
):
    chan = act_ref.shape[1]
    base = 2 * (ny + 4)
    even = jnp.broadcast_to(even_ref[0], (chan, LANES)) == 1

    def beside(side, index):
        near, cross = near_ref[index], cross_ref[index]
        return jnp.where(even, near, cross) if side else jnp.where(even, cross, near)

    for side in range(2):
        edges = beside(side, base + ny + 2)
        for k in range(2):
            for tall in range(ny + 4):
                from_x = nx - 2 + k if side == 0 else k
                store_shifts(
                    far, 2 * side + k, tall, beside(side, k * (ny + 4) + tall), edges, tall_spot(nx, ny, from_x, tall)
                )

    def plane_at(c, wide, at):
        if wide < 2:
            return far[c, wide, :, at]
        if wide < nx + 2:
            return own_ref[c, wide - 2, :, at]
        return far[c, wide - nx, :, at]

    one_edges = inner_edge_ref[...]
    totals = [None] * 3
    for wide in (0, 1, nx, nx + 1):
        if wide == 0:
            blocks = [beside(0, base + tall) for tall in range(ny + 2)]
        elif wide == nx + 1:
            blocks = [beside(1, base + tall) for tall in range(ny + 2)]
        else:
            blocks = [
                tall_act(nx, ny, act_ref, up_ref, down_ref, wide - 1, tall) for tall in range(ny + 2)
            ]
        acts = jnp.concatenate(blocks, 1)
        taps = [a for a in range(3) if a not in own_taps(nx, wide)]
        rows = tap_rows(ny, plane_at, wide, taps)
        back = part_ref[wide if wide < 2 else wide - nx + 2] + tap_back(w_ref, rows, taps)
        if 1 <= wide <= nx:
            add_two(ny, totals, rows, acts, taps)
        one_ref[wide], one_edges = finish_plane(ny, back, acts, wide, one_edges)
    third = 9 * chan
    for a in range(3):
        part = slice(third * a, third * (a + 1))
        grad_two[part, 0:chan] = two_ref[part, :] if totals[a] is None else two_ref[part, :] + totals[a]
    for x in range(1, nx - 1):
        one_ref[x + 1] = inner_ref[x - 1]
    one_edge_ref[...] = one_edges.astype(BF16).astype(F32)

    per = first_ref.shape[0] // 3
    totals = [first_ref[per * a : per * (a + 1), :] for a in range(3)]
    middle = slice(2 * LANES, (ny + 2) * LANES)
    for wide in (0, 1, nx, nx + 1):
        plane = own_ref[1, wide - 1, :, middle] if 1 <= wide <= nx else None
        add_one(nx, ny, totals, one_ref[wide], wide, vol_ref, plane)
    total_one = jnp.concatenate(
        [total[:, : 3 * chan] for total in totals] + [totals[1][:, 3 * chan :]], 1
    )

    lane = lane_ids(8)
    slots = grad_two.shape[0] // 8
    per = LANES // chan
    groups = -(-slots // per)
    tail = jnp.zeros((8, 2 * LANES - total_one.shape[1]), F32)
    tiles = [jnp.concatenate([total_one[8 * c : 8 * c + 8], tail], 1) for c in range(3)]
    head = lax.broadcasted_iota(jnp.int32, (8, 2 * LANES), 0) < 4
    first = jnp.where(head, tiles[0], pltpu.roll(tiles[1], 4, 0))
    second = jnp.where(head, tiles[2], tiles[1])
    sums_ref[groups * 8 : groups * 8 + 8, :] = first[:, :LANES]
    sums_ref[groups * 8 + 8 : groups * 8 + 16, :] = second[:, :LANES]
    rest = second[:, LANES:]
    rest = jnp.where(head[:, :LANES], rest, pltpu.roll(rest, LANES - chan, 1))
    spare = {slots: first[:, LANES:], slots + 1: rest}
    for group in range(groups):
        packed = jnp.zeros((8, LANES), F32)
        for s in range(per):
            slot = group * per + s
            if slot < slots:
                moved = grad_two[slot * 8 : slot * 8 + 8, :]
            else:
                moved = spare[slot]
            if s:
                moved = pltpu.roll(moved, chan * s, 1)
            packed = jnp.where((lane >= chan * s) & (lane < chan * (s + 1)), moved, packed)
        sums_ref[group * 8 : group * 8 + 8, :] = packed


def unpack_body(norm, sums_ref, one_ref, bias_one_ref, two_ref, bias_two_ref):
    chan = two_ref.shape[2]
    per = LANES // chan
    slots = 2 * two_ref.shape[0]
    for slot in range(slots):
        group, s = divmod(slot, per)
        block = sums_ref[group * 8 : group * 8 + 8, :] * norm
        if s:
            block = pltpu.roll(block, LANES - chan * s, 1)
        two_ref[slot // 2, (slot % 2) * 8 : (slot % 2) * 8 + 8, :] = block[:, :chan]
    base = slots // per * 8

    def piece(k, index):
        if index < per:
            block, s = sums_ref[base + 8 * (k + 1) : base + 8 * (k + 2), :], index
        else:
            block, s = sums_ref[base : base + 8, :], slots % per + k
        return (pltpu.roll(block, LANES - chan * s, 1) if s else block) * norm

    ins = one_ref.shape[1]
    for ab in range(9):
        first = piece(0, ab)
        second = piece(1, ab)
        one_ref[3 * ab] = first[0:ins, :chan]
        one_ref[3 * ab + 1] = first[4 : 4 + ins, :chan]
        one_ref[3 * ab + 2] = second[0:ins, :chan]
    bias_one_ref[...] = piece(1, 4)[4:5, :chan]
    bias_two_ref[...] = piece(1, 8)[4:5, :chan]


def volume_body(nx, ny, one_ref, edge_ref, w_ref, out_ref, shifted):
    edges = edge_ref[...].astype(BF16)
    for wide in range(nx + 2):
        for tall in range(ny + 2):
            at = slice(tall * LANES, (tall + 1) * LANES)
            block = one_ref[wide, :, at]
            before, after = z_shifts(block, edges, wide * (ny + 2) + tall)
            shifted[0, wide, :, at] = after
            shifted[1, wide, :, at] = before
    weights = w_ref[...]
    ins = out_ref.shape[0]
    for x in range(nx):
        rows = []
        for a in range(3):
            for b in range(3):
                at = slice((2 - b) * LANES, (2 - b + ny) * LANES)
                rows += [shifted[0, x + 2 - a, :, at], one_ref[x + 2 - a, :, at], shifted[1, x + 2 - a, :, at]]
        grad = jnp.dot(weights, jnp.concatenate(rows, 0), preferred_element_type=F32)
        stack = jnp.stack([grad[:8, y * LANES : (y + 1) * LANES] for y in range(ny)], 0)
        out_ref[:, x] = jnp.swapaxes(stack, 0, 1)[:ins]


def ring(axis, step):
    count = lax.axis_size(axis)
    return [(i, (i + step) % count) for i in range(count)]


def swap_edges(edges):
    if lax.axis_size("gz") == 2:
        return lax.ppermute(edges, "gz", ring("gz", 1))
    before = lax.ppermute(edges, "gz", ring("gz", 1))
    after = lax.ppermute(edges, "gz", ring("gz", -1))
    even = lax.broadcasted_iota(jnp.int32, edges.shape, 1) % 2 == 0
    return jnp.where(even, before, after)


def exchange(total, axis, step, cross):
    count = lax.axis_size(axis)
    if axis == "gx":
        return lax.ppermute(total, "gx", [(i, i ^ step ^ cross) for i in range(count)])
    pairs = [
        (i * count + k, (i ^ cross) * count + (k ^ step))
        for i in range(lax.axis_size("gx"))
        for k in range(count)
    ]
    return lax.ppermute(total, ("gx", axis), pairs)


def doublings(axis, first=1):
    step = first
    while step < lax.axis_size(axis):
        yield step
        step *= 2


def near(array):
    return pltpu.with_memory_space_constraint(array, pltpu.VMEM)


def call(body, out_shape, scratch, flops, *args):
    many = isinstance(out_shape, (tuple, list))
    spec = pl.BlockSpec(memory_space=pltpu.VMEM)
    return pl.pallas_call(
        body,
        out_shape=out_shape,
        in_specs=[
            pl.BlockSpec(memory_space=pltpu.SMEM) if arg.dtype == jnp.int32 else spec for arg in args
        ],
        out_specs=[spec] * len(out_shape) if many else spec,
        scratch_shapes=scratch,
        cost_estimate=pl.CostEstimate(flops=flops, bytes_accessed=1 << 18, transcendentals=0),
    )(*args)


def local(volume, act_one, act_two, weight_one, weight_two, cotangent):
    chan, nx, ny, nz = act_one.shape
    ins = volume.shape[0]
    cells = nx * ny * nz
    for axis in AXES:
        cells *= lax.axis_size(axis)
    norm = 1.0 / math.sqrt(cells)
    flat_two = jnp.transpose(weight_two, (1, 2, 3, 4, 0)).reshape(chan, 27 * chan)
    flat_one = jnp.transpose(weight_one, (1, 2, 3, 4, 0)).reshape(ins, 27 * chan)
    flat_one = jnp.pad(flat_one, ((0, chan - ins), (0, 0)))
    blocks = pltpu.VMEM((nx * ny, chan, LANES), BF16)
    edge = pltpu.VMEM((chan, LANES), BF16)
    flat_two = near(flat_two)
    flat_one = near(flat_one)

    delta, edges, vols = call(
        lambda *refs: prep_body(nx, ny, *refs),
        (blocks, edge, pltpu.VMEM((nx, ny, 8, LANES), F32)),
        [],
        1 << 20,
        cotangent, act_two, volume,
    )
    edges, act_one = lax.optimization_barrier((edges, act_one))
    act = call(lambda *refs: act_body(nx, ny, *refs), blocks, [], 1 << 24, act_one)
    edges = near(swap_edges(edges))
    delta, act = near(delta), near(act)
    side = pltpu.VMEM((3 * nx + 1, chan, LANES), BF16)
    low, high = call(
        lambda *refs: pack_y_body(nx, ny, *refs), (side, side), [], 1 << 20, delta, act, edges
    )
    down = near(lax.ppermute(low, "gy", ring("gy", -1)))
    up = near(lax.ppermute(high, "gy", ring("gy", 1)))
    side = pltpu.VMEM((3 * (ny + 4) - 1, chan, LANES), BF16)
    across = lax.axis_size("gx")
    even = (lax.axis_index("gx") % 2 == 0).astype(jnp.int32).reshape(1)
    near_side, cross_side, merged = call(
        lambda *refs: pack_x_body(nx, ny, *refs), (side, side, edge), [], 1 << 20,
        even, delta, act, edges, up, down,
    )
    near_side = near(lax.ppermute(near_side, "gx", [(i, i ^ 1) for i in range(across)]))
    cross_side = near(lax.ppermute(cross_side, "gx", [(i, (i + i % 2 * 2 - 1) % across) for i in range(across)]))
    span = (ny + 2) * LANES
    own, inner, inner_edges, inner_two, vols, part, inner_one = call(
        lambda *refs: inner_body(nx, ny, *refs),
        (
            pltpu.VMEM((3, nx, chan, (ny + 4) * LANES), BF16),
            pltpu.VMEM((nx - 2, chan, span), BF16),
            pltpu.VMEM((chan, LANES), F32),
            pltpu.VMEM((27 * chan, chan), F32),
            pltpu.VMEM((nx, 32, ny * LANES), BF16),
            pltpu.VMEM((4, chan, span), F32),
            pltpu.VMEM((96, 4 * chan), F32),
        ),
        [],
        1 << 27,
        delta, act, edges, near(merged), up, down, near(vols), flat_two,
    )
    slots = 27 * chan // 8
    rows = -(-slots // (LANES // chan)) * 8 + 16
    sums, one, one_edges = call(
        lambda *refs: outer_body(nx, ny, *refs),
        (
            pltpu.VMEM((rows, LANES), F32),
            pltpu.VMEM((nx + 2, chan, span), BF16),
            pltpu.VMEM((chan, LANES), F32),
        ),
        [
            pltpu.VMEM((3, 4, chan, (ny + 4) * LANES), BF16),
            pltpu.VMEM((27 * chan, LANES), F32),
        ],
        1 << 28,
        even, act, up, down, cross_side, near_side, flat_two,
        near(own), near(inner), near(inner_edges), near(inner_two), near(vols), near(part), near(inner_one),
    )
    if lax.axis_size("gz") == 2:
        moved = exchange(jnp.concatenate([sums, one_edges], 0), "gx", 1, 0)
        sums = sums + moved[:rows]
        moved = exchange(jnp.concatenate([sums, moved[rows:]], 0), "gz", 1, 1)
        sums = sums + moved[:rows]
        one_edges = moved[rows:]
    else:
        one_edges = swap_edges(one_edges)
        sums = sums + exchange(sums, "gx", 1, 0)
        for step in doublings("gz"):
            sums = sums + exchange(sums, "gz", step, 1)
    for step in doublings("gx", 2):
        sums = sums + exchange(sums, "gx", step, 1)
    grad_volume = call(
        lambda *refs: volume_body(nx, ny, *refs),
        jax.ShapeDtypeStruct(volume.shape, F32),
        [pltpu.VMEM((2, nx + 2, chan, span), BF16)],
        1 << 27,
        near(one), near(one_edges), flat_one,
    )
    sums, grad_volume = lax.optimization_barrier((sums, grad_volume))
    for step in doublings("gy"):
        sums = sums + exchange(sums, "gy", step, 1)
    sums = near(sums)
    grad_one, bias_one, grad_two, bias_two = call(
        lambda *refs: unpack_body(norm, *refs),
        (
            jax.ShapeDtypeStruct((27, ins, chan), F32),
            jax.ShapeDtypeStruct((1, chan), F32),
            jax.ShapeDtypeStruct((27, chan, chan), F32),
            jax.ShapeDtypeStruct((1, chan), F32),
        ),
        [],
        1 << 20,
        sums,
    )
    grad_one = jnp.transpose(grad_one.reshape(3, 3, 3, ins, chan), (4, 3, 0, 1, 2))
    grad_two = jnp.transpose(grad_two.reshape(3, 3, 3, chan, chan), (3, 4, 0, 1, 2))
    return (grad_one, bias_one.reshape(chan), grad_two, bias_two.reshape(chan), grad_volume)


def solution(mesh):
    placed = P(None, *AXES)
    return jax.shard_map(
        local,
        mesh=mesh,
        in_specs=(placed, placed, placed, P(), P(), placed),
        out_specs=(P(), P(), P(), P(), placed),
        check_vma=False,
    )
```

```python
import math

import jax
import jax.numpy as jnp
from jax import lax
from jax.experimental import pallas as pl
from jax.experimental.pallas import tpu as pltpu
from jax.sharding import PartitionSpec as P

AXES = ("gx", "gy", "gz")
F32 = jnp.float32
BF16 = jnp.bfloat16
LANES = 128


def lane_ids(rows):
    return lax.broadcasted_iota(jnp.int32, (rows, LANES), 1)


def slope(saved):
    return jnp.where(saved > 0, 1.0, 0.3).astype(F32)


def put_edges(packed, block, spot):
    lane = lane_ids(block.shape[0])
    moved = pltpu.roll(block, (2 * spot + 1) % LANES, 1)
    return jnp.where((lane == 2 * spot) | (lane == 2 * spot + 1), moved, packed)


def z_shifts(block, edges, spot):
    lane = lane_ids(block.shape[0])
    near = pltpu.roll(edges, (LANES - 2 * spot - 1) % LANES, 1)
    after = pltpu.roll(jnp.where(lane == 0, near, block), LANES - 1, 1)
    before = pltpu.roll(jnp.where(lane == LANES - 1, near, block), 1, 1)
    return before, after


def prep_body(nx, ny, cot_ref, act_two_ref, vol_ref, delta_ref, edge_ref, rows_ref):
    chan = cot_ref.shape[0]
    edges = jnp.zeros((chan, LANES), F32)
    vol_edges = jnp.zeros((8, LANES), F32)
    for x in range(nx):
        delta = cot_ref[:, x].astype(F32) * slope(act_two_ref[:, x].astype(F32))
        delta = jnp.swapaxes(delta, 0, 1)
        for y in range(ny):
            spot = x * ny + y
            delta_ref[spot] = delta[y].astype(BF16)
            edges = put_edges(edges, delta[y], spot)
        vol = vol_rows(vol_ref, x)
        for y in range(ny):
            rows_ref[x, y] = vol[y]
            vol_edges = put_edges(vol_edges, vol[y], nx * ny + x * ny + y)
    vol_edges = jnp.concatenate([vol_edges] * (chan // 8), 0)
    half = lane_ids(chan) < 2 * nx * ny
    edge_ref[...] = jnp.where(half, edges, vol_edges).astype(BF16)


def act_body(nx, ny, even_ref, act_one_ref, act_ref, face_ref):
    for x in range(nx):
        act = jnp.swapaxes(act_one_ref[:, x].astype(F32), 0, 1)
        for y in range(ny):
            act_ref[x * ny + y] = act[y].astype(BF16)

    @pl.when(even_ref[0] == 1)
    def _():
        for y in range(ny):
            face_ref[y] = act_ref[y]

    @pl.when(even_ref[0] == 0)
    def _():
        for y in range(ny):
            face_ref[y] = act_ref[(nx - 1) * ny + y]


def vol_rows(vol_ref, x):
    vol = vol_ref[:, x].astype(F32)
    rest = jnp.ones((8 - vol.shape[0],) + vol.shape[1:], F32)
    return jnp.swapaxes(jnp.concatenate([vol, rest], 0), 0, 1)


def pack_y_body(nx, ny, delta_ref, act_ref, edge_ref, low_ref, high_ref):
    for x in range(nx):
        for k in range(2):
            low_ref[2 * x + k] = delta_ref[x * ny + k]
            high_ref[2 * x + k] = delta_ref[x * ny + ny - 2 + k]
        low_ref[2 * nx + x] = act_ref[x * ny]
        high_ref[2 * nx + x] = act_ref[x * ny + ny - 1]
    low_ref[3 * nx] = edge_ref[...]
    high_ref[3 * nx] = edge_ref[...]


def tall_delta(ny, delta_ref, up_ref, down_ref, x, tall):
    if tall < 2:
        return up_ref[2 * x + tall]
    if tall < ny + 2:
        return delta_ref[x * ny + tall - 2]
    return down_ref[2 * x + tall - ny - 2]


def tall_act(nx, ny, act_ref, up_ref, down_ref, x, tall):
    if tall == 0:
        return up_ref[2 * nx + x]
    if tall == ny + 1:
        return down_ref[2 * nx + x]
    return act_ref[x * ny + tall - 1]


def tall_spot(nx, ny, x, tall):
    if tall < 2:
        return nx * ny + x * ny + ny - 2 + tall
    if tall < ny + 2:
        return x * ny + tall - 2
    return nx * ny + x * ny + tall - ny - 2


def pack_x_body(
    nx, ny, even_ref, delta_ref, act_ref, edge_ref, up_ref, down_ref, near_ref, cross_ref, merged_ref
):
    lane = lane_ids(edge_ref.shape[0])
    half = 2 * nx * ny
    up = pltpu.roll(up_ref[3 * nx], half, 1)
    down = pltpu.roll(down_ref[3 * nx], half, 1)
    beyond = jnp.where(lax.rem(lane, 2 * ny) < ny, down, up)
    merged = jnp.where(lane < half, edge_ref[...], beyond)
    merged_ref[...] = merged

    def fill(ref, planes, act_plane, rows):
        for k in range(2):
            for tall in range(ny + 4):
                ref[k * (ny + 4) + tall] = tall_delta(ny, delta_ref, up_ref, down_ref, planes[k], tall)
        base = 2 * (ny + 4)
        for k, tall in enumerate(rows):
            ref[base + k] = tall_act(nx, ny, act_ref, up_ref, down_ref, act_plane, tall)
        ref[base + len(rows)] = merged

    low, high = ((0, 1), 0), ((nx - 2, nx - 1), nx - 1)
    every, ends = list(range(ny + 2)), [0, ny + 1]

    @pl.when(even_ref[0] == 1)
    def _():
        fill(cross_ref, *low, ends)
        fill(near_ref, *high, every)

    @pl.when(even_ref[0] == 0)
    def _():
        fill(cross_ref, *high, ends)
        fill(near_ref, *low, every)


def store_shifts(shifted, plane, tall, block, edges, spot):
    before, after = z_shifts(block, edges, spot)
    at = slice(tall * LANES, (tall + 1) * LANES)
    shifted[0, plane, :, at] = after
    shifted[1, plane, :, at] = block
    shifted[2, plane, :, at] = before


def tap_rows(ny, plane_at, wide, taps):
    span = (ny + 2) * LANES
    return jnp.concatenate(
        [
            plane_at(c, wide + 2 - a, slice((2 - b) * LANES, (2 - b) * LANES + span))
            for a in taps
            for b in range(3)
            for c in range(3)
        ],
        0,
    )


def tap_back(w_ref, rows, taps):
    per = w_ref.shape[1] // 3
    return jnp.dot(
        w_ref[:, per * taps[0] : per * (taps[-1] + 1)], rows, preferred_element_type=F32
    )


def add_two(ny, totals, rows, acts, taps):
    inner = slice(LANES, (ny + 1) * LANES)
    term = lax.dot_general(
        rows[:, inner], acts[:, inner], (((1,), (1,)), ((), ())), preferred_element_type=F32
    )
    per = rows.shape[0] // len(taps)
    for k, a in enumerate(taps):
        totals[a] = add(totals[a], term[k * per : (k + 1) * per])


def finish_plane(ny, back, acts, wide, one_edges):
    delta = back * slope(acts.astype(F32))
    for tall in range(ny + 2):
        one_edges = put_edges(
            one_edges, delta[:, tall * LANES : (tall + 1) * LANES], wide * (ny + 2) + tall
        )
    return delta.astype(BF16), one_edges


def add_one(nx, ny, totals, one, wide, vol_ref, delta_plane):
    taps = [a for a in range(3) if 0 <= wide - 2 + a < nx]
    rhs = [one[:, (2 - b) * LANES : (2 - b + ny) * LANES] for b in range(3)]
    if delta_plane is not None:
        rhs.append(delta_plane)
    rhs = jnp.concatenate(rhs, 0)
    lhs = jnp.concatenate([vol_ref[wide - 2 + a] for a in taps], 0)
    term = lax.dot_general(lhs, rhs, (((1,), (1,)), ((), ())), preferred_element_type=F32)
    if delta_plane is None:
        term = jnp.concatenate([term, jnp.zeros((term.shape[0], one.shape[0]), F32)], 1)
    per = lhs.shape[0] // len(taps)
    for k, a in enumerate(taps):
        totals[a] = add(totals[a], term[k * per : (k + 1) * per])


def own_taps(nx, wide):
    return [a for a in range(3) if 2 <= wide + 2 - a <= nx + 1]


def add(total, term):
    return term if total is None else total + term


def inner_body(
    nx, ny, delta_ref, act_ref, edge_ref, merged_ref, up_ref, down_ref, vol_ref, w_ref,
    shifted, one_ref, one_edge_ref, two_ref, vol_out_ref, part_ref, first_ref,
):
    chan = edge_ref.shape[0]
    merged = merged_ref[...]
    for x in range(nx):
        for tall in range(ny + 4):
            block = tall_delta(ny, delta_ref, up_ref, down_ref, x, tall)
            store_shifts(shifted, x, tall, block, merged, tall_spot(nx, ny, x, tall))
    one_edges = jnp.zeros((chan, LANES), F32)
    totals = [None] * 3
    for wide in range(nx + 2):
        taps = own_taps(nx, wide)
        rows = tap_rows(ny, lambda c, plane, at: shifted[c, plane - 2, :, at], wide, taps)
        back = tap_back(w_ref, rows, taps)
        if 1 <= wide <= nx:
            acts = jnp.concatenate(
                [tall_act(nx, ny, act_ref, up_ref, down_ref, wide - 1, tall) for tall in range(ny + 2)], 1
            )
            add_two(ny, totals, rows, acts, taps)
        if 2 <= wide < nx:
            one_ref[wide - 2], one_edges = finish_plane(ny, back, acts, wide, one_edges)
        else:
            part_ref[wide if wide < 2 else wide - nx + 2] = back
    total = jnp.concatenate(totals, 0)
    one_edge_ref[...] = one_edges
    two_ref[...] = total
    edges = edge_ref[0:8].astype(F32)
    for x in range(nx):
        vol = vol_ref[x]
        shifts = [[], [], []]
        for y in range(ny):
            before, after = z_shifts(vol[y], edges, nx * ny + x * ny + y)
            shifts[0].append(before)
            shifts[1].append(vol[y])
            shifts[2].append(after)
        lhs = [jnp.concatenate(row, 1) for row in shifts] + [jnp.zeros((8, ny * LANES), F32)]
        vol_out_ref[x] = jnp.concatenate(lhs, 0).astype(BF16)
    totals = [None] * 3
    middle = slice(2 * LANES, (ny + 2) * LANES)
    for wide in range(2, nx):
        add_one(nx, ny, totals, one_ref[wide - 2], wide, vol_out_ref, shifted[1, wide - 1, :, middle])
    first_ref[...] = jnp.concatenate(totals, 0)


def outer_body(
    nx, ny, even_ref, act_ref, up_ref, down_ref, near_ref, cross_ref, face_ref, w_ref,
    own_ref, inner_ref, inner_edge_ref, two_ref, vol_ref, part_ref, first_ref,
    sums_ref, one_ref, one_edge_ref, far, grad_two,
):
    chan = act_ref.shape[1]
    base = 2 * (ny + 4)
    even = jnp.broadcast_to(even_ref[0], (chan, LANES)) == 1

    def choose(side, near, cross):
        return jnp.where(even, near, cross) if side else jnp.where(even, cross, near)

    def act_beside(side, tall):
        if tall == 0:
            cross = cross_ref[base]
        elif tall == ny + 1:
            cross = cross_ref[base + 1]
        else:
            cross = face_ref[tall - 1]
        return choose(side, near_ref[base + tall], cross)

    for side in range(2):
        edges = choose(side, near_ref[base + ny + 2], cross_ref[base + 2])
        for k in range(2):
            for tall in range(ny + 4):
                from_x = nx - 2 + k if side == 0 else k
                at = k * (ny + 4) + tall
                block = choose(side, near_ref[at], cross_ref[at])
                store_shifts(far, 2 * side + k, tall, block, edges, tall_spot(nx, ny, from_x, tall))

    def plane_at(c, wide, at):
        if wide < 2:
            return far[c, wide, :, at]
        if wide < nx + 2:
            return own_ref[c, wide - 2, :, at]
        return far[c, wide - nx, :, at]

    one_edges = inner_edge_ref[...]
    totals = [None] * 3
    for wide in (0, 1, nx, nx + 1):
        if wide == 0:
            blocks = [act_beside(0, tall) for tall in range(ny + 2)]
        elif wide == nx + 1:
            blocks = [act_beside(1, tall) for tall in range(ny + 2)]
        else:
            blocks = [
                tall_act(nx, ny, act_ref, up_ref, down_ref, wide - 1, tall) for tall in range(ny + 2)
            ]
        acts = jnp.concatenate(blocks, 1)
        taps = [a for a in range(3) if a not in own_taps(nx, wide)]
        rows = tap_rows(ny, plane_at, wide, taps)
        back = part_ref[wide if wide < 2 else wide - nx + 2] + tap_back(w_ref, rows, taps)
        if 1 <= wide <= nx:
            add_two(ny, totals, rows, acts, taps)
        one_ref[wide], one_edges = finish_plane(ny, back, acts, wide, one_edges)
    third = 9 * chan
    for a in range(3):
        part = slice(third * a, third * (a + 1))
        grad_two[part, 0:chan] = two_ref[part, :] if totals[a] is None else two_ref[part, :] + totals[a]
    for x in range(1, nx - 1):
        one_ref[x + 1] = inner_ref[x - 1]
    one_edge_ref[...] = one_edges.astype(BF16).astype(F32)

    per = first_ref.shape[0] // 3
    totals = [first_ref[per * a : per * (a + 1), :] for a in range(3)]
    middle = slice(2 * LANES, (ny + 2) * LANES)
    for wide in (0, 1, nx, nx + 1):
        plane = own_ref[1, wide - 1, :, middle] if 1 <= wide <= nx else None
        add_one(nx, ny, totals, one_ref[wide], wide, vol_ref, plane)
    total_one = jnp.concatenate(
        [total[:, : 3 * chan] for total in totals] + [totals[1][:, 3 * chan :]], 1
    )

    lane = lane_ids(8)
    slots = grad_two.shape[0] // 8
    per = LANES // chan
    groups = -(-slots // per)
    tail = jnp.zeros((8, 2 * LANES - total_one.shape[1]), F32)
    tiles = [jnp.concatenate([total_one[8 * c : 8 * c + 8], tail], 1) for c in range(3)]
    head = lax.broadcasted_iota(jnp.int32, (8, 2 * LANES), 0) < 4
    first = jnp.where(head, tiles[0], pltpu.roll(tiles[1], 4, 0))
    second = jnp.where(head, tiles[2], tiles[1])
    sums_ref[groups * 8 : groups * 8 + 8, :] = first[:, :LANES]
    sums_ref[groups * 8 + 8 : groups * 8 + 16, :] = second[:, :LANES]
    rest = second[:, LANES:]
    rest = jnp.where(head[:, :LANES], rest, pltpu.roll(rest, LANES - chan, 1))
    spare = {slots: first[:, LANES:], slots + 1: rest}
    for group in range(groups):
        packed = jnp.zeros((8, LANES), F32)
        for s in range(per):
            slot = group * per + s
            if slot < slots:
                moved = grad_two[slot * 8 : slot * 8 + 8, :]
            else:
                moved = spare[slot]
            if s:
                moved = pltpu.roll(moved, chan * s, 1)
            packed = jnp.where((lane >= chan * s) & (lane < chan * (s + 1)), moved, packed)
        sums_ref[group * 8 : group * 8 + 8, :] = packed


def unpack_body(norm, sums_ref, one_ref, bias_one_ref, two_ref, bias_two_ref):
    chan = two_ref.shape[2]
    per = LANES // chan
    slots = 2 * two_ref.shape[0]
    for slot in range(slots):
        group, s = divmod(slot, per)
        block = sums_ref[group * 8 : group * 8 + 8, :] * norm
        if s:
            block = pltpu.roll(block, LANES - chan * s, 1)
        two_ref[slot // 2, (slot % 2) * 8 : (slot % 2) * 8 + 8, :] = block[:, :chan]
    base = slots // per * 8

    def piece(k, index):
        if index < per:
            block, s = sums_ref[base + 8 * (k + 1) : base + 8 * (k + 2), :], index
        else:
            block, s = sums_ref[base : base + 8, :], slots % per + k
        return (pltpu.roll(block, LANES - chan * s, 1) if s else block) * norm

    ins = one_ref.shape[1]
    for ab in range(9):
        first = piece(0, ab)
        second = piece(1, ab)
        one_ref[3 * ab] = first[0:ins, :chan]
        one_ref[3 * ab + 1] = first[4 : 4 + ins, :chan]
        one_ref[3 * ab + 2] = second[0:ins, :chan]
    bias_one_ref[...] = piece(1, 4)[4:5, :chan]
    bias_two_ref[...] = piece(1, 8)[4:5, :chan]


def volume_body(nx, ny, one_ref, edge_ref, w_ref, out_ref, shifted):
    edges = edge_ref[...].astype(BF16)
    for wide in range(nx + 2):
        for tall in range(ny + 2):
            at = slice(tall * LANES, (tall + 1) * LANES)
            block = one_ref[wide, :, at]
            before, after = z_shifts(block, edges, wide * (ny + 2) + tall)
            shifted[0, wide, :, at] = after
            shifted[1, wide, :, at] = before
    weights = w_ref[...]
    ins = out_ref.shape[0]
    for x in range(nx):
        rows = []
        for a in range(3):
            for b in range(3):
                at = slice((2 - b) * LANES, (2 - b + ny) * LANES)
                rows += [shifted[0, x + 2 - a, :, at], one_ref[x + 2 - a, :, at], shifted[1, x + 2 - a, :, at]]
        grad = jnp.dot(weights, jnp.concatenate(rows, 0), preferred_element_type=F32)
        stack = jnp.stack([grad[:8, y * LANES : (y + 1) * LANES] for y in range(ny)], 0)
        out_ref[:, x] = jnp.swapaxes(stack, 0, 1)[:ins]


def ring(axis, step):
    count = lax.axis_size(axis)
    return [(i, (i + step) % count) for i in range(count)]


def swap_edges(edges):
    if lax.axis_size("gz") == 2:
        return lax.ppermute(edges, "gz", ring("gz", 1))
    before = lax.ppermute(edges, "gz", ring("gz", 1))
    after = lax.ppermute(edges, "gz", ring("gz", -1))
    even = lax.broadcasted_iota(jnp.int32, edges.shape, 1) % 2 == 0
    return jnp.where(even, before, after)


def exchange(total, axis, step, cross):
    count = lax.axis_size(axis)
    if axis == "gx":
        return lax.ppermute(total, "gx", [(i, i ^ step ^ cross) for i in range(count)])
    pairs = [
        (i * count + k, (i ^ cross) * count + (k ^ step))
        for i in range(lax.axis_size("gx"))
        for k in range(count)
    ]
    return lax.ppermute(total, ("gx", axis), pairs)


def doublings(axis, first=1):
    step = first
    while step < lax.axis_size(axis):
        yield step
        step *= 2


def near(array):
    return pltpu.with_memory_space_constraint(array, pltpu.VMEM)


def call(body, out_shape, scratch, flops, *args):
    many = isinstance(out_shape, (tuple, list))
    spec = pl.BlockSpec(memory_space=pltpu.VMEM)
    return pl.pallas_call(
        body,
        out_shape=out_shape,
        in_specs=[
            pl.BlockSpec(memory_space=pltpu.SMEM) if arg.dtype == jnp.int32 else spec for arg in args
        ],
        out_specs=[spec] * len(out_shape) if many else spec,
        scratch_shapes=scratch,
        cost_estimate=pl.CostEstimate(flops=flops, bytes_accessed=1 << 18, transcendentals=0),
    )(*args)


def local(volume, act_one, act_two, weight_one, weight_two, cotangent):
    chan, nx, ny, nz = act_one.shape
    ins = volume.shape[0]
    cells = nx * ny * nz
    for axis in AXES:
        cells *= lax.axis_size(axis)
    norm = 1.0 / math.sqrt(cells)
    flat_two = jnp.transpose(weight_two, (1, 2, 3, 4, 0)).reshape(chan, 27 * chan)
    flat_one = jnp.transpose(weight_one, (1, 2, 3, 4, 0)).reshape(ins, 27 * chan)
    flat_one = jnp.pad(flat_one, ((0, chan - ins), (0, 0)))
    blocks = pltpu.VMEM((nx * ny, chan, LANES), BF16)
    edge = pltpu.VMEM((chan, LANES), BF16)
    flat_two = near(flat_two)
    flat_one = near(flat_one)

    delta, edges, vols = call(
        lambda *refs: prep_body(nx, ny, *refs),
        (blocks, edge, pltpu.VMEM((nx, ny, 8, LANES), F32)),
        [],
        1 << 20,
        cotangent, act_two, volume,
    )
    edges, act_one = lax.optimization_barrier((edges, act_one))
    across = lax.axis_size("gx")
    even = (lax.axis_index("gx") % 2 == 0).astype(jnp.int32).reshape(1)
    act, face = call(
        lambda *refs: act_body(nx, ny, *refs),
        (blocks, pltpu.VMEM((ny, chan, LANES), BF16)),
        [],
        1 << 24,
        even, act_one,
    )
    edges = near(swap_edges(edges))
    delta, act = near(delta), near(act)
    side = pltpu.VMEM((3 * nx + 1, chan, LANES), BF16)
    low, high = call(
        lambda *refs: pack_y_body(nx, ny, *refs), (side, side), [], 1 << 20, delta, act, edges
    )
    crossing = [(i, (i + i % 2 * 2 - 1) % across) for i in range(across)]
    low, high, face = lax.optimization_barrier((low, high, face))
    down = lax.ppermute(low, "gy", ring("gy", -1))
    up = lax.ppermute(high, "gy", ring("gy", 1))
    face = lax.ppermute(face, "gx", crossing)
    up, down, face = lax.optimization_barrier((up, down, face))
    up, down, face = near(up), near(down), near(face)
    near_side, cross_side, merged = call(
        lambda *refs: pack_x_body(nx, ny, *refs),
        (
            pltpu.VMEM((3 * (ny + 4) - 1, chan, LANES), BF16),
            pltpu.VMEM((2 * (ny + 4) + 3, chan, LANES), BF16),
            edge,
        ),
        [],
        1 << 20,
        even, delta, act, edges, up, down,
    )
    cross_side = near(lax.ppermute(cross_side, "gx", crossing))
    near_side = near(lax.ppermute(near_side, "gx", [(i, i ^ 1) for i in range(across)]))
    span = (ny + 2) * LANES
    own, inner, inner_edges, inner_two, vols, part, inner_one = call(
        lambda *refs: inner_body(nx, ny, *refs),
        (
            pltpu.VMEM((3, nx, chan, (ny + 4) * LANES), BF16),
            pltpu.VMEM((nx - 2, chan, span), BF16),
            pltpu.VMEM((chan, LANES), F32),
            pltpu.VMEM((27 * chan, chan), F32),
            pltpu.VMEM((nx, 32, ny * LANES), BF16),
            pltpu.VMEM((4, chan, span), F32),
            pltpu.VMEM((96, 4 * chan), F32),
        ),
        [],
        1 << 27,
        delta, act, edges, near(merged), up, down, near(vols), flat_two,
    )
    slots = 27 * chan // 8
    rows = -(-slots // (LANES // chan)) * 8 + 16
    sums, one, one_edges = call(
        lambda *refs: outer_body(nx, ny, *refs),
        (
            pltpu.VMEM((rows, LANES), F32),
            pltpu.VMEM((nx + 2, chan, span), BF16),
            pltpu.VMEM((chan, LANES), F32),
        ),
        [
            pltpu.VMEM((3, 4, chan, (ny + 4) * LANES), BF16),
            pltpu.VMEM((27 * chan, LANES), F32),
        ],
        1 << 28,
        even, act, up, down, near_side, cross_side, face, flat_two,
        near(own), near(inner), near(inner_edges), near(inner_two), near(vols), near(part), near(inner_one),
    )
    if lax.axis_size("gz") == 2:
        moved = exchange(jnp.concatenate([sums, one_edges], 0), "gx", 1, 0)
        sums = sums + moved[:rows]
        moved = exchange(jnp.concatenate([sums, moved[rows:]], 0), "gz", 1, 1)
        sums = sums + moved[:rows]
        one_edges = moved[rows:]
    else:
        one_edges = swap_edges(one_edges)
        sums = sums + exchange(sums, "gx", 1, 0)
        for step in doublings("gz"):
            sums = sums + exchange(sums, "gz", step, 1)
    for step in doublings("gx", 2):
        sums = sums + exchange(sums, "gx", step, 1)
    grad_volume = call(
        lambda *refs: volume_body(nx, ny, *refs),
        jax.ShapeDtypeStruct(volume.shape, F32),
        [pltpu.VMEM((2, nx + 2, chan, span), BF16)],
        1 << 27,
        near(one), near(one_edges), flat_one,
    )
    sums, grad_volume = lax.optimization_barrier((sums, grad_volume))
    for step in doublings("gy"):
        sums = sums + exchange(sums, "gy", step, 1)
    sums = near(sums)
    grad_one, bias_one, grad_two, bias_two = call(
        lambda *refs: unpack_body(norm, *refs),
        (
            jax.ShapeDtypeStruct((27, ins, chan), F32),
            jax.ShapeDtypeStruct((1, chan), F32),
            jax.ShapeDtypeStruct((27, chan, chan), F32),
            jax.ShapeDtypeStruct((1, chan), F32),
        ),
        [],
        1 << 20,
        sums,
    )
    grad_one = jnp.transpose(grad_one.reshape(3, 3, 3, ins, chan), (4, 3, 0, 1, 2))
    grad_two = jnp.transpose(grad_two.reshape(3, 3, 3, chan, chan), (3, 4, 0, 1, 2))
    return (grad_one, bias_one.reshape(chan), grad_two, bias_two.reshape(chan), grad_volume)


def solution(mesh):
    placed = P(None, *AXES)
    return jax.shard_map(
        local,
        mesh=mesh,
        in_specs=(placed, placed, placed, P(), P(), placed),
        out_specs=(P(), P(), P(), P(), placed),
        check_vma=False,
    )
```

```python
import math

import jax
import jax.numpy as jnp
from jax import lax
from jax.experimental import pallas as pl
from jax.experimental.pallas import tpu as pltpu
from jax.sharding import PartitionSpec as P


AXES = ("gx", "gy", "gz")
F32 = jnp.float32
BF16 = jnp.bfloat16
LANES = 128


def lane_ids(rows):
    return lax.broadcasted_iota(jnp.int32, (rows, LANES), 1)


def slope(saved):
    return jnp.where(saved > 0, 1.0, 0.3).astype(F32)


def put_edges(packed, block, spot):
    lane = lane_ids(block.shape[0])
    moved = pltpu.roll(block, (2 * spot + 1) % LANES, 1)
    return jnp.where((lane == 2 * spot) | (lane == 2 * spot + 1), moved, packed)


def z_shifts(block, edges, spot):
    lane = lane_ids(block.shape[0])
    near = pltpu.roll(edges, (LANES - 2 * spot - 1) % LANES, 1)
    after = pltpu.roll(jnp.where(lane == 0, near, block), LANES - 1, 1)
    before = pltpu.roll(jnp.where(lane == LANES - 1, near, block), 1, 1)
    return before, after


def prep_body(nx, ny, cot_ref, act_two_ref, vol_ref, delta_ref, edge_ref, rows_ref):
    chan = cot_ref.shape[0]
    edges = jnp.zeros((chan, LANES), F32)
    vol_edges = jnp.zeros((8, LANES), F32)
    for x in range(nx):
        delta = cot_ref[:, x].astype(F32) * slope(act_two_ref[:, x].astype(F32))
        delta = jnp.swapaxes(delta, 0, 1)
        for y in range(ny):
            spot = x * ny + y
            delta_ref[spot] = delta[y].astype(BF16)
            edges = put_edges(edges, delta[y], spot)
        vol = vol_rows(vol_ref, x)
        for y in range(ny):
            rows_ref[x, y] = vol[y]
            vol_edges = put_edges(vol_edges, vol[y], nx * ny + x * ny + y)
    vol_edges = jnp.concatenate([vol_edges] * (chan // 8), 0)
    half = lane_ids(chan) < 2 * nx * ny
    edge_ref[...] = jnp.where(half, edges, vol_edges).astype(BF16)


def act_body(nx, ny, even_ref, act_one_ref, act_ref, face_ref):
    for x in range(nx):
        act = jnp.swapaxes(act_one_ref[:, x].astype(F32), 0, 1)
        for y in range(ny):
            act_ref[x * ny + y] = act[y].astype(BF16)

    @pl.when(even_ref[0] == 1)
    def _():
        for y in range(ny):
            face_ref[y] = act_ref[y]

    @pl.when(even_ref[0] == 0)
    def _():
        for y in range(ny):
            face_ref[y] = act_ref[(nx - 1) * ny + y]


def vol_rows(vol_ref, x):
    vol = vol_ref[:, x].astype(F32)
    rest = jnp.ones((8 - vol.shape[0],) + vol.shape[1:], F32)
    return jnp.swapaxes(jnp.concatenate([vol, rest], 0), 0, 1)


def pack_y_body(nx, ny, delta_ref, act_ref, edge_ref, low_ref, high_ref):
    for x in range(nx):
        for k in range(2):
            low_ref[2 * x + k] = delta_ref[x * ny + k]
            high_ref[2 * x + k] = delta_ref[x * ny + ny - 2 + k]
        low_ref[2 * nx + x] = act_ref[x * ny]
        high_ref[2 * nx + x] = act_ref[x * ny + ny - 1]
    low_ref[3 * nx] = edge_ref[...]
    high_ref[3 * nx] = edge_ref[...]


def tall_delta(ny, delta_ref, up_ref, down_ref, x, tall):
    if tall < 2:
        return up_ref[2 * x + tall]
    if tall < ny + 2:
        return delta_ref[x * ny + tall - 2]
    return down_ref[2 * x + tall - ny - 2]


def tall_act(nx, ny, act_ref, up_ref, down_ref, x, tall):
    if tall == 0:
        return up_ref[2 * nx + x]
    if tall == ny + 1:
        return down_ref[2 * nx + x]
    return act_ref[x * ny + tall - 1]


def tall_spot(nx, ny, x, tall):
    if tall < 2:
        return nx * ny + x * ny + ny - 2 + tall
    if tall < ny + 2:
        return x * ny + tall - 2
    return nx * ny + x * ny + tall - ny - 2


def pack_x_body(
    nx, ny, even_ref, delta_ref, act_ref, edge_ref, up_ref, down_ref, near_ref, cross_ref, merged_ref
):
    lane = lane_ids(edge_ref.shape[0])
    half = 2 * nx * ny
    up = pltpu.roll(up_ref[3 * nx], half, 1)
    down = pltpu.roll(down_ref[3 * nx], half, 1)
    beyond = jnp.where(lax.rem(lane, 2 * ny) < ny, down, up)
    merged = jnp.where(lane < half, edge_ref[...], beyond)
    merged_ref[...] = merged

    def fill(ref, planes, act_plane, rows):
        for k in range(2):
            for tall in range(ny + 4):
                ref[k * (ny + 4) + tall] = tall_delta(ny, delta_ref, up_ref, down_ref, planes[k], tall)
        base = 2 * (ny + 4)
        for k, tall in enumerate(rows):
            ref[base + k] = tall_act(nx, ny, act_ref, up_ref, down_ref, act_plane, tall)
        ref[base + len(rows)] = merged

    low, high = ((0, 1), 0), ((nx - 2, nx - 1), nx - 1)
    every, ends = list(range(ny + 2)), [0, ny + 1]

    @pl.when(even_ref[0] == 1)
    def _():
        fill(cross_ref, *low, ends)
        fill(near_ref, *high, every)

    @pl.when(even_ref[0] == 0)
    def _():
        fill(cross_ref, *high, ends)
        fill(near_ref, *low, every)


def store_shifts(shifted, plane, tall, block, edges, spot):
    before, after = z_shifts(block, edges, spot)
    at = slice(tall * LANES, (tall + 1) * LANES)
    shifted[0, plane, :, at] = after
    shifted[1, plane, :, at] = block
    shifted[2, plane, :, at] = before


def tap_rows(ny, plane_at, wide, taps):
    span = (ny + 2) * LANES
    return jnp.concatenate(
        [
            plane_at(c, wide + 2 - a, slice((2 - b) * LANES, (2 - b) * LANES + span))
            for a in taps
            for b in range(3)
            for c in range(3)
        ],
        0,
    )


def tap_back(w_ref, rows, taps):
    per = w_ref.shape[1] // 3
    return jnp.dot(
        w_ref[:, per * taps[0] : per * (taps[-1] + 1)], rows, preferred_element_type=F32
    )


def add_two(ny, totals, rows, acts, taps):
    inner = slice(LANES, (ny + 1) * LANES)
    term = lax.dot_general(
        rows[:, inner], acts[:, inner], (((1,), (1,)), ((), ())), preferred_element_type=F32
    )
    per = rows.shape[0] // len(taps)
    for k, a in enumerate(taps):
        totals[a] = add(totals[a], term[k * per : (k + 1) * per])


def finish_plane(ny, back, acts, wide, one_edges):
    delta = back * slope(acts.astype(F32))
    for tall in range(ny + 2):
        one_edges = put_edges(
            one_edges, delta[:, tall * LANES : (tall + 1) * LANES], wide * (ny + 2) + tall
        )
    return delta.astype(BF16), one_edges


def add_one(nx, ny, totals, one, wide, vol_ref, delta_plane):
    taps = [a for a in range(3) if 0 <= wide - 2 + a < nx]
    rhs = [one[:, (2 - b) * LANES : (2 - b + ny) * LANES] for b in range(3)]
    if delta_plane is not None:
        rhs.append(delta_plane)
    rhs = jnp.concatenate(rhs, 0)
    lhs = jnp.concatenate([vol_ref[wide - 2 + a] for a in taps], 0)
    term = lax.dot_general(lhs, rhs, (((1,), (1,)), ((), ())), preferred_element_type=F32)
    if delta_plane is None:
        term = jnp.concatenate([term, jnp.zeros((term.shape[0], one.shape[0]), F32)], 1)
    per = lhs.shape[0] // len(taps)
    for k, a in enumerate(taps):
        totals[a] = add(totals[a], term[k * per : (k + 1) * per])


def own_taps(nx, wide):
    return [a for a in range(3) if 2 <= wide + 2 - a <= nx + 1]


def add(total, term):
    return term if total is None else total + term


def inner_body(
    nx, ny, delta_ref, act_ref, edge_ref, merged_ref, up_ref, down_ref, vol_ref, w_ref,
    shifted, one_ref, one_edge_ref, two_ref, vol_out_ref, part_ref, first_ref,
):
    chan = edge_ref.shape[0]
    merged = merged_ref[...]
    for x in range(nx):
        for tall in range(ny + 4):
            block = tall_delta(ny, delta_ref, up_ref, down_ref, x, tall)
            store_shifts(shifted, x, tall, block, merged, tall_spot(nx, ny, x, tall))
    one_edges = jnp.zeros((chan, LANES), F32)
    totals = [None] * 3
    for wide in range(nx + 2):
        taps = own_taps(nx, wide)
        rows = tap_rows(ny, lambda c, plane, at: shifted[c, plane - 2, :, at], wide, taps)
        back = tap_back(w_ref, rows, taps)
        if 1 <= wide <= nx:
            acts = jnp.concatenate(
                [tall_act(nx, ny, act_ref, up_ref, down_ref, wide - 1, tall) for tall in range(ny + 2)], 1
            )
            add_two(ny, totals, rows, acts, taps)
        if 2 <= wide < nx:
            one_ref[wide - 2], one_edges = finish_plane(ny, back, acts, wide, one_edges)
        else:
            part_ref[wide if wide < 2 else wide - nx + 2] = back
    total = jnp.concatenate(totals, 0)
    one_edge_ref[...] = one_edges
    two_ref[...] = total
    edges = edge_ref[0:8].astype(F32)
    for x in range(nx):
        vol = vol_ref[x]
        shifts = [[], [], []]
        for y in range(ny):
            before, after = z_shifts(vol[y], edges, nx * ny + x * ny + y)
            shifts[0].append(before)
            shifts[1].append(vol[y])
            shifts[2].append(after)
        lhs = [jnp.concatenate(row, 1) for row in shifts] + [jnp.zeros((8, ny * LANES), F32)]
        vol_out_ref[x] = jnp.concatenate(lhs, 0).astype(BF16)
    totals = [None] * 3
    middle = slice(2 * LANES, (ny + 2) * LANES)
    for wide in range(2, nx):
        add_one(nx, ny, totals, one_ref[wide - 2], wide, vol_out_ref, shifted[1, wide - 1, :, middle])
    first_ref[...] = jnp.concatenate(totals, 0)


def outer_body(
    nx, ny, even_ref, act_ref, up_ref, down_ref, near_ref, cross_ref, face_ref, w_ref,
    own_ref, inner_ref, inner_edge_ref, two_ref, vol_ref, part_ref, first_ref,
    sums_ref, one_ref, one_edge_ref, far, grad_two,
):
    chan = act_ref.shape[1]
    base = 2 * (ny + 4)
    even = jnp.broadcast_to(even_ref[0], (chan, LANES)) == 1

    def choose(side, near, cross):
        return jnp.where(even, near, cross) if side else jnp.where(even, cross, near)

    def act_beside(side, tall):
        if tall == 0:
            cross = cross_ref[base]
        elif tall == ny + 1:
            cross = cross_ref[base + 1]
        else:
            cross = face_ref[tall - 1]
        return choose(side, near_ref[base + tall], cross)

    for side in range(2):
        edges = choose(side, near_ref[base + ny + 2], cross_ref[base + 2])
        for k in range(2):
            for tall in range(ny + 4):
                from_x = nx - 2 + k if side == 0 else k
                at = k * (ny + 4) + tall
                block = choose(side, near_ref[at], cross_ref[at])
                store_shifts(far, 2 * side + k, tall, block, edges, tall_spot(nx, ny, from_x, tall))

    def plane_at(c, wide, at):
        if wide < 2:
            return far[c, wide, :, at]
        if wide < nx + 2:
            return own_ref[c, wide - 2, :, at]
        return far[c, wide - nx, :, at]

    one_edges = inner_edge_ref[...]
    totals = [None] * 3
    for wide in (0, 1, nx, nx + 1):
        if wide == 0:
            blocks = [act_beside(0, tall) for tall in range(ny + 2)]
        elif wide == nx + 1:
            blocks = [act_beside(1, tall) for tall in range(ny + 2)]
        else:
            blocks = [
                tall_act(nx, ny, act_ref, up_ref, down_ref, wide - 1, tall) for tall in range(ny + 2)
            ]
        acts = jnp.concatenate(blocks, 1)
        taps = [a for a in range(3) if a not in own_taps(nx, wide)]
        rows = tap_rows(ny, plane_at, wide, taps)
        back = part_ref[wide if wide < 2 else wide - nx + 2] + tap_back(w_ref, rows, taps)
        if 1 <= wide <= nx:
            add_two(ny, totals, rows, acts, taps)
        one_ref[wide], one_edges = finish_plane(ny, back, acts, wide, one_edges)
    third = 9 * chan
    for a in range(3):
        part = slice(third * a, third * (a + 1))
        grad_two[part, 0:chan] = two_ref[part, :] if totals[a] is None else two_ref[part, :] + totals[a]
    for x in range(1, nx - 1):
        one_ref[x + 1] = inner_ref[x - 1]
    one_edge_ref[...] = one_edges.astype(BF16).astype(F32)

    per = first_ref.shape[0] // 3
    totals = [first_ref[per * a : per * (a + 1), :] for a in range(3)]
    middle = slice(2 * LANES, (ny + 2) * LANES)
    for wide in (0, 1, nx, nx + 1):
        plane = own_ref[1, wide - 1, :, middle] if 1 <= wide <= nx else None
        add_one(nx, ny, totals, one_ref[wide], wide, vol_ref, plane)
    total_one = jnp.concatenate(
        [total[:, : 3 * chan] for total in totals] + [totals[1][:, 3 * chan :]], 1
    )

    lane = lane_ids(8)
    slots = grad_two.shape[0] // 8
    per = LANES // chan
    groups = -(-slots // per)
    tail = jnp.zeros((8, 2 * LANES - total_one.shape[1]), F32)
    tiles = [jnp.concatenate([total_one[8 * c : 8 * c + 8], tail], 1) for c in range(3)]
    head = lax.broadcasted_iota(jnp.int32, (8, 2 * LANES), 0) < 4
    first = jnp.where(head, tiles[0], pltpu.roll(tiles[1], 4, 0))
    second = jnp.where(head, tiles[2], tiles[1])
    sums_ref[groups * 8 : groups * 8 + 8, :] = first[:, :LANES]
    sums_ref[groups * 8 + 8 : groups * 8 + 16, :] = second[:, :LANES]
    rest = second[:, LANES:]
    rest = jnp.where(head[:, :LANES], rest, pltpu.roll(rest, LANES - chan, 1))
    spare = {slots: first[:, LANES:], slots + 1: rest}
    for group in range(groups):
        packed = jnp.zeros((8, LANES), F32)
        for s in range(per):
            slot = group * per + s
            if slot < slots:
                moved = grad_two[slot * 8 : slot * 8 + 8, :]
            else:
                moved = spare[slot]
            if s:
                moved = pltpu.roll(moved, chan * s, 1)
            packed = jnp.where((lane >= chan * s) & (lane < chan * (s + 1)), moved, packed)
        sums_ref[group * 8 : group * 8 + 8, :] = packed


def unpack_body(norm, sums_ref, one_ref, bias_one_ref, two_ref, bias_two_ref):
    chan = two_ref.shape[2]
    per = LANES // chan
    slots = 2 * two_ref.shape[0]
    for slot in range(slots):
        group, s = divmod(slot, per)
        block = sums_ref[group * 8 : group * 8 + 8, :] * norm
        if s:
            block = pltpu.roll(block, LANES - chan * s, 1)
        two_ref[slot // 2, (slot % 2) * 8 : (slot % 2) * 8 + 8, :] = block[:, :chan]
    base = slots // per * 8

    def piece(k, index):
        if index < per:
            block, s = sums_ref[base + 8 * (k + 1) : base + 8 * (k + 2), :], index
        else:
            block, s = sums_ref[base : base + 8, :], slots % per + k
        return (pltpu.roll(block, LANES - chan * s, 1) if s else block) * norm

    ins = one_ref.shape[1]
    for ab in range(9):
        first = piece(0, ab)
        second = piece(1, ab)
        one_ref[3 * ab] = first[0:ins, :chan]
        one_ref[3 * ab + 1] = first[4 : 4 + ins, :chan]
        one_ref[3 * ab + 2] = second[0:ins, :chan]
    bias_one_ref[...] = piece(1, 4)[4:5, :chan]
    bias_two_ref[...] = piece(1, 8)[4:5, :chan]


def volume_body(nx, ny, one_ref, edge_ref, w_ref, out_ref, shifted):
    edges = edge_ref[...].astype(BF16)
    for wide in range(nx + 2):
        for tall in range(ny + 2):
            at = slice(tall * LANES, (tall + 1) * LANES)
            block = one_ref[wide, :, at]
            before, after = z_shifts(block, edges, wide * (ny + 2) + tall)
            shifted[0, wide, :, at] = after
            shifted[1, wide, :, at] = before
    weights = w_ref[...]
    ins = out_ref.shape[0]
    for x in range(nx):
        rows = []
        for a in range(3):
            for b in range(3):
                at = slice((2 - b) * LANES, (2 - b + ny) * LANES)
                rows += [shifted[0, x + 2 - a, :, at], one_ref[x + 2 - a, :, at], shifted[1, x + 2 - a, :, at]]
        grad = jnp.dot(weights, jnp.concatenate(rows, 0), preferred_element_type=F32)
        stack = jnp.stack([grad[:8, y * LANES : (y + 1) * LANES] for y in range(ny)], 0)
        out_ref[:, x] = jnp.swapaxes(stack, 0, 1)[:ins]


def ring(axis, step):
    count = lax.axis_size(axis)
    return [(i, (i + step) % count) for i in range(count)]


def swap_edges(edges):
    if lax.axis_size("gz") == 2:
        return lax.ppermute(edges, "gz", ring("gz", 1))
    before = lax.ppermute(edges, "gz", ring("gz", 1))
    after = lax.ppermute(edges, "gz", ring("gz", -1))
    even = lax.broadcasted_iota(jnp.int32, edges.shape, 1) % 2 == 0
    return jnp.where(even, before, after)


def exchange(total, axis, step, cross):
    count = lax.axis_size(axis)
    if axis == "gx":
        return lax.ppermute(total, "gx", [(i, i ^ step ^ cross) for i in range(count)])
    pairs = [
        (i * count + k, (i ^ cross) * count + (k ^ step))
        for i in range(lax.axis_size("gx"))
        for k in range(count)
    ]
    return lax.ppermute(total, ("gx", axis), pairs)


def doublings(axis, first=1):
    step = first
    while step < lax.axis_size(axis):
        yield step
        step *= 2


def near(array):
    return pltpu.with_memory_space_constraint(array, pltpu.VMEM)


def call(body, out_shape, scratch, flops, *args):
    many = isinstance(out_shape, (tuple, list))
    spec = pl.BlockSpec(memory_space=pltpu.VMEM)
    return pl.pallas_call(
        body,
        out_shape=out_shape,
        in_specs=[
            pl.BlockSpec(memory_space=pltpu.SMEM) if arg.dtype == jnp.int32 else spec for arg in args
        ],
        out_specs=[spec] * len(out_shape) if many else spec,
        scratch_shapes=scratch,
        cost_estimate=pl.CostEstimate(flops=flops, bytes_accessed=1 << 18, transcendentals=0),
    )(*args)


def compute(volume, act_one, act_two, weight_one, weight_two, cotangent):
    chan, nx, ny, nz = act_one.shape
    ins = volume.shape[0]
    cells = nx * ny * nz
    for axis in AXES:
        cells *= lax.axis_size(axis)
    norm = 1.0 / math.sqrt(cells)
    flat_two = jnp.transpose(weight_two, (1, 2, 3, 4, 0)).reshape(chan, 27 * chan)
    flat_one = jnp.transpose(weight_one, (1, 2, 3, 4, 0)).reshape(ins, 27 * chan)
    flat_one = jnp.pad(flat_one, ((0, chan - ins), (0, 0)))
    blocks = pltpu.VMEM((nx * ny, chan, LANES), BF16)
    edge = pltpu.VMEM((chan, LANES), BF16)
    flat_two = near(flat_two)
    flat_one = near(flat_one)

    delta, edges, vols = call(
        lambda *refs: prep_body(nx, ny, *refs),
        (blocks, edge, pltpu.VMEM((nx, ny, 8, LANES), F32)),
        [],
        1 << 20,
        cotangent, act_two, volume,
    )
    edges, act_one = lax.optimization_barrier((edges, act_one))
    across = lax.axis_size("gx")
    even = (lax.axis_index("gx") % 2 == 0).astype(jnp.int32).reshape(1)
    act, face = call(
        lambda *refs: act_body(nx, ny, *refs),
        (blocks, pltpu.VMEM((ny, chan, LANES), BF16)),
        [],
        1 << 24,
        even, act_one,
    )
    edges = near(swap_edges(edges))
    delta, act = near(delta), near(act)
    side = pltpu.VMEM((3 * nx + 1, chan, LANES), BF16)
    low, high = call(
        lambda *refs: pack_y_body(nx, ny, *refs), (side, side), [], 1 << 20, delta, act, edges
    )
    crossing = [(i, (i + i % 2 * 2 - 1) % across) for i in range(across)]
    low, high, face = lax.optimization_barrier((low, high, face))
    down = lax.ppermute(low, "gy", ring("gy", -1))
    up = lax.ppermute(high, "gy", ring("gy", 1))
    face = lax.ppermute(face, "gx", crossing)
    up, down, face = near(up), near(down), near(face)
    near_side, cross_side, merged = call(
        lambda *refs: pack_x_body(nx, ny, *refs),
        (
            pltpu.VMEM((3 * (ny + 4) - 1, chan, LANES), BF16),
            pltpu.VMEM((2 * (ny + 4) + 3, chan, LANES), BF16),
            edge,
        ),
        [],
        1 << 20,
        even, delta, act, edges, up, down,
    )
    cross_side = near(lax.ppermute(cross_side, "gx", crossing))
    near_side = near(lax.ppermute(near_side, "gx", [(i, i ^ 1) for i in range(across)]))
    span = (ny + 2) * LANES
    own, inner, inner_edges, inner_two, vols, part, inner_one = call(
        lambda *refs: inner_body(nx, ny, *refs),
        (
            pltpu.VMEM((3, nx, chan, (ny + 4) * LANES), BF16),
            pltpu.VMEM((nx - 2, chan, span), BF16),
            pltpu.VMEM((chan, LANES), F32),
            pltpu.VMEM((27 * chan, chan), F32),
            pltpu.VMEM((nx, 32, ny * LANES), BF16),
            pltpu.VMEM((4, chan, span), F32),
            pltpu.VMEM((96, 4 * chan), F32),
        ),
        [],
        1 << 27,
        delta, act, edges, near(merged), up, down, near(vols), flat_two,
    )
    slots = 27 * chan // 8
    rows = -(-slots // (LANES // chan)) * 8 + 16
    sums, one, one_edges = call(
        lambda *refs: outer_body(nx, ny, *refs),
        (
            pltpu.VMEM((rows, LANES), F32),
            pltpu.VMEM((nx + 2, chan, span), BF16),
            pltpu.VMEM((chan, LANES), F32),
        ),
        [
            pltpu.VMEM((3, 4, chan, (ny + 4) * LANES), BF16),
            pltpu.VMEM((27 * chan, LANES), F32),
        ],
        1 << 28,
        even, act, up, down, near_side, cross_side, face, flat_two,
        near(own), near(inner), near(inner_edges), near(inner_two), near(vols), near(part), near(inner_one),
    )
    if lax.axis_size("gz") == 2:
        moved = exchange(jnp.concatenate([sums, one_edges], 0), "gx", 1, 0)
        sums = sums + moved[:rows]
        moved = exchange(jnp.concatenate([sums, moved[rows:]], 0), "gz", 1, 1)
        sums = sums + moved[:rows]
        one_edges = moved[rows:]
    else:
        one_edges = swap_edges(one_edges)
        sums = sums + exchange(sums, "gx", 1, 0)
        for step in doublings("gz"):
            sums = sums + exchange(sums, "gz", step, 1)
    for step in doublings("gx", 2):
        sums = sums + exchange(sums, "gx", step, 1)
    grad_volume = call(
        lambda *refs: volume_body(nx, ny, *refs),
        jax.ShapeDtypeStruct(volume.shape, F32),
        [pltpu.VMEM((2, nx + 2, chan, span), BF16)],
        1 << 27,
        near(one), near(one_edges), flat_one,
    )
    sums, grad_volume = lax.optimization_barrier((sums, grad_volume))
    for step in doublings("gy"):
        sums = sums + exchange(sums, "gy", step, 1)
    sums = near(sums)
    grad_one, bias_one, grad_two, bias_two = call(
        lambda *refs: unpack_body(norm, *refs),
        (
            jax.ShapeDtypeStruct((27, ins, chan), F32),
            jax.ShapeDtypeStruct((1, chan), F32),
            jax.ShapeDtypeStruct((27, chan, chan), F32),
            jax.ShapeDtypeStruct((1, chan), F32),
        ),
        [],
        1 << 20,
        sums,
    )
    grad_one = jnp.transpose(grad_one.reshape(3, 3, 3, ins, chan), (4, 3, 0, 1, 2))
    grad_two = jnp.transpose(grad_two.reshape(3, 3, 3, chan, chan), (3, 4, 0, 1, 2))
    return (grad_one, bias_one.reshape(chan), grad_two, bias_two.reshape(chan), grad_volume)


def solution(mesh):
    placed = P(None, *AXES)
    return jax.shard_map(
        compute,
        mesh=mesh,
        in_specs=(placed, placed, placed, P(), P(), placed),
        out_specs=(P(), P(), P(), P(), placed),
        check_vma=False,
    )
```

```python
import math

import jax
import jax.numpy as jnp
from jax import lax
from jax.experimental import pallas as pl
from jax.experimental.pallas import tpu as pltpu
from jax.sharding import PartitionSpec as P


AXES = ("gx", "gy", "gz")
F32 = jnp.float32
BF16 = jnp.bfloat16
LANES = 128


def lane_ids(rows):
    return lax.broadcasted_iota(jnp.int32, (rows, LANES), 1)


def slope(saved):
    return jnp.where(saved > 0, 1.0, 0.3).astype(F32)


def put_edges(packed, block, spot):
    lane = lane_ids(block.shape[0])
    moved = pltpu.roll(block, (2 * spot + 1) % LANES, 1)
    return jnp.where((lane == 2 * spot) | (lane == 2 * spot + 1), moved, packed)


def z_shifts(block, edges, spot):
    lane = lane_ids(block.shape[0])
    near = pltpu.roll(edges, (LANES - 2 * spot - 1) % LANES, 1)
    after = pltpu.roll(jnp.where(lane == 0, near, block), LANES - 1, 1)
    before = pltpu.roll(jnp.where(lane == LANES - 1, near, block), 1, 1)
    return before, after


def prep_body(nx, ny, cot_ref, act_two_ref, vol_ref, delta_ref, edge_ref, rows_ref):
    chan = cot_ref.shape[0]
    edges = jnp.zeros((chan, LANES), F32)
    vol_edges = jnp.zeros((8, LANES), F32)
    for x in range(nx):
        delta = cot_ref[:, x].astype(F32) * slope(act_two_ref[:, x].astype(F32))
        delta = jnp.swapaxes(delta, 0, 1)
        for y in range(ny):
            spot = x * ny + y
            delta_ref[spot] = delta[y].astype(BF16)
            edges = put_edges(edges, delta[y], spot)
        vol = vol_rows(vol_ref, x)
        for y in range(ny):
            rows_ref[x, y] = vol[y]
            vol_edges = put_edges(vol_edges, vol[y], nx * ny + x * ny + y)
    vol_edges = jnp.concatenate([vol_edges] * (chan // 8), 0)
    half = lane_ids(chan) < 2 * nx * ny
    edge_ref[...] = jnp.where(half, edges, vol_edges).astype(BF16)


def act_body(nx, ny, even_ref, act_one_ref, delta_ref, act_ref, face_ref):
    for x in range(nx):
        act = jnp.swapaxes(act_one_ref[:, x].astype(F32), 0, 1)
        for y in range(ny):
            act_ref[x * ny + y] = act[y].astype(BF16)

    def fill(planes, act_plane):
        for y in range(ny):
            for k in range(2):
                face_ref[k * ny + y] = delta_ref[planes[k] * ny + y]
            face_ref[2 * ny + y] = act_ref[act_plane * ny + y]

    @pl.when(even_ref[0] == 1)
    def _():
        fill((0, 1), 0)

    @pl.when(even_ref[0] == 0)
    def _():
        fill((nx - 2, nx - 1), nx - 1)


def vol_rows(vol_ref, x):
    vol = vol_ref[:, x].astype(F32)
    rest = jnp.ones((8 - vol.shape[0],) + vol.shape[1:], F32)
    return jnp.swapaxes(jnp.concatenate([vol, rest], 0), 0, 1)


def pack_y_body(nx, ny, delta_ref, act_ref, edge_ref, low_ref, high_ref):
    for x in range(nx):
        for k in range(2):
            low_ref[2 * x + k] = delta_ref[x * ny + k]
            high_ref[2 * x + k] = delta_ref[x * ny + ny - 2 + k]
        low_ref[2 * nx + x] = act_ref[x * ny]
        high_ref[2 * nx + x] = act_ref[x * ny + ny - 1]
    low_ref[3 * nx] = edge_ref[...]
    high_ref[3 * nx] = edge_ref[...]


def tall_delta(ny, delta_ref, up_ref, down_ref, x, tall):
    if tall < 2:
        return up_ref[2 * x + tall]
    if tall < ny + 2:
        return delta_ref[x * ny + tall - 2]
    return down_ref[2 * x + tall - ny - 2]


def tall_act(nx, ny, act_ref, up_ref, down_ref, x, tall):
    if tall == 0:
        return up_ref[2 * nx + x]
    if tall == ny + 1:
        return down_ref[2 * nx + x]
    return act_ref[x * ny + tall - 1]


def tall_spot(nx, ny, x, tall):
    if tall < 2:
        return nx * ny + x * ny + ny - 2 + tall
    if tall < ny + 2:
        return x * ny + tall - 2
    return nx * ny + x * ny + tall - ny - 2


def pack_x_body(
    nx, ny, even_ref, delta_ref, act_ref, edge_ref, up_ref, down_ref, near_ref, cross_ref, merged_ref
):
    lane = lane_ids(edge_ref.shape[0])
    half = 2 * nx * ny
    up = pltpu.roll(up_ref[3 * nx], half, 1)
    down = pltpu.roll(down_ref[3 * nx], half, 1)
    beyond = jnp.where(lax.rem(lane, 2 * ny) < ny, down, up)
    merged = jnp.where(lane < half, edge_ref[...], beyond)
    merged_ref[...] = merged

    def fill(ref, planes, act_plane, deltas, acts):
        for k in range(2):
            for at, tall in enumerate(deltas):
                ref[k * len(deltas) + at] = tall_delta(ny, delta_ref, up_ref, down_ref, planes[k], tall)
        base = 2 * len(deltas)
        for at, tall in enumerate(acts):
            ref[base + at] = tall_act(nx, ny, act_ref, up_ref, down_ref, act_plane, tall)
        ref[base + len(acts)] = merged

    low, high = ((0, 1), 0), ((nx - 2, nx - 1), nx - 1)
    every = list(range(ny + 4)), list(range(ny + 2))
    ends = [0, 1, ny + 2, ny + 3], [0, ny + 1]

    @pl.when(even_ref[0] == 1)
    def _():
        fill(cross_ref, *low, *ends)
        fill(near_ref, *high, *every)

    @pl.when(even_ref[0] == 0)
    def _():
        fill(cross_ref, *high, *ends)
        fill(near_ref, *low, *every)


def store_shifts(shifted, plane, tall, block, edges, spot):
    before, after = z_shifts(block, edges, spot)
    at = slice(tall * LANES, (tall + 1) * LANES)
    shifted[0, plane, :, at] = after
    shifted[1, plane, :, at] = block
    shifted[2, plane, :, at] = before


def tap_rows(plane_at, wide, taps, groups):
    def piece(c, plane, b):
        parts = [
            plane_at(c, plane, slice((2 - b + first) * LANES, (2 - b + first + count) * LANES))
            for first, count in groups
        ]
        return parts[0] if len(parts) == 1 else jnp.concatenate(parts, 1)

    return jnp.concatenate(
        [piece(c, wide + 2 - a, b) for a in taps for b in range(3) for c in range(3)], 0
    )


def tap_back(w_ref, rows, taps):
    per = w_ref.shape[1] // 3
    return jnp.dot(
        w_ref[:, per * taps[0] : per * (taps[-1] + 1)], rows, preferred_element_type=F32
    )


def add_two(totals, rows, acts, taps):
    term = lax.dot_general(rows, acts, (((1,), (1,)), ((), ())), preferred_element_type=F32)
    per = rows.shape[0] // len(taps)
    for k, a in enumerate(taps):
        totals[a] = add(totals[a], term[k * per : (k + 1) * per])


def finish_plane(ny, back, acts, wide, one_edges):
    delta = back * slope(acts.astype(F32))
    for tall in range(ny + 2):
        one_edges = put_edges(
            one_edges, delta[:, tall * LANES : (tall + 1) * LANES], wide * (ny + 2) + tall
        )
    return delta.astype(BF16), one_edges


def add_one(nx, ny, totals, one, wide, vol_ref, delta_plane):
    taps = [a for a in range(3) if 0 <= wide - 2 + a < nx]
    rhs = [one[:, (2 - b) * LANES : (2 - b + ny) * LANES] for b in range(3)]
    if delta_plane is not None:
        rhs.append(delta_plane)
    rhs = jnp.concatenate(rhs, 0)
    lhs = jnp.concatenate([vol_ref[wide - 2 + a] for a in taps], 0)
    term = lax.dot_general(lhs, rhs, (((1,), (1,)), ((), ())), preferred_element_type=F32)
    if delta_plane is None:
        term = jnp.concatenate([term, jnp.zeros((term.shape[0], one.shape[0]), F32)], 1)
    per = lhs.shape[0] // len(taps)
    for k, a in enumerate(taps):
        totals[a] = add(totals[a], term[k * per : (k + 1) * per])


def own_taps(nx, wide):
    return [a for a in range(3) if 2 <= wide + 2 - a <= nx + 1]


def add(total, term):
    return term if total is None else total + term


def core_body(
    nx, ny, delta_ref, act_ref, edge_ref, vol_ref, w_ref, shifted, back_ref, two_ref, vol_out_ref
):
    for x in range(nx):
        for y in range(ny):
            store_shifts(shifted, x, y + 2, delta_ref[x * ny + y], edge_ref[...], x * ny + y)
    totals = [None] * 3
    for wide in range(nx + 2):
        taps = own_taps(nx, wide)
        rows = tap_rows(lambda c, plane, at: shifted[c, plane - 2, :, at], wide, taps, [(2, ny - 2)])
        back_ref[wide] = tap_back(w_ref, rows, taps)
        if 1 <= wide <= nx:
            acts = jnp.concatenate([act_ref[(wide - 1) * ny + y] for y in range(1, ny - 1)], 1)
            add_two(totals, rows, acts, taps)
    two_ref[...] = jnp.concatenate(totals, 0)
    edges = edge_ref[0:8].astype(F32)
    for x in range(nx):
        vol = vol_ref[x]
        shifts = [[], [], []]
        for y in range(ny):
            before, after = z_shifts(vol[y], edges, nx * ny + x * ny + y)
            shifts[0].append(before)
            shifts[1].append(vol[y])
            shifts[2].append(after)
        lhs = [jnp.concatenate(row, 1) for row in shifts] + [jnp.zeros((8, ny * LANES), F32)]
        vol_out_ref[x] = jnp.concatenate(lhs, 0).astype(BF16)


def inner_body(
    nx, ny, delta_ref, act_ref, merged_ref, up_ref, down_ref, w_ref, core_ref, back_ref, core_two_ref, vol_ref,
    shifted, one_ref, one_edge_ref, two_ref, part_ref, first_ref,
):
    chan = merged_ref.shape[0]
    merged = merged_ref[...]
    own = slice(2 * LANES, (ny + 2) * LANES)
    for x in range(nx):
        for c in range(3):
            shifted[c, x, :, own] = core_ref[c, x, :, own]
        for tall in (0, 1, ny + 2, ny + 3):
            block = tall_delta(ny, delta_ref, up_ref, down_ref, x, tall)
            store_shifts(shifted, x, tall, block, merged, tall_spot(nx, ny, x, tall))
    one_edges = jnp.zeros((chan, LANES), F32)
    totals = [None] * 3
    rim = slice(LANES, 3 * LANES)
    for wide in range(nx + 2):
        taps = own_taps(nx, wide)
        rows = tap_rows(
            lambda c, plane, at: shifted[c, plane - 2, :, at], wide, taps, [(0, 2), (ny, 2)]
        )
        ends = tap_back(w_ref, rows, taps)
        back = jnp.concatenate([ends[:, : 2 * LANES], back_ref[wide], ends[:, 2 * LANES :]], 1)
        if 1 <= wide <= nx:
            acts = jnp.concatenate(
                [tall_act(nx, ny, act_ref, up_ref, down_ref, wide - 1, tall) for tall in range(ny + 2)], 1
            )
            act_rim = jnp.concatenate([act_ref[(wide - 1) * ny], act_ref[wide * ny - 1]], 1)
            add_two(totals, rows[:, rim], act_rim, taps)
        if 2 <= wide < nx:
            one_ref[wide - 2], one_edges = finish_plane(ny, back, acts, wide, one_edges)
        else:
            part_ref[wide if wide < 2 else wide - nx + 2] = back
    one_edge_ref[...] = one_edges
    two_ref[...] = core_two_ref[...] + jnp.concatenate(totals, 0)
    totals = [None] * 3
    for wide in range(2, nx):
        add_one(nx, ny, totals, one_ref[wide - 2], wide, vol_ref, shifted[1, wide - 1, :, own])
    first_ref[...] = jnp.concatenate(totals, 0)


def outer_body(
    nx, ny, even_ref, act_ref, up_ref, down_ref, near_ref, cross_ref, face_ref, w_ref,
    own_ref, inner_ref, inner_edge_ref, two_ref, vol_ref, part_ref, first_ref,
    sums_ref, one_ref, one_edge_ref, far, grad_two,
):
    chan = act_ref.shape[1]
    base = 2 * (ny + 4)
    even = jnp.broadcast_to(even_ref[0], (chan, LANES)) == 1

    def choose(side, near, cross):
        return jnp.where(even, near, cross) if side else jnp.where(even, cross, near)

    def act_beside(side, tall):
        if tall == 0:
            cross = cross_ref[8]
        elif tall == ny + 1:
            cross = cross_ref[9]
        else:
            cross = face_ref[2 * ny + tall - 1]
        return choose(side, near_ref[base + tall], cross)

    def cross_delta(k, tall):
        if 2 <= tall < ny + 2:
            return face_ref[k * ny + tall - 2]
        return cross_ref[4 * k + (tall if tall < 2 else tall - ny)]

    for side in range(2):
        edges = choose(side, near_ref[base + ny + 2], cross_ref[10])
        for k in range(2):
            for tall in range(ny + 4):
                from_x = nx - 2 + k if side == 0 else k
                block = choose(side, near_ref[k * (ny + 4) + tall], cross_delta(k, tall))
                store_shifts(far, 2 * side + k, tall, block, edges, tall_spot(nx, ny, from_x, tall))

    def plane_at(c, wide, at):
        if wide < 2:
            return far[c, wide, :, at]
        if wide < nx + 2:
            return own_ref[c, wide - 2, :, at]
        return far[c, wide - nx, :, at]

    one_edges = inner_edge_ref[...]
    totals = [None] * 3
    for wide in (0, 1, nx, nx + 1):
        if wide == 0:
            blocks = [act_beside(0, tall) for tall in range(ny + 2)]
        elif wide == nx + 1:
            blocks = [act_beside(1, tall) for tall in range(ny + 2)]
        else:
            blocks = [
                tall_act(nx, ny, act_ref, up_ref, down_ref, wide - 1, tall) for tall in range(ny + 2)
            ]
        acts = jnp.concatenate(blocks, 1)
        taps = [a for a in range(3) if a not in own_taps(nx, wide)]
        rows = tap_rows(plane_at, wide, taps, [(0, ny + 2)])
        back = part_ref[wide if wide < 2 else wide - nx + 2] + tap_back(w_ref, rows, taps)
        if 1 <= wide <= nx:
            inside = slice(LANES, (ny + 1) * LANES)
            add_two(totals, rows[:, inside], acts[:, inside], taps)
        one_ref[wide], one_edges = finish_plane(ny, back, acts, wide, one_edges)
    third = 9 * chan
    for a in range(3):
        part = slice(third * a, third * (a + 1))
        grad_two[part, 0:chan] = two_ref[part, :] if totals[a] is None else two_ref[part, :] + totals[a]
    for x in range(1, nx - 1):
        one_ref[x + 1] = inner_ref[x - 1]
    one_edge_ref[...] = one_edges.astype(BF16).astype(F32)

    per = first_ref.shape[0] // 3
    totals = [first_ref[per * a : per * (a + 1), :] for a in range(3)]
    middle = slice(2 * LANES, (ny + 2) * LANES)
    for wide in (0, 1, nx, nx + 1):
        plane = own_ref[1, wide - 1, :, middle] if 1 <= wide <= nx else None
        add_one(nx, ny, totals, one_ref[wide], wide, vol_ref, plane)
    total_one = jnp.concatenate(
        [total[:, : 3 * chan] for total in totals] + [totals[1][:, 3 * chan :]], 1
    )

    lane = lane_ids(8)
    slots = grad_two.shape[0] // 8
    per = LANES // chan
    groups = -(-slots // per)
    tail = jnp.zeros((8, 2 * LANES - total_one.shape[1]), F32)
    tiles = [jnp.concatenate([total_one[8 * c : 8 * c + 8], tail], 1) for c in range(3)]
    head = lax.broadcasted_iota(jnp.int32, (8, 2 * LANES), 0) < 4
    first = jnp.where(head, tiles[0], pltpu.roll(tiles[1], 4, 0))
    second = jnp.where(head, tiles[2], tiles[1])
    sums_ref[groups * 8 : groups * 8 + 8, :] = first[:, :LANES]
    sums_ref[groups * 8 + 8 : groups * 8 + 16, :] = second[:, :LANES]
    rest = second[:, LANES:]
    rest = jnp.where(head[:, :LANES], rest, pltpu.roll(rest, LANES - chan, 1))
    spare = {slots: first[:, LANES:], slots + 1: rest}
    for group in range(groups):
        packed = jnp.zeros((8, LANES), F32)
        for s in range(per):
            slot = group * per + s
            if slot < slots:
                moved = grad_two[slot * 8 : slot * 8 + 8, :]
            else:
                moved = spare[slot]
            if s:
                moved = pltpu.roll(moved, chan * s, 1)
            packed = jnp.where((lane >= chan * s) & (lane < chan * (s + 1)), moved, packed)
        sums_ref[group * 8 : group * 8 + 8, :] = packed


def unpack_body(norm, sums_ref, one_ref, bias_one_ref, two_ref, bias_two_ref):
    chan = two_ref.shape[2]
    per = LANES // chan
    slots = 2 * two_ref.shape[0]
    for slot in range(slots):
        group, s = divmod(slot, per)
        block = sums_ref[group * 8 : group * 8 + 8, :] * norm
        if s:
            block = pltpu.roll(block, LANES - chan * s, 1)
        two_ref[slot // 2, (slot % 2) * 8 : (slot % 2) * 8 + 8, :] = block[:, :chan]
    base = slots // per * 8

    def piece(k, index):
        if index < per:
            block, s = sums_ref[base + 8 * (k + 1) : base + 8 * (k + 2), :], index
        else:
            block, s = sums_ref[base : base + 8, :], slots % per + k
        return (pltpu.roll(block, LANES - chan * s, 1) if s else block) * norm

    ins = one_ref.shape[1]
    for ab in range(9):
        first = piece(0, ab)
        second = piece(1, ab)
        one_ref[3 * ab] = first[0:ins, :chan]
        one_ref[3 * ab + 1] = first[4 : 4 + ins, :chan]
        one_ref[3 * ab + 2] = second[0:ins, :chan]
    bias_one_ref[...] = piece(1, 4)[4:5, :chan]
    bias_two_ref[...] = piece(1, 8)[4:5, :chan]


def volume_body(nx, ny, one_ref, edge_ref, w_ref, out_ref, shifted):
    edges = edge_ref[...].astype(BF16)
    for wide in range(nx + 2):
        for tall in range(ny + 2):
            at = slice(tall * LANES, (tall + 1) * LANES)
            block = one_ref[wide, :, at]
            before, after = z_shifts(block, edges, wide * (ny + 2) + tall)
            shifted[0, wide, :, at] = after
            shifted[1, wide, :, at] = before
    weights = w_ref[...]
    ins = out_ref.shape[0]
    for x in range(nx):
        rows = []
        for a in range(3):
            for b in range(3):
                at = slice((2 - b) * LANES, (2 - b + ny) * LANES)
                rows += [shifted[0, x + 2 - a, :, at], one_ref[x + 2 - a, :, at], shifted[1, x + 2 - a, :, at]]
        grad = jnp.dot(weights, jnp.concatenate(rows, 0), preferred_element_type=F32)
        stack = jnp.stack([grad[:8, y * LANES : (y + 1) * LANES] for y in range(ny)], 0)
        out_ref[:, x] = jnp.swapaxes(stack, 0, 1)[:ins]


def ring(axis, step):
    count = lax.axis_size(axis)
    return [(i, (i + step) % count) for i in range(count)]


def swap_edges(edges):
    if lax.axis_size("gz") == 2:
        return lax.ppermute(edges, "gz", ring("gz", 1))
    before = lax.ppermute(edges, "gz", ring("gz", 1))
    after = lax.ppermute(edges, "gz", ring("gz", -1))
    even = lax.broadcasted_iota(jnp.int32, edges.shape, 1) % 2 == 0
    return jnp.where(even, before, after)


def exchange(total, axis, step, cross):
    count = lax.axis_size(axis)
    if axis == "gx":
        return lax.ppermute(total, "gx", [(i, i ^ step ^ cross) for i in range(count)])
    pairs = [
        (i * count + k, (i ^ cross) * count + (k ^ step))
        for i in range(lax.axis_size("gx"))
        for k in range(count)
    ]
    return lax.ppermute(total, ("gx", axis), pairs)


def doublings(axis, first=1):
    step = first
    while step < lax.axis_size(axis):
        yield step
        step *= 2


def near(array):
    return pltpu.with_memory_space_constraint(array, pltpu.VMEM)


def call(body, out_shape, scratch, flops, *args, limit=None):
    many = isinstance(out_shape, (tuple, list))
    spec = pl.BlockSpec(memory_space=pltpu.VMEM)
    return pl.pallas_call(
        body,
        out_shape=out_shape,
        in_specs=[
            pl.BlockSpec(memory_space=pltpu.SMEM) if arg.dtype == jnp.int32 else spec for arg in args
        ],
        out_specs=[spec] * len(out_shape) if many else spec,
        scratch_shapes=scratch,
        compiler_params=pltpu.CompilerParams(vmem_limit_bytes=limit),
        cost_estimate=pl.CostEstimate(flops=flops, bytes_accessed=1 << 18, transcendentals=0),
    )(*args)


def compute(volume, act_one, act_two, weight_one, weight_two, cotangent):
    chan, nx, ny, nz = act_one.shape
    ins = volume.shape[0]
    cells = nx * ny * nz
    for axis in AXES:
        cells *= lax.axis_size(axis)
    norm = 1.0 / math.sqrt(cells)
    flat_two = jnp.transpose(weight_two, (1, 2, 3, 4, 0)).reshape(chan, 27 * chan)
    flat_one = jnp.transpose(weight_one, (1, 2, 3, 4, 0)).reshape(ins, 27 * chan)
    flat_one = jnp.pad(flat_one, ((0, chan - ins), (0, 0)))
    blocks = pltpu.VMEM((nx * ny, chan, LANES), BF16)
    edge = pltpu.VMEM((chan, LANES), BF16)
    flat_two = near(flat_two)
    flat_one = near(flat_one)

    delta, edges, vols = call(
        lambda *refs: prep_body(nx, ny, *refs),
        (blocks, edge, pltpu.VMEM((nx, ny, 8, LANES), F32)),
        [],
        1 << 20,
        cotangent, act_two, volume,
    )
    delta = near(delta)
    edges, act_one = lax.optimization_barrier((edges, act_one))
    across = lax.axis_size("gx")
    even = (lax.axis_index("gx") % 2 == 0).astype(jnp.int32).reshape(1)
    act, face = call(
        lambda *refs: act_body(nx, ny, *refs),
        (blocks, pltpu.VMEM((3 * ny, chan, LANES), BF16)),
        [],
        1 << 24,
        even, act_one, delta,
    )
    edges = near(swap_edges(edges))
    act = near(act)
    side = pltpu.VMEM((3 * nx + 1, chan, LANES), BF16)
    low, high = call(
        lambda *refs: pack_y_body(nx, ny, *refs), (side, side), [], 1 << 20, delta, act, edges
    )
    crossing = [(i, (i + i % 2 * 2 - 1) % across) for i in range(across)]
    low, high, face = lax.optimization_barrier((low, high, face))
    down = lax.ppermute(low, "gy", ring("gy", -1))
    up = lax.ppermute(high, "gy", ring("gy", 1))
    face = lax.ppermute(face, "gx", crossing)
    up, down, face = near(up), near(down), near(face)
    core, core_back, core_two, vols = call(
        lambda *refs: core_body(nx, ny, *refs),
        (
            pltpu.VMEM((3, nx, chan, (ny + 4) * LANES), BF16),
            pltpu.VMEM((nx + 2, chan, (ny - 2) * LANES), F32),
            pltpu.VMEM((27 * chan, chan), F32),
            pltpu.VMEM((nx, 32, ny * LANES), BF16),
        ),
        [],
        1 << 27,
        delta, act, edges, near(vols), flat_two,
        limit=24 << 20,
    )
    near_side, cross_side, merged = call(
        lambda *refs: pack_x_body(nx, ny, *refs),
        (
            pltpu.VMEM((3 * (ny + 4) - 1, chan, LANES), BF16),
            pltpu.VMEM((11, chan, LANES), BF16),
            edge,
        ),
        [],
        1 << 20,
        even, delta, act, edges, up, down,
        limit=24 << 20,
    )
    cross_side = near(lax.ppermute(cross_side, "gx", crossing))
    near_side = near(lax.ppermute(near_side, "gx", [(i, i ^ 1) for i in range(across)]))
    span = (ny + 2) * LANES
    own, inner, inner_edges, inner_two, part, inner_one = call(
        lambda *refs: inner_body(nx, ny, *refs),
        (
            pltpu.VMEM((3, nx, chan, (ny + 4) * LANES), BF16),
            pltpu.VMEM((nx - 2, chan, span), BF16),
            pltpu.VMEM((chan, LANES), F32),
            pltpu.VMEM((27 * chan, chan), F32),
            pltpu.VMEM((4, chan, span), F32),
            pltpu.VMEM((96, 4 * chan), F32),
        ),
        [],
        1 << 27,
        delta, act, near(merged), up, down, flat_two,
        near(core), near(core_back), near(core_two), near(vols),
        limit=24 << 20,
    )
    slots = 27 * chan // 8
    rows = -(-slots // (LANES // chan)) * 8 + 16
    sums, one, one_edges = call(
        lambda *refs: outer_body(nx, ny, *refs),
        (
            pltpu.VMEM((rows, LANES), F32),
            pltpu.VMEM((nx + 2, chan, span), BF16),
            pltpu.VMEM((chan, LANES), F32),
        ),
        [
            pltpu.VMEM((3, 4, chan, (ny + 4) * LANES), BF16),
            pltpu.VMEM((27 * chan, LANES), F32),
        ],
        1 << 28,
        even, act, up, down, near_side, cross_side, face, flat_two,
        near(own), near(inner), near(inner_edges), near(inner_two), near(vols), near(part), near(inner_one),
        limit=24 << 20,
    )
    if lax.axis_size("gz") == 2:
        moved = exchange(jnp.concatenate([sums, one_edges], 0), "gx", 1, 0)
        sums = sums + moved[:rows]
        moved = exchange(jnp.concatenate([sums, moved[rows:]], 0), "gz", 1, 1)
        sums = sums + moved[:rows]
        one_edges = moved[rows:]
    else:
        one_edges = swap_edges(one_edges)
        sums = sums + exchange(sums, "gx", 1, 0)
        for step in doublings("gz"):
            sums = sums + exchange(sums, "gz", step, 1)
    for step in doublings("gx", 2):
        sums = sums + exchange(sums, "gx", step, 1)
    grad_volume = call(
        lambda *refs: volume_body(nx, ny, *refs),
        jax.ShapeDtypeStruct(volume.shape, F32),
        [pltpu.VMEM((2, nx + 2, chan, span), BF16)],
        1 << 27,
        near(one), near(one_edges), flat_one,
    )
    sums, grad_volume = lax.optimization_barrier((sums, grad_volume))
    for step in doublings("gy"):
        sums = sums + exchange(sums, "gy", step, 1)
    sums = near(sums)
    grad_one, bias_one, grad_two, bias_two = call(
        lambda *refs: unpack_body(norm, *refs),
        (
            jax.ShapeDtypeStruct((27, ins, chan), F32),
            jax.ShapeDtypeStruct((1, chan), F32),
            jax.ShapeDtypeStruct((27, chan, chan), F32),
            jax.ShapeDtypeStruct((1, chan), F32),
        ),
        [],
        1 << 20,
        sums,
    )
    grad_one = jnp.transpose(grad_one.reshape(3, 3, 3, ins, chan), (4, 3, 0, 1, 2))
    grad_two = jnp.transpose(grad_two.reshape(3, 3, 3, chan, chan), (3, 4, 0, 1, 2))
    return (grad_one, bias_one.reshape(chan), grad_two, bias_two.reshape(chan), grad_volume)


def solution(mesh):
    placed = P(None, *AXES)
    return jax.shard_map(
        compute,
        mesh=mesh,
        in_specs=(placed, placed, placed, P(), P(), placed),
        out_specs=(P(), P(), P(), P(), placed),
        check_vma=False,
    )
```

```python
import math

import jax
import jax.numpy as jnp
from jax import lax
from jax.experimental import pallas as pl
from jax.experimental.pallas import tpu as pltpu
from jax.sharding import PartitionSpec as P


AXES = ("gx", "gy", "gz")
F32 = jnp.float32
BF16 = jnp.bfloat16
LANES = 128


def lane_ids(rows):
    return lax.broadcasted_iota(jnp.int32, (rows, LANES), 1)


def slope(saved):
    return jnp.where(saved > 0, 1.0, 0.3).astype(F32)


def put_edges(packed, block, spot):
    lane = lane_ids(block.shape[0])
    moved = pltpu.roll(block, (2 * spot + 1) % LANES, 1)
    return jnp.where((lane == 2 * spot) | (lane == 2 * spot + 1), moved, packed)


def z_shifts(block, edges, spot):
    lane = lane_ids(block.shape[0])
    near = pltpu.roll(edges, (LANES - 2 * spot - 1) % LANES, 1)
    after = pltpu.roll(jnp.where(lane == 0, near, block), LANES - 1, 1)
    before = pltpu.roll(jnp.where(lane == LANES - 1, near, block), 1, 1)
    return before, after


def prep_body(nx, ny, cot_ref, act_two_ref, vol_ref, delta_ref, edge_ref, rows_ref):
    chan = cot_ref.shape[0]
    edges = jnp.zeros((chan, LANES), F32)
    vol_edges = jnp.zeros((8, LANES), F32)
    for x in range(nx):
        delta = cot_ref[:, x].astype(F32) * slope(act_two_ref[:, x].astype(F32))
        delta = jnp.swapaxes(delta, 0, 1)
        for y in range(ny):
            spot = x * ny + y
            delta_ref[spot] = delta[y].astype(BF16)
            edges = put_edges(edges, delta[y], spot)
        vol = vol_rows(vol_ref, x)
        for y in range(ny):
            rows_ref[x, y] = vol[y]
            vol_edges = put_edges(vol_edges, vol[y], nx * ny + x * ny + y)
    vol_edges = jnp.concatenate([vol_edges] * (chan // 8), 0)
    half = lane_ids(chan) < 2 * nx * ny
    edge_ref[...] = jnp.where(half, edges, vol_edges).astype(BF16)


def act_body(nx, ny, even_ref, act_one_ref, delta_ref, act_ref, face_ref):
    for x in range(nx):
        act = jnp.swapaxes(act_one_ref[:, x].astype(F32), 0, 1)
        for y in range(ny):
            act_ref[x * ny + y] = act[y].astype(BF16)

    def fill(planes, act_plane):
        for y in range(ny):
            for k in range(2):
                face_ref[k * ny + y] = delta_ref[planes[k] * ny + y]
            face_ref[2 * ny + y] = act_ref[act_plane * ny + y]

    @pl.when(even_ref[0] == 1)
    def _():
        fill((0, 1), 0)

    @pl.when(even_ref[0] == 0)
    def _():
        fill((nx - 2, nx - 1), nx - 1)


def vol_rows(vol_ref, x):
    vol = vol_ref[:, x].astype(F32)
    rest = jnp.ones((8 - vol.shape[0],) + vol.shape[1:], F32)
    return jnp.swapaxes(jnp.concatenate([vol, rest], 0), 0, 1)


def pack_y_body(nx, ny, delta_ref, act_ref, edge_ref, low_ref, high_ref):
    for x in range(nx):
        for k in range(2):
            low_ref[2 * x + k] = delta_ref[x * ny + k]
            high_ref[2 * x + k] = delta_ref[x * ny + ny - 2 + k]
        low_ref[2 * nx + x] = act_ref[x * ny]
        high_ref[2 * nx + x] = act_ref[x * ny + ny - 1]
    low_ref[3 * nx] = edge_ref[...]
    high_ref[3 * nx] = edge_ref[...]


def tall_delta(ny, delta_ref, up_ref, down_ref, x, tall):
    if tall < 2:
        return up_ref[2 * x + tall]
    if tall < ny + 2:
        return delta_ref[x * ny + tall - 2]
    return down_ref[2 * x + tall - ny - 2]


def tall_act(nx, ny, act_ref, up_ref, down_ref, x, tall):
    if tall == 0:
        return up_ref[2 * nx + x]
    if tall == ny + 1:
        return down_ref[2 * nx + x]
    return act_ref[x * ny + tall - 1]


def tall_spot(nx, ny, x, tall):
    if tall < 2:
        return nx * ny + x * ny + ny - 2 + tall
    if tall < ny + 2:
        return x * ny + tall - 2
    return nx * ny + x * ny + tall - ny - 2


def pack_x_body(
    nx, ny, even_ref, delta_ref, act_ref, edge_ref, up_ref, down_ref, near_ref, cross_ref, merged_ref
):
    lane = lane_ids(edge_ref.shape[0])
    half = 2 * nx * ny
    up = pltpu.roll(up_ref[3 * nx], half, 1)
    down = pltpu.roll(down_ref[3 * nx], half, 1)
    beyond = jnp.where(lax.rem(lane, 2 * ny) < ny, down, up)
    merged = jnp.where(lane < half, edge_ref[...], beyond)
    merged_ref[...] = merged

    def fill(ref, planes, act_plane, deltas, acts):
        for k in range(2):
            for at, tall in enumerate(deltas):
                ref[k * len(deltas) + at] = tall_delta(ny, delta_ref, up_ref, down_ref, planes[k], tall)
        base = 2 * len(deltas)
        for at, tall in enumerate(acts):
            ref[base + at] = tall_act(nx, ny, act_ref, up_ref, down_ref, act_plane, tall)
        ref[base + len(acts)] = merged

    low, high = ((0, 1), 0), ((nx - 2, nx - 1), nx - 1)
    every = list(range(ny + 4)), list(range(ny + 2))
    ends = [0, 1, ny + 2, ny + 3], [0, ny + 1]

    @pl.when(even_ref[0] == 1)
    def _():
        fill(cross_ref, *low, *ends)
        fill(near_ref, *high, *every)

    @pl.when(even_ref[0] == 0)
    def _():
        fill(cross_ref, *high, *ends)
        fill(near_ref, *low, *every)


def store_shifts(shifted, plane, tall, block, edges, spot):
    before, after = z_shifts(block, edges, spot)
    at = slice(tall * LANES, (tall + 1) * LANES)
    shifted[0, plane, :, at] = after
    shifted[1, plane, :, at] = block
    shifted[2, plane, :, at] = before


def tap_rows(ny, plane_at, wide, taps):
    span = (ny + 2) * LANES
    return jnp.concatenate(
        [
            plane_at(c, wide + 2 - a, slice((2 - b) * LANES, (2 - b) * LANES + span))
            for a in taps
            for b in range(3)
            for c in range(3)
        ],
        0,
    )


def tap_back(w_ref, rows, taps):
    per = w_ref.shape[1] // 3
    return jnp.dot(
        w_ref[:, per * taps[0] : per * (taps[-1] + 1)], rows, preferred_element_type=F32
    )


def add_two(ny, totals, rows, acts, taps):
    inner = slice(LANES, (ny + 1) * LANES)
    term = lax.dot_general(
        rows[:, inner], acts[:, inner], (((1,), (1,)), ((), ())), preferred_element_type=F32
    )
    per = rows.shape[0] // len(taps)
    for k, a in enumerate(taps):
        totals[a] = add(totals[a], term[k * per : (k + 1) * per])


def finish_plane(ny, back, acts, wide, one_edges):
    delta = back * slope(acts.astype(F32))
    for tall in range(ny + 2):
        one_edges = put_edges(
            one_edges, delta[:, tall * LANES : (tall + 1) * LANES], wide * (ny + 2) + tall
        )
    return delta.astype(BF16), one_edges


def add_one(nx, ny, totals, one, wide, vol_ref, delta_plane):
    taps = [a for a in range(3) if 0 <= wide - 2 + a < nx]
    rhs = [one[:, (2 - b) * LANES : (2 - b + ny) * LANES] for b in range(3)]
    if delta_plane is not None:
        rhs.append(delta_plane)
    rhs = jnp.concatenate(rhs, 0)
    lhs = jnp.concatenate([vol_ref[wide - 2 + a] for a in taps], 0)
    term = lax.dot_general(lhs, rhs, (((1,), (1,)), ((), ())), preferred_element_type=F32)
    if delta_plane is None:
        term = jnp.concatenate([term, jnp.zeros((term.shape[0], one.shape[0]), F32)], 1)
    per = lhs.shape[0] // len(taps)
    for k, a in enumerate(taps):
        totals[a] = add(totals[a], term[k * per : (k + 1) * per])


def own_taps(nx, wide):
    return [a for a in range(3) if 2 <= wide + 2 - a <= nx + 1]


def add(total, term):
    return term if total is None else total + term


def inner_body(
    nx, ny, delta_ref, act_ref, edge_ref, merged_ref, up_ref, down_ref, vol_ref, w_ref,
    shifted, one_ref, one_edge_ref, two_ref, vol_out_ref, part_ref, first_ref,
):
    chan = edge_ref.shape[0]
    merged = merged_ref[...]
    for x in range(nx):
        for tall in range(ny + 4):
            block = tall_delta(ny, delta_ref, up_ref, down_ref, x, tall)
            store_shifts(shifted, x, tall, block, merged, tall_spot(nx, ny, x, tall))
    one_edges = jnp.zeros((chan, LANES), F32)
    totals = [None] * 3
    for wide in range(nx + 2):
        taps = own_taps(nx, wide)
        rows = tap_rows(ny, lambda c, plane, at: shifted[c, plane - 2, :, at], wide, taps)
        back = tap_back(w_ref, rows, taps)
        if 1 <= wide <= nx:
            acts = jnp.concatenate(
                [tall_act(nx, ny, act_ref, up_ref, down_ref, wide - 1, tall) for tall in range(ny + 2)], 1
            )
            add_two(ny, totals, rows, acts, taps)
        if 2 <= wide < nx:
            one_ref[wide - 2], one_edges = finish_plane(ny, back, acts, wide, one_edges)
        else:
            part_ref[wide if wide < 2 else wide - nx + 2] = back
    total = jnp.concatenate(totals, 0)
    one_edge_ref[...] = one_edges
    two_ref[...] = total
    edges = edge_ref[0:8].astype(F32)
    for x in range(nx):
        vol = vol_ref[x]
        shifts = [[], [], []]
        for y in range(ny):
            before, after = z_shifts(vol[y], edges, nx * ny + x * ny + y)
            shifts[0].append(before)
            shifts[1].append(vol[y])
            shifts[2].append(after)
        lhs = [jnp.concatenate(row, 1) for row in shifts] + [jnp.zeros((8, ny * LANES), F32)]
        vol_out_ref[x] = jnp.concatenate(lhs, 0).astype(BF16)
    totals = [None] * 3
    middle = slice(2 * LANES, (ny + 2) * LANES)
    for wide in range(2, nx):
        add_one(nx, ny, totals, one_ref[wide - 2], wide, vol_out_ref, shifted[1, wide - 1, :, middle])
    first_ref[...] = jnp.concatenate(totals, 0)


def outer_body(
    nx, ny, even_ref, act_ref, up_ref, down_ref, near_ref, cross_ref, face_ref, w_ref,
    own_ref, inner_ref, inner_edge_ref, two_ref, vol_ref, part_ref, first_ref,
    sums_ref, one_ref, one_edge_ref, far, grad_two,
):
    chan = act_ref.shape[1]
    base = 2 * (ny + 4)
    even = jnp.broadcast_to(even_ref[0], (chan, LANES)) == 1

    def choose(side, near, cross):
        return jnp.where(even, near, cross) if side else jnp.where(even, cross, near)

    def act_beside(side, tall):
        if tall == 0:
            cross = cross_ref[8]
        elif tall == ny + 1:
            cross = cross_ref[9]
        else:
            cross = face_ref[2 * ny + tall - 1]
        return choose(side, near_ref[base + tall], cross)

    def cross_delta(k, tall):
        if 2 <= tall < ny + 2:
            return face_ref[k * ny + tall - 2]
        return cross_ref[4 * k + (tall if tall < 2 else tall - ny)]

    for side in range(2):
        edges = choose(side, near_ref[base + ny + 2], cross_ref[10])
        for k in range(2):
            for tall in range(ny + 4):
                from_x = nx - 2 + k if side == 0 else k
                block = choose(side, near_ref[k * (ny + 4) + tall], cross_delta(k, tall))
                store_shifts(far, 2 * side + k, tall, block, edges, tall_spot(nx, ny, from_x, tall))

    def plane_at(c, wide, at):
        if wide < 2:
            return far[c, wide, :, at]
        if wide < nx + 2:
            return own_ref[c, wide - 2, :, at]
        return far[c, wide - nx, :, at]

    one_edges = inner_edge_ref[...]
    totals = [None] * 3
    for wide in (0, 1, nx, nx + 1):
        if wide == 0:
            blocks = [act_beside(0, tall) for tall in range(ny + 2)]
        elif wide == nx + 1:
            blocks = [act_beside(1, tall) for tall in range(ny + 2)]
        else:
            blocks = [
                tall_act(nx, ny, act_ref, up_ref, down_ref, wide - 1, tall) for tall in range(ny + 2)
            ]
        acts = jnp.concatenate(blocks, 1)
        taps = [a for a in range(3) if a not in own_taps(nx, wide)]
        rows = tap_rows(ny, plane_at, wide, taps)
        back = part_ref[wide if wide < 2 else wide - nx + 2] + tap_back(w_ref, rows, taps)
        if 1 <= wide <= nx:
            add_two(ny, totals, rows, acts, taps)
        one_ref[wide], one_edges = finish_plane(ny, back, acts, wide, one_edges)
    third = 9 * chan
    for a in range(3):
        part = slice(third * a, third * (a + 1))
        grad_two[part, 0:chan] = two_ref[part, :] if totals[a] is None else two_ref[part, :] + totals[a]
    for x in range(1, nx - 1):
        one_ref[x + 1] = inner_ref[x - 1]
    one_edge_ref[...] = one_edges.astype(BF16).astype(F32)

    per = first_ref.shape[0] // 3
    totals = [first_ref[per * a : per * (a + 1), :] for a in range(3)]
    middle = slice(2 * LANES, (ny + 2) * LANES)
    for wide in (0, 1, nx, nx + 1):
        plane = own_ref[1, wide - 1, :, middle] if 1 <= wide <= nx else None
        add_one(nx, ny, totals, one_ref[wide], wide, vol_ref, plane)
    total_one = jnp.concatenate(
        [total[:, : 3 * chan] for total in totals] + [totals[1][:, 3 * chan :]], 1
    )

    lane = lane_ids(8)
    slots = grad_two.shape[0] // 8
    per = LANES // chan
    groups = -(-slots // per)
    tail = jnp.zeros((8, 2 * LANES - total_one.shape[1]), F32)
    tiles = [jnp.concatenate([total_one[8 * c : 8 * c + 8], tail], 1) for c in range(3)]
    head = lax.broadcasted_iota(jnp.int32, (8, 2 * LANES), 0) < 4
    first = jnp.where(head, tiles[0], pltpu.roll(tiles[1], 4, 0))
    second = jnp.where(head, tiles[2], tiles[1])
    sums_ref[groups * 8 : groups * 8 + 8, :] = first[:, :LANES]
    sums_ref[groups * 8 + 8 : groups * 8 + 16, :] = second[:, :LANES]
    rest = second[:, LANES:]
    rest = jnp.where(head[:, :LANES], rest, pltpu.roll(rest, LANES - chan, 1))
    spare = {slots: first[:, LANES:], slots + 1: rest}
    for group in range(groups):
        packed = jnp.zeros((8, LANES), F32)
        for s in range(per):
            slot = group * per + s
            if slot < slots:
                moved = grad_two[slot * 8 : slot * 8 + 8, :]
            else:
                moved = spare[slot]
            if s:
                moved = pltpu.roll(moved, chan * s, 1)
            packed = jnp.where((lane >= chan * s) & (lane < chan * (s + 1)), moved, packed)
        sums_ref[group * 8 : group * 8 + 8, :] = packed


def unpack_body(norm, sums_ref, one_ref, bias_one_ref, two_ref, bias_two_ref):
    chan = two_ref.shape[2]
    per = LANES // chan
    slots = 2 * two_ref.shape[0]
    for slot in range(slots):
        group, s = divmod(slot, per)
        block = sums_ref[group * 8 : group * 8 + 8, :] * norm
        if s:
            block = pltpu.roll(block, LANES - chan * s, 1)
        two_ref[slot // 2, (slot % 2) * 8 : (slot % 2) * 8 + 8, :] = block[:, :chan]
    base = slots // per * 8

    def piece(k, index):
        if index < per:
            block, s = sums_ref[base + 8 * (k + 1) : base + 8 * (k + 2), :], index
        else:
            block, s = sums_ref[base : base + 8, :], slots % per + k
        return (pltpu.roll(block, LANES - chan * s, 1) if s else block) * norm

    ins = one_ref.shape[1]
    for ab in range(9):
        first = piece(0, ab)
        second = piece(1, ab)
        one_ref[3 * ab] = first[0:ins, :chan]
        one_ref[3 * ab + 1] = first[4 : 4 + ins, :chan]
        one_ref[3 * ab + 2] = second[0:ins, :chan]
    bias_one_ref[...] = piece(1, 4)[4:5, :chan]
    bias_two_ref[...] = piece(1, 8)[4:5, :chan]


def volume_body(nx, ny, one_ref, edge_ref, w_ref, out_ref, shifted):
    edges = edge_ref[...].astype(BF16)
    for wide in range(nx + 2):
        for tall in range(ny + 2):
            at = slice(tall * LANES, (tall + 1) * LANES)
            block = one_ref[wide, :, at]
            before, after = z_shifts(block, edges, wide * (ny + 2) + tall)
            shifted[0, wide, :, at] = after
            shifted[1, wide, :, at] = before
    weights = w_ref[...]
    ins = out_ref.shape[0]
    for x in range(nx):
        rows = []
        for a in range(3):
            for b in range(3):
                at = slice((2 - b) * LANES, (2 - b + ny) * LANES)
                rows += [shifted[0, x + 2 - a, :, at], one_ref[x + 2 - a, :, at], shifted[1, x + 2 - a, :, at]]
        grad = jnp.dot(weights, jnp.concatenate(rows, 0), preferred_element_type=F32)
        stack = jnp.stack([grad[:8, y * LANES : (y + 1) * LANES] for y in range(ny)], 0)
        out_ref[:, x] = jnp.swapaxes(stack, 0, 1)[:ins]


def ring(axis, step):
    count = lax.axis_size(axis)
    return [(i, (i + step) % count) for i in range(count)]


def swap_edges(edges):
    if lax.axis_size("gz") == 2:
        return lax.ppermute(edges, "gz", ring("gz", 1))
    before = lax.ppermute(edges, "gz", ring("gz", 1))
    after = lax.ppermute(edges, "gz", ring("gz", -1))
    even = lax.broadcasted_iota(jnp.int32, edges.shape, 1) % 2 == 0
    return jnp.where(even, before, after)


def exchange(total, axis, step, cross):
    count = lax.axis_size(axis)
    if axis == "gx":
        return lax.ppermute(total, "gx", [(i, i ^ step ^ cross) for i in range(count)])
    pairs = [
        (i * count + k, (i ^ cross) * count + (k ^ step))
        for i in range(lax.axis_size("gx"))
        for k in range(count)
    ]
    return lax.ppermute(total, ("gx", axis), pairs)


def doublings(axis, first=1):
    step = first
    while step < lax.axis_size(axis):
        yield step
        step *= 2


def near(array):
    return pltpu.with_memory_space_constraint(array, pltpu.VMEM)


def call(body, out_shape, scratch, flops, *args):
    many = isinstance(out_shape, (tuple, list))
    spec = pl.BlockSpec(memory_space=pltpu.VMEM)
    return pl.pallas_call(
        body,
        out_shape=out_shape,
        in_specs=[
            pl.BlockSpec(memory_space=pltpu.SMEM) if arg.dtype == jnp.int32 else spec for arg in args
        ],
        out_specs=[spec] * len(out_shape) if many else spec,
        scratch_shapes=scratch,
        cost_estimate=pl.CostEstimate(flops=flops, bytes_accessed=1 << 18, transcendentals=0),
    )(*args)


def compute(volume, act_one, act_two, weight_one, weight_two, cotangent):
    chan, nx, ny, nz = act_one.shape
    ins = volume.shape[0]
    cells = nx * ny * nz
    for axis in AXES:
        cells *= lax.axis_size(axis)
    norm = 1.0 / math.sqrt(cells)
    flat_two = jnp.transpose(weight_two, (1, 2, 3, 4, 0)).reshape(chan, 27 * chan)
    flat_one = jnp.transpose(weight_one, (1, 2, 3, 4, 0)).reshape(ins, 27 * chan)
    flat_one = jnp.pad(flat_one, ((0, chan - ins), (0, 0)))
    blocks = pltpu.VMEM((nx * ny, chan, LANES), BF16)
    edge = pltpu.VMEM((chan, LANES), BF16)
    flat_two = near(flat_two)
    flat_one = near(flat_one)

    delta, edges, vols = call(
        lambda *refs: prep_body(nx, ny, *refs),
        (blocks, edge, pltpu.VMEM((nx, ny, 8, LANES), F32)),
        [],
        1 << 20,
        cotangent, act_two, volume,
    )
    delta = near(delta)
    edges, act_one = lax.optimization_barrier((edges, act_one))
    across = lax.axis_size("gx")
    even = (lax.axis_index("gx") % 2 == 0).astype(jnp.int32).reshape(1)
    act, face = call(
        lambda *refs: act_body(nx, ny, *refs),
        (blocks, pltpu.VMEM((3 * ny, chan, LANES), BF16)),
        [],
        1 << 24,
        even, act_one, delta,
    )
    edges = near(swap_edges(edges))
    act = near(act)
    side = pltpu.VMEM((3 * nx + 1, chan, LANES), BF16)
    low, high = call(
        lambda *refs: pack_y_body(nx, ny, *refs), (side, side), [], 1 << 20, delta, act, edges
    )
    crossing = [(i, (i + i % 2 * 2 - 1) % across) for i in range(across)]
    low, high, face = lax.optimization_barrier((low, high, face))
    down = lax.ppermute(low, "gy", ring("gy", -1))
    up = lax.ppermute(high, "gy", ring("gy", 1))
    face = lax.ppermute(face, "gx", crossing)
    up, down, face = near(up), near(down), near(face)
    near_side, cross_side, merged = call(
        lambda *refs: pack_x_body(nx, ny, *refs),
        (
            pltpu.VMEM((3 * (ny + 4) - 1, chan, LANES), BF16),
            pltpu.VMEM((11, chan, LANES), BF16),
            edge,
        ),
        [],
        1 << 20,
        even, delta, act, edges, up, down,
    )
    cross_side = near(lax.ppermute(cross_side, "gx", crossing))
    near_side = near(lax.ppermute(near_side, "gx", [(i, i ^ 1) for i in range(across)]))
    span = (ny + 2) * LANES
    own, inner, inner_edges, inner_two, vols, part, inner_one = call(
        lambda *refs: inner_body(nx, ny, *refs),
        (
            pltpu.VMEM((3, nx, chan, (ny + 4) * LANES), BF16),
            pltpu.VMEM((nx - 2, chan, span), BF16),
            pltpu.VMEM((chan, LANES), F32),
            pltpu.VMEM((27 * chan, chan), F32),
            pltpu.VMEM((nx, 32, ny * LANES), BF16),
            pltpu.VMEM((4, chan, span), F32),
            pltpu.VMEM((96, 4 * chan), F32),
        ),
        [],
        1 << 27,
        delta, act, edges, near(merged), up, down, near(vols), flat_two,
    )
    slots = 27 * chan // 8
    rows = -(-slots // (LANES // chan)) * 8 + 16
    sums, one, one_edges = call(
        lambda *refs: outer_body(nx, ny, *refs),
        (
            pltpu.VMEM((rows, LANES), F32),
            pltpu.VMEM((nx + 2, chan, span), BF16),
            pltpu.VMEM((chan, LANES), F32),
        ),
        [
            pltpu.VMEM((3, 4, chan, (ny + 4) * LANES), BF16),
            pltpu.VMEM((27 * chan, LANES), F32),
        ],
        1 << 28,
        even, act, up, down, near_side, cross_side, face, flat_two,
        near(own), near(inner), near(inner_edges), near(inner_two), near(vols), near(part), near(inner_one),
    )
    if lax.axis_size("gz") == 2:
        moved = exchange(jnp.concatenate([sums, one_edges], 0), "gx", 1, 0)
        sums = sums + moved[:rows]
        moved = exchange(jnp.concatenate([sums, moved[rows:]], 0), "gz", 1, 1)
        sums = sums + moved[:rows]
        one_edges = moved[rows:]
    else:
        one_edges = swap_edges(one_edges)
        sums = sums + exchange(sums, "gx", 1, 0)
        for step in doublings("gz"):
            sums = sums + exchange(sums, "gz", step, 1)
    for step in doublings("gx", 2):
        sums = sums + exchange(sums, "gx", step, 1)
    grad_volume = call(
        lambda *refs: volume_body(nx, ny, *refs),
        jax.ShapeDtypeStruct(volume.shape, F32),
        [pltpu.VMEM((2, nx + 2, chan, span), BF16)],
        1 << 27,
        near(one), near(one_edges), flat_one,
    )
    sums, grad_volume = lax.optimization_barrier((sums, grad_volume))
    for step in doublings("gy"):
        sums = sums + exchange(sums, "gy", step, 1)
    sums = near(sums)
    grad_one, bias_one, grad_two, bias_two = call(
        lambda *refs: unpack_body(norm, *refs),
        (
            jax.ShapeDtypeStruct((27, ins, chan), F32),
            jax.ShapeDtypeStruct((1, chan), F32),
            jax.ShapeDtypeStruct((27, chan, chan), F32),
            jax.ShapeDtypeStruct((1, chan), F32),
        ),
        [],
        1 << 20,
        sums,
    )
    grad_one = jnp.transpose(grad_one.reshape(3, 3, 3, ins, chan), (4, 3, 0, 1, 2))
    grad_two = jnp.transpose(grad_two.reshape(3, 3, 3, chan, chan), (3, 4, 0, 1, 2))
    return (grad_one, bias_one.reshape(chan), grad_two, bias_two.reshape(chan), grad_volume)


def solution(mesh):
    placed = P(None, *AXES)
    return jax.shard_map(
        compute,
        mesh=mesh,
        in_specs=(placed, placed, placed, P(), P(), placed),
        out_specs=(P(), P(), P(), P(), placed),
        check_vma=False,
    )
```
